128 devices in a mesh: req: 16 (over x, y), exp: 8 (over z, core).
Axes of the slice: x: 4, y: 4, z: 4, core: 2. Of those that a mesh axis runs over, the one named last changes fastest.
Arguments:
- hidden: bfloat16 [3072, 2048], P('req'), may hold values from -6 to 6
- gain_attn: bfloat16 [2048], replicated, may hold values from 0.099609375 to 1.8984375
- w_qkv: bfloat16 [2048, 3, 2048], P(None, None, 'exp'), may hold values from -0.125 to 0.125
- w_out: bfloat16 [2048, 2048], P('exp'), may hold values from -0.125 to 0.125
- cache_keys: bfloat16 [64, 2048, 2048], P('req', 'exp'), may hold values from -160 to 160
- cache_values: bfloat16 [64, 2048, 2048], P('req', 'exp'), may hold values from -6 to 6
- cache_lengths: int32 [64], P('req'), may hold values from 1 to 2048, as said below
- parents: int32 [64, 48], P('req'), may hold values from 0 to 46, as said below
- gain_moe: bfloat16 [2048], replicated, may hold values from 0.099609375 to 1.8984375
- w_router: bfloat16 [2048, 64], replicated, may hold values from -0.125 to 0.125
- routes: int32 [3072, 8], P(('req', 'exp')), may hold values from 0 to 63, all different within a row; in each aligned block of 24 rows (0 to 23, 24 to 47, ...) at most 6 rows name the same one
- w_gate_up: bfloat16 [128, 2048, 1024], P(('req', 'exp')), may hold values from -0.125 to 0.125
- w_down: bfloat16 [128, 512, 2048], P(('req', 'exp')), may hold values from -0.1875 to 0.1875
Outputs:
- layer_out: bfloat16 [3072, 2048], P(('req', 'exp'))
The draws below stay inside these ranges and needn't reach their ends.
Inputs may be any that keep to these rules, and one draw needn't show every extreme that they name: `cache_lengths`: each request has 1 to 2048 live positions; some requests hold exactly 2048. `parents`: the parent of tree token t is below t; token 0 is its own parent; the last token's parent is the one before it. In each aligned block of 24 tokens no expert is named by more than 6 of the block's routes; the routes of one token differ.
All inputs are finite; a program needn't handle non-finite values.
Results may differ from the reference program's by a relative error of at most 0.017.
Values may be sent and summed in bfloat16 or wider, within the bound.
No kernel may reach another device: no remote copies, remote signals or barrier semaphores. Data moves between devices by JAX's collectives and lax.ppermute only.
A program may use at most 128 MiB of HBM per device.

```python
import math
import jax
import jax.numpy as jnp
import numpy as np
from jax import lax

D = 2048
HEADS = 16
HEAD_DIM = 128
FF = 1024
TOP = 8
EXP_SPLIT = 2
TREE = 48
EXPERTS = 64
REQS = 64
CACHE = 2048
TOKENS = 3072
TOK_DEV = 24
CAP = 6


def draw_cache_keys(key, part):
    drawn = jax.random.normal(key, (REQS, CACHE, HEADS * HEAD_DIM), jnp.float32)
    return jnp.clip(drawn, -160.0, 160.0).astype(jnp.bfloat16)


def draw_cache_lengths(key, part):
    short_lengths = jax.random.randint(key, (REQS,), 1, CACHE // 8 + 1, dtype=jnp.int32)
    ranking = jax.random.permutation(jax.random.fold_in(key, 3), REQS)
    return jnp.where(ranking < max(1, REQS // 16), CACHE, short_lengths).astype(jnp.int32)


def draw_parents(key, part):
    upper_bound = jnp.maximum(jnp.arange(TREE, dtype=jnp.int32), 1)
    chosen_parents = jax.random.randint(key, (REQS, TREE), 0, jnp.broadcast_to(upper_bound, (REQS, TREE)), dtype=jnp.int32)
    return chosen_parents.at[:, TREE - 1].set(TREE - 2)


def levels(rng, shape, shards, smallest, top_value):
    def one(axis_at, shards_of):
        draws = jax.random.uniform(jax.random.fold_in(jax.random.fold_in(rng, 6), axis_at), (shards_of,), jnp.float32, smallest / len(shards), top_value / len(shards))
        return jnp.repeat(jnp.exp(draws), shape[axis_at] // shards_of).reshape((-1,) + (1,) * (len(shape) - axis_at - 1))

    gain = one(*shards[0])
    for cut in shards[1:]:
        gain = gain * one(*cut)
    return gain


def assign_block(key, own, number, rows, amount, top, limit, slope):
    order = jax.random.permutation(key, amount)
    heavy_load, usual = portions_of(amount, rows * top, limit, slope, True), portions_of(amount, rows * top, limit, slope, False)
    places = jnp.arange(amount)

    def named(sizes, offset_by):
        used = int((sizes > 0).sum())
        fixed = max(1, used // 4)
        shifted = fixed + (places - fixed + offset_by * (used - fixed)) % max(1, amount - fixed)
        return jnp.zeros((amount,), jnp.int32).at[order[jnp.where(places < fixed, places, shifted)]].set(jnp.asarray(sizes, jnp.int32))

    sizes = jnp.where(number % 4 == 0, named(heavy_load, number // 4), named(usual, number - number // 4 - 1))
    mixed = jax.random.permutation(jax.random.fold_in(own, 3), amount)
    giver, sink = mixed[0:amount // 2 * 2:2], mixed[1:amount // 2 * 2:2]
    room = jnp.minimum(sizes[giver] - 1, limit - sizes[sink]) // 2
    room = jnp.where((giver == order[0]) | (sink == order[0]) | (sizes[sink] == 0), 0, jnp.maximum(room, 0))
    shifted = jax.random.randint(jax.random.fold_in(own, 4), (amount // 2,), 0, 1 << 20) % (room + 1)
    sizes = sizes.at[giver].add(-shifted).at[sink].add(shifted)
    items = jnp.searchsorted(jnp.cumsum(sizes), jnp.arange(rows * top), side="right").astype(jnp.int32)
    listing = items.reshape(top, rows).T
    listing = listing[jax.random.permutation(jax.random.fold_in(own, 1), rows)]
    offset_by = jax.random.randint(jax.random.fold_in(own, 2), (rows, 1), 0, top)
    return jnp.take_along_axis(listing, (jnp.arange(top)[None, :] + offset_by) % top, axis=1)


def portions_of(number_of, total, limit, skew, full):
    portions = [(1 << 20) // math.isqrt(rank ** skew) + 1 for rank in range(1, number_of + 1)]
    largest = limit if full else min(limit, max(-(-total // number_of), total * portions[0] // sum(portions)))
    least = 1 if total - largest >= number_of - 1 else 0
    given, rest = [largest] + [least] * (number_of - 1), total - largest - least * (number_of - 1)
    while rest > 0:
        candidates = [i for i in range(1, number_of) if given[i] < largest] or [i for i in range(1, number_of) if given[i] < limit]
        mass, budget = sum([portions[i] for i in candidates]), rest
        for i in candidates:
            more = min(limit - given[i], max(1, budget * portions[i] // mass), rest)
            given[i] = given[i] + more
            rest = rest - more
    return np.array(given)


def centred(key, shape, scale, most, cuts=(), held_as=jnp.bfloat16):
    entries = scale * jax.random.normal(key, shape, jnp.float32)
    if cuts:
        entries = entries * levels(key, shape, cuts, -0.22, 0.18)
    return jnp.clip(entries, -most, most).astype(held_as)


def setup_inputs(seed: int = 0) -> dict:
    arg_keys = jax.random.split(jax.random.key(seed), 14)
    hidden = centred(arg_keys[0], (TOKENS, D), 1.0, 6.0, ((0, 16),))
    gain_attn = jnp.clip(1.0 + 0.18 * jax.random.normal(arg_keys[1], (D,), jnp.float32), 0.099609375, 1.8984375).astype(jnp.bfloat16)
    w_qkv = centred(arg_keys[2], (D, 3, HEADS * HEAD_DIM), D ** -0.5, 0.125, ((2, 8),))
    w_out = centred(arg_keys[3], (HEADS * HEAD_DIM, D), (HEADS * HEAD_DIM) ** -0.5, 0.125, ((0, 8),))
    cache_keys = draw_cache_keys(jax.random.fold_in(arg_keys[13], 71), 0)
    cache_values = centred(arg_keys[5], (REQS, CACHE, HEADS * HEAD_DIM), 1.0, 6.0, ((0, 16), (1, 8)))
    cache_lengths = draw_cache_lengths(jax.random.fold_in(arg_keys[13], 71), 0)
    parents = draw_parents(jax.random.fold_in(arg_keys[13], 71), 0)
    gain_moe = jnp.clip(1.0 + 0.18 * jax.random.normal(arg_keys[8], (D,), jnp.float32), 0.099609375, 1.8984375).astype(jnp.bfloat16)
    w_router = centred(arg_keys[9], (D, EXPERTS), D ** -0.5, 0.125)
    routes_keys = jax.random.split(jax.random.fold_in(arg_keys[10], 1), TOKENS // TOK_DEV)
    routes_turns = jax.random.permutation(jax.random.fold_in(arg_keys[10], 3), TOKENS // TOK_DEV)
    routes = jax.vmap(lambda own, number: assign_block(jax.random.fold_in(arg_keys[10], 2), own, number, TOK_DEV, EXPERTS, TOP, CAP, 1))(routes_keys, routes_turns).reshape((TOKENS, TOP))
    w_gate_up = centred(arg_keys[11], (EXPERTS * EXP_SPLIT, D, FF), D ** -0.5, 0.125, ((0, 128),))
    w_down = centred(arg_keys[12], (EXPERTS * EXP_SPLIT, FF // EXP_SPLIT, D), FF ** -0.5, 0.1875, ((0, 128),))
    return {"hidden": hidden, "gain_attn": gain_attn, "w_qkv": w_qkv, "w_out": w_out, "cache_keys": cache_keys, "cache_values": cache_values, "cache_lengths": cache_lengths, "parents": parents, "gain_moe": gain_moe, "w_router": w_router, "routes": routes, "w_gate_up": w_gate_up, "w_down": w_down}


EPSILON = 1e-05
NEGATIVE = -1e+30

def rms_scaled(values, gain_row):
    values = values.astype(jnp.float32)
    inverse = lax.rsqrt(lax.optimization_barrier(jnp.mean(values * values, axis=-1, keepdims=True)) + EPSILON)
    return values * inverse * gain_row.astype(jnp.float32)

def ancestor_mask(parents):
    tree_width = parents.shape[-1]
    column = jnp.arange(tree_width, dtype=jnp.int32)
    reached = (column[:, None] == column[None, :])[None, :, :] | (parents[:, :, None] == column[None, None, :])
    jumper = parents
    for repeat in range(tree_width.bit_length()):
        row_index = jnp.broadcast_to(jumper[:, :, None], reached.shape)
        reached = reached | jnp.take_along_axis(reached, row_index, axis=1)
        jumper = jnp.take_along_axis(jumper, jumper, axis=1)
    return reached

def reference(hidden, gain_attn, w_qkv, w_out, cache_keys, cache_values, cache_lengths, parents, gain_moe, w_router, routes, w_gate_up, w_down):
    highest_precision = lax.Precision.HIGHEST
    score_scale = HEAD_DIM ** (-0.5)
    normed = rms_scaled(hidden, gain_attn).astype(jnp.bfloat16)
    projected = jnp.dot(normed, w_qkv.reshape(D, 3 * HEADS * HEAD_DIM), preferred_element_type=jnp.float32)
    projected = projected.astype(jnp.bfloat16).reshape(REQS, TREE, 3, HEADS, HEAD_DIM)
    reached = ancestor_mask(parents)
    positions = jnp.arange(CACHE, dtype=jnp.int32)

    def one_request(inputs):
        fresh_rows, key_block, value_block, length, tree_mask = inputs
        query_rows = fresh_rows[:, 0].astype(jnp.float32)
        tree_keys = fresh_rows[:, 1].astype(jnp.float32)
        tree_values = fresh_rows[:, 2].astype(jnp.float32)
        old_keys = key_block.reshape(CACHE, HEADS, HEAD_DIM).astype(jnp.float32)
        old_values = value_block.reshape(CACHE, HEADS, HEAD_DIM).astype(jnp.float32)
        usable = (positions < length)[None, None, :]
        visible = tree_mask[:, None, :]
        cache_scores = jnp.einsum('thd,phd->thp', query_rows, old_keys, precision=highest_precision) * score_scale
        cache_scores = jnp.where(usable, cache_scores, NEGATIVE)
        tree_scores = jnp.einsum('thd,shd->ths', query_rows, tree_keys, precision=highest_precision) * score_scale
        tree_scores = jnp.where(visible, tree_scores, NEGATIVE)
        highest = jnp.maximum(lax.optimization_barrier(jnp.max(cache_scores, axis=-1)), lax.optimization_barrier(jnp.max(tree_scores, axis=-1)))
        cache_weights = jnp.where(usable, jnp.exp(cache_scores - highest[..., None]), 0.0)
        tree_weights = jnp.where(visible, jnp.exp(tree_scores - highest[..., None]), 0.0)
        totals = lax.optimization_barrier(jnp.sum(cache_weights, axis=-1)) + lax.optimization_barrier(jnp.sum(tree_weights, axis=-1))
        cache_rounded = lax.optimization_barrier(cache_weights.astype(jnp.bfloat16)).astype(jnp.float32)
        tree_rounded = lax.optimization_barrier(tree_weights.astype(jnp.bfloat16)).astype(jnp.float32)
        summed = jnp.einsum('thp,phd->thd', cache_rounded, old_values, precision=highest_precision)
        summed = summed + jnp.einsum('ths,shd->thd', tree_rounded, tree_values, precision=highest_precision)
        return (summed / totals[..., None]).astype(jnp.bfloat16)
    attention = lax.map(one_request, (projected, cache_keys, cache_values, cache_lengths, reached))
    attention = attention.reshape(TOKENS, HEADS * HEAD_DIM)
    residual = hidden.astype(jnp.float32) + jnp.dot(attention, w_out, preferred_element_type=jnp.float32)
    normed_moe = rms_scaled(residual, gain_moe).astype(jnp.bfloat16)
    logits = jnp.dot(normed_moe, w_router, preferred_element_type=jnp.float32)
    exponent = jnp.exp(logits)
    chances = exponent / lax.optimization_barrier(jnp.sum(exponent, axis=-1, keepdims=True))
    picked = jnp.take_along_axis(chances, routes, axis=1)
    gate_weights = picked / lax.optimization_barrier(jnp.sum(picked, axis=-1, keepdims=True))
    blocks = TOKENS // TOK_DEV
    assigned = routes.reshape(blocks, TOK_DEV * TOP)
    expert_ids = jnp.arange(EXPERTS, dtype=jnp.int32)
    chosen = (assigned[:, :, None] == expert_ids[None, None, :]).astype(jnp.int32)
    slot_rank = lax.optimization_barrier(jnp.sum((jnp.cumsum(chosen, axis=1) - chosen) * chosen, axis=-1))
    token_of = jnp.arange(TOK_DEV * TOP, dtype=jnp.int32) // TOP
    token_hot = (token_of[:, None] == jnp.arange(TOK_DEV, dtype=jnp.int32)[None, :]).astype(jnp.float32)
    slot_ids = jnp.arange(CAP, dtype=jnp.int32)
    block_rows = normed_moe.reshape(blocks, TOK_DEV, D).astype(jnp.float32)
    block_gates = gate_weights.reshape(blocks, TOK_DEV * TOP)
    group_units = FF // EXP_SPLIT

    def one_expert(moe_sum, expert):
        placing = ((assigned == expert)[:, :, None] & (slot_rank[:, :, None] == slot_ids[None, None, :])).astype(jnp.float32)
        picking = jnp.einsum('bac,at->bct', placing, token_hot, precision=highest_precision)
        gathered = jnp.einsum('bct,btd->bcd', picking, block_rows, precision=highest_precision)
        gathered = gathered.astype(jnp.bfloat16).reshape(blocks * CAP, D)
        paired = jnp.zeros((blocks * CAP, D), jnp.float32)
        for half_index in range(EXP_SPLIT):
            row_id = expert * EXP_SPLIT + half_index
            gate_up_rows = lax.dynamic_index_in_dim(w_gate_up, row_id, 0, keepdims=False)
            down_rows = lax.dynamic_index_in_dim(w_down, row_id, 0, keepdims=False)
            both_proj = jnp.dot(gathered, gate_up_rows, preferred_element_type=jnp.float32)
            hidden_units = (jax.nn.silu(both_proj[:, :group_units]) * both_proj[:, group_units:]).astype(jnp.bfloat16)
            expert_out = jnp.dot(hidden_units, down_rows, preferred_element_type=jnp.float32).astype(jnp.bfloat16)
            paired = paired + lax.optimization_barrier(expert_out).astype(jnp.float32)
        weighting = jnp.einsum('bac,ba,at->btc', placing, block_gates, token_hot, precision=highest_precision)
        moe_sum = moe_sum + jnp.einsum('btc,bcd->btd', weighting, paired.reshape(blocks, CAP, D), precision=highest_precision)
        return (moe_sum, None)
    moe_total, unused = lax.scan(one_expert, jnp.zeros((blocks, TOK_DEV, D), jnp.float32), expert_ids)
    return (residual + moe_total.reshape(TOKENS, D)).astype(jnp.bfloat16)
```

```python
import functools

import jax
import jax.numpy as jnp
from jax import lax
from jax.experimental import pallas as pl
from jax.experimental.pallas import tpu as pltpu
from jax.sharding import Mesh
from jax.sharding import PartitionSpec as P

HEAD_DIM = 128
EXP_SPLIT = 2
CORES = 2
CAP = 6
SLOTS = 8

EPSILON = 1e-05
NEGATIVE = -1e30
F32 = jnp.float32
BF16 = jnp.bfloat16
VMEM = pltpu.VMEM
SMEM = pltpu.SMEM


def dot(a, b):
    return jnp.dot(a, b, preferred_element_type=F32)


def dot_t(a, b):
    return lax.dot_general(a, b, (((1,), (1,)), ((), ())), preferred_element_type=F32)


def iota(shape, axis):
    return lax.broadcasted_iota(jnp.int32, shape, axis)


def call(body, out, in_spaces, scratch=(), flops=0, bytes_accessed=0, vmem=48 << 20):
    out_spec = jax.tree.map(lambda _: pl.BlockSpec(memory_space=VMEM), out)
    return pl.pallas_call(
        body,
        out_shape=out,
        in_specs=[pl.BlockSpec(memory_space=s) for s in in_spaces],
        out_specs=out_spec,
        scratch_shapes=list(scratch),
        compiler_params=pltpu.CompilerParams(vmem_limit_bytes=vmem),
        cost_estimate=pl.CostEstimate(
            flops=flops, bytes_accessed=bytes_accessed, transcendentals=0
        ),
    )


def sds(shape, dtype):
    return jax.ShapeDtypeStruct(shape, dtype)


def normed_rows(values, gain):
    inverse = lax.rsqrt(jnp.mean(values * values, axis=-1, keepdims=True) + EPSILON)
    return (values * inverse * gain).astype(BF16)


def query_kernel(x_ref, g_ref, w_ref, q_ref):
    normed = normed_rows(x_ref[...].astype(F32), g_ref[...].astype(F32))
    q_ref[...] = dot(normed, w_ref[...]).astype(BF16)


def tree_kernel(scale, x_ref, g_ref, w_ref, q_ref, up_ref, o_ref, lse_ref, turn):
    tokens, width = q_ref.shape
    normed = normed_rows(x_ref[...].astype(F32), g_ref[...].astype(F32))
    keys = dot(normed, w_ref[0]).astype(BF16)
    values = dot(normed, w_ref[1]).astype(BF16)
    row = iota((tokens, tokens), 0)
    column = iota((tokens, tokens), 1)
    reach = jnp.where((row == column) | (up_ref[...] == column), 1.0, 0.0)
    for _ in range(6):
        half = reach.astype(BF16)
        reach = jnp.minimum(dot(half, half), 1.0)
    visible = reach > 0.5
    lane = iota((tokens, 128), 1)
    stats = jnp.zeros((tokens, 128), F32)
    for h in range(width // HEAD_DIM):
        cut = slice(h * HEAD_DIM, (h + 1) * HEAD_DIM)
        scores = dot_t(q_ref[:, cut], keys[:, cut]) * scale
        scores = jnp.where(visible, scores, NEGATIVE)
        high = jnp.max(scores, axis=-1, keepdims=True)
        weights = jnp.where(visible, jnp.exp(scores - high), 0.0)
        total = jnp.sum(weights, axis=-1, keepdims=True)
        o_ref[:, cut] = dot(weights.astype(BF16), values[:, cut]) / total
        stats = jnp.where(lane == h, high + jnp.log(total), stats)
    turn[0:tokens, :] = stats
    lse_ref[...] = jnp.transpose(turn[...])[0:8, :]


def page_kernel(scale, tree, meta_ref, *refs):
    pieces = refs[:8]
    k_ref, v_ref, out_ref, q_all, turn = refs[8:]
    requests, page = k_ref.shape[0], k_ref.shape[1]
    owners = out_ref.shape[0]
    tokens = requests * tree
    heads = pieces[0].shape[1] // HEAD_DIM
    for i, piece in enumerate(pieces):
        q_all[meta_ref[8 + i]] = piece[...]
    lane = iota((tree, 128), 1)
    column = iota((tree, page), 1)
    for r in range(requests):
        rows = slice(r * tree, (r + 1) * tree)
        live = meta_ref[r]

        @pl.when(live > 0)
        def _():
            stats = jnp.zeros((tree, 128), F32)
            usable = column < live
            for e in range(owners):
                for h in range(heads):
                    at = slice((e * heads + h) * HEAD_DIM, (e * heads + h + 1) * HEAD_DIM)
                    cut = slice(h * HEAD_DIM, (h + 1) * HEAD_DIM)
                    scores = dot_t(q_all[e, rows, cut], k_ref[r, :, at]) * scale
                    scores = jnp.where(usable, scores, NEGATIVE)
                    high = jnp.max(scores, axis=-1, keepdims=True)
                    weights = jnp.exp(scores - high)
                    total = jnp.sum(weights, axis=-1, keepdims=True)
                    summed = dot(weights.astype(BF16), v_ref[r, :, at])
                    out_ref[e, rows, cut] = (summed / total).astype(BF16)
                    lse = high + jnp.log(total)
                    first = lse.astype(BF16).astype(F32)
                    second = (lse - first).astype(BF16).astype(F32)
                    third = lse - first - second
                    stats = jnp.where(lane == e * 8 + h, first, stats)
                    stats = jnp.where(lane == e * 8 + 2 + h, second, stats)
                    stats = jnp.where(lane == e * 8 + 4 + h, third, stats)
            turn[rows, :] = stats

        @pl.when(live <= 0)
        def _():
            for e in range(owners):
                out_ref[e, rows, :] = jnp.zeros((tree, heads * HEAD_DIM), BF16)
            turn[rows, :] = jnp.where(lane % 8 < 2, NEGATIVE, 0.0)

    turn[tokens:, :] = jnp.zeros((turn.shape[0] - tokens, 128), F32)
    turned = jnp.transpose(turn[...])
    for e in range(owners):
        out_ref[e, tokens:, :] = turned[e * 8 : (e + 1) * 8, :].astype(BF16)


def out_kernel(parts_ref, tree_o_ref, tree_lse_ref, w_ref, out_ref, turn):
    parts, padded, width = parts_ref.shape
    tokens = padded - 8
    heads = width // HEAD_DIM
    lses = []
    for s in range(parts):
        rows = parts_ref[s, tokens:, :].astype(F32)
        lses.append(rows[0:2] + rows[2:4] + rows[4:6])
    lses.append(tree_lse_ref[0:2, :])
    high = functools.reduce(jnp.maximum, lses)
    factors = [jnp.exp(value - high) for value in lses]
    whole = functools.reduce(lambda a, b: a + b, factors)
    for s, factor in enumerate(factors):
        turn[2 * s : 2 * s + 2, :] = factor / whole
    turned = jnp.transpose(turn[...])[0:tokens, :]
    columns = []
    for h in range(heads):
        cut = slice(h * HEAD_DIM, (h + 1) * HEAD_DIM)
        at = 2 * parts + h
        total = turned[:, at : at + 1] * tree_o_ref[:, cut]
        for s in range(parts):
            at = 2 * s + h
            total = total + turned[:, at : at + 1] * parts_ref[s, 0:tokens, cut].astype(F32)
        columns.append(total.astype(BF16))
    attention = jnp.concatenate(columns, axis=1)
    out_ref[...] = dot(attention, w_ref[...]).astype(BF16)


def expert_of_row(rows, experts):
    return jnp.where(iota((rows, experts), 0) // SLOTS == iota((rows, experts), 1), 1.0, 0.0)


def place_kernel(routes_ref, place_ref):
    top, tokens = routes_ref.shape
    chunks, rows, _ = place_ref.shape
    experts = rows // SLOTS
    named = iota((experts, tokens), 0)
    chosen = jnp.zeros((experts, tokens), F32)
    for k in range(top):
        chosen = jnp.where(routes_ref[k : k + 1, :] == named, 1.0, chosen)
    source = iota((tokens, 2 * tokens), 0)
    target = iota((tokens, 2 * tokens), 1) % tokens
    chosen = chosen.astype(BF16)
    rank = dot(chosen, jnp.where(source < target, 1.0, 0.0).astype(BF16))
    both = dot(chosen, jnp.where(source == target, 1.0, 0.0).astype(BF16))
    rank = jnp.where(both > 0.5, rank, -1.0).astype(BF16)
    spread = dot(expert_of_row(rows, experts).astype(BF16), rank)
    slot = iota((rows, 2 * tokens), 0) % SLOTS
    is_tail = iota((rows, 2 * tokens), 1) >= tokens
    for j in range(chunks):
        wanted = jnp.where(is_tail, (slot - CAP) * chunks + j, slot)
        valid = is_tail == (slot >= CAP)
        hit = valid & (spread == wanted.astype(F32))
        place_ref[j] = jnp.where(hit, 1.0, 0.0).astype(BF16)


def residual_kernel(
    meta_ref, parts_ref, x_ref, g_ref, place_ref, res_ref, normed_ref, out_ref
):
    parts, tokens, width = parts_ref.shape
    chunks = place_ref.shape[0]
    cut = width // (chunks + 1)
    start = pl.multiple_of(meta_ref[0] * tokens, 8)
    residual = parts_ref[0].astype(F32)
    for s in range(1, parts):
        residual = residual + parts_ref[s].astype(F32)
    residual = x_ref[pl.ds(start, tokens), :].astype(F32) + residual
    res_ref[...] = residual
    inverse = lax.rsqrt(jnp.mean(residual * residual, axis=-1, keepdims=True) + EPSILON)
    normed = residual * inverse * g_ref[...].astype(F32)
    normed_ref[...] = normed.astype(BF16)
    tail = normed[:, chunks * cut :]
    for j in range(chunks):
        pair = jnp.concatenate([normed[:, j * cut : (j + 1) * cut], tail], axis=0).astype(BF16)
        out_ref[:, j * cut : (j + 1) * cut] = dot(place_ref[j], pair).astype(BF16)


def gate_kernel(normed_ref, router_ref, routes_ref, table_ref):
    tokens, top = routes_ref.shape
    experts = router_ref.shape[0]
    chunks, _, rows = table_ref.shape
    logits = dot_t(normed_ref[...], router_ref[...])
    exponent = jnp.exp(logits)
    chances = exponent / jnp.sum(exponent, axis=-1, keepdims=True)
    named = iota((tokens, experts), 1)
    chosen = jnp.zeros((tokens, experts), F32)
    for k in range(top):
        chosen = jnp.where(routes_ref[:, k : k + 1] == named, 1.0, chosen)
    picked = chances * chosen
    gates = picked / jnp.sum(picked, axis=-1, keepdims=True)
    earlier = jnp.where(iota((tokens, tokens), 0) > iota((tokens, tokens), 1), 1.0, 0.0)
    rank = dot(earlier.astype(BF16), chosen.astype(BF16))
    rank = jnp.where(chosen > 0.5, rank, -1.0).astype(BF16)
    first = gates.astype(BF16)
    second = (gates - first.astype(F32)).astype(BF16)
    home = iota((experts, rows), 0) == iota((experts, rows), 1) // SLOTS
    home = jnp.where(home, 1.0, 0.0).astype(BF16)
    rank, first, second = dot(rank, home), dot(first, home), dot(second, home)
    slot = iota((tokens, rows), 1) % SLOTS
    main = (slot < CAP) & (rank == slot.astype(F32))
    for j in range(chunks):
        tail = (slot >= CAP) & (rank == ((slot - CAP) * chunks + j).astype(F32))
        table_ref[j] = jnp.concatenate(
            [
                jnp.where(main, first, 0.0),
                jnp.where(main, second, 0.0),
                jnp.where(tail, first, 0.0),
                jnp.where(tail, second, 0.0),
            ],
            axis=0,
        ).astype(BF16)


def expert_kernel(block, x_ref, gate_up_ref, down_ref, out_ref):
    rows, packed = x_ref.shape
    width, both = gate_up_ref.shape
    units = both // 2
    cut = width - packed
    chunks = packed // cut
    a = iota((block, block), 0)
    b = iota((block, block), 1)
    same = a // SLOTS == b // SLOTS
    slot_a, slot_b = a % SLOTS, b % SLOTS
    unpack, pack = [], []
    for k in range(chunks):
        hit = same & (slot_a < CAP) & (slot_b >= CAP) & (slot_a == (slot_b - CAP) * chunks + k)
        unpack.append(jnp.where(hit, 1.0, 0.0).astype(BF16))
        hit = same & (slot_b < CAP) & (slot_a >= CAP) & (slot_b == (slot_a - CAP) * chunks + k)
        pack.append(jnp.where(hit, 1.0, 0.0).astype(BF16))
    is_tail = iota((block, cut), 0) % SLOTS >= CAP
    for at in range(0, rows, block):
        span = slice(at, at + block)
        tail = dot(unpack[0], x_ref[span, 0:cut])
        for k in range(1, chunks):
            tail = tail + dot(unpack[k], x_ref[span, k * cut : (k + 1) * cut])
        up = dot(x_ref[span, :], gate_up_ref[0:packed, :])
        up = up + dot(tail.astype(BF16), gate_up_ref[packed:, :])
        gate = up[:, :units]
        hidden = (gate / (1.0 + jnp.exp(-gate)) * up[:, units:]).astype(BF16)
        last = dot(hidden, down_ref[:, packed:]).astype(BF16)
        for k in range(chunks):
            main = dot(hidden, down_ref[:, k * cut : (k + 1) * cut])
            out_ref[span, k * cut : (k + 1) * cut] = jnp.where(
                is_tail, dot(pack[k], last), main
            ).astype(BF16)


def final_kernel(back_ref, table_ref, res_ref, out_ref):
    tokens, width = res_ref.shape
    chunks = table_ref.shape[0]
    cut = width // (chunks + 1)
    tail = res_ref[:, chunks * cut :]
    for j in range(chunks):
        span = slice(j * cut, (j + 1) * cut)
        sums = dot(table_ref[j], back_ref[:, span])
        main = sums[0:tokens] + sums[tokens : 2 * tokens]
        out_ref[:, span] = (res_ref[:, span] + main).astype(BF16)
        tail = tail + (sums[2 * tokens : 3 * tokens] + sums[3 * tokens :])
    out_ref[:, chunks * cut :] = tail.astype(BF16)


def per_device(
    hidden,
    gain_attn,
    w_qkv,
    w_out,
    cache_keys,
    cache_values,
    cache_lengths,
    parents,
    gain_moe,
    w_router,
    routes,
    w_gate_up,
    w_down,
):
    z_count = lax.axis_size("z")
    exp_count = z_count * CORES
    z_index = lax.axis_index("z")
    core = lax.axis_index("core")
    exp_index = z_index * CORES + core
    tokens, width = hidden.shape
    requests, tree = parents.shape
    page = cache_keys.shape[1]
    local_width = w_qkv.shape[2]
    scale = HEAD_DIM ** (-0.5)
    own = tokens // exp_count
    experts = w_router.shape[1]
    packed = width * CAP // SLOTS
    chunks = packed // (width - packed)
    padded = tokens + 8

    gain_a = gain_attn.reshape(1, width)
    gain_m = gain_moe.reshape(1, width)
    w_three = jnp.transpose(w_qkv, (1, 0, 2))

    query = call(
        query_kernel,
        sds((tokens, local_width), BF16),
        [VMEM] * 3,
        flops=2 * tokens * width * local_width,
        bytes_accessed=2 * width * (tokens + local_width),
    )(hidden, gain_a, w_three[0])

    def over_z(value, step):
        return lax.ppermute(value, "z", [(i, (i + step) % z_count) for i in range(z_count)])

    def over_core(value):
        return lax.ppermute(value, "core", [(0, 1), (1, 0)])

    pieces = [query] + [over_z(query, step) for step in range(1, z_count)]
    owners = [((z_index - step) % z_count) * CORES + core for step in range(z_count)]
    pieces = pieces + [over_core(piece) for piece in pieces]
    owners = owners + [owner + 1 - 2 * core for owner in owners]

    up = (parents + tree * jnp.arange(requests, dtype=jnp.int32)[:, None]).reshape(tokens, 1)
    tree_o, tree_lse = call(
        functools.partial(tree_kernel, scale),
        (sds((tokens, local_width), F32), sds((8, 256), F32)),
        [VMEM] * 5,
        [pltpu.VMEM((256, 128), F32)],
        flops=4 * tokens * width * local_width,
        bytes_accessed=2 * width * (tokens + 2 * local_width),
    )(hidden, gain_a, w_three[1:], query, up)

    place = call(
        place_kernel,
        sds((chunks, experts * SLOTS, 2 * own), BF16),
        [VMEM],
        flops=1 << 22,
        bytes_accessed=1 << 18,
    )(routes.T)

    meta = jnp.concatenate(
        [
            cache_lengths - exp_index * page,
            jnp.zeros((8 - requests,), jnp.int32),
            jnp.stack(owners).astype(jnp.int32),
        ]
    )
    partial = call(
        functools.partial(page_kernel, scale, tree),
        sds((exp_count, padded, local_width), BF16),
        [SMEM] + [VMEM] * 10,
        [pltpu.VMEM((exp_count, tokens, local_width), BF16), pltpu.VMEM((256, 128), F32)],
        flops=4 * tokens * page * width,
        bytes_accessed=4 * requests * page * width,
    )(meta, *pieces, cache_keys, cache_values)
    arrived = lax.all_to_all(
        partial.reshape(exp_count * padded, local_width),
        ("z", "core"),
        split_axis=0,
        concat_axis=0,
        tiled=True,
    ).reshape(exp_count, padded, local_width)
    mixed = call(
        out_kernel,
        sds((tokens, width), BF16),
        [VMEM] * 4,
        [pltpu.VMEM((128, 256), F32)],
        flops=2 * tokens * width * local_width,
        bytes_accessed=2 * width * (tokens + local_width),
    )(arrived, tree_o, tree_lse, w_out)
    mixed = lax.all_to_all(
        mixed, ("z", "core"), split_axis=0, concat_axis=0, tiled=True
    ).reshape(exp_count, own, width)

    residual, normed, outgoing = call(
        residual_kernel,
        (
            sds((own, width), F32),
            sds((own, width), BF16),
            sds((experts * SLOTS, packed), BF16),
        ),
        [SMEM] + [VMEM] * 4,
        flops=1 << 27,
        bytes_accessed=1 << 22,
    )(exp_index.reshape(1).astype(jnp.int32), mixed, hidden, gain_m, place)
    rows = lax.all_to_all(
        outgoing.reshape(experts, SLOTS, packed),
        ("req", "z"),
        split_axis=0,
        concat_axis=0,
        tiled=True,
    ).reshape(experts * SLOTS, packed)
    table = call(
        gate_kernel,
        sds((chunks, 4 * own, experts * SLOTS), BF16),
        [VMEM] * 3,
        flops=1 << 24,
        bytes_accessed=1 << 19,
    )(normed, w_router.T, routes)

    expert = call(
        functools.partial(expert_kernel, 256),
        sds((experts * SLOTS, packed), BF16),
        [VMEM] * 3,
        flops=6 * experts * SLOTS * width * w_down.shape[1],
        bytes_accessed=6 * width * w_down.shape[1],
    )
    theirs = over_core(rows)
    mine_out = expert(rows, w_gate_up[0], w_down[0])
    their_out = expert(theirs, w_gate_up[0], w_down[0])
    other_out = over_core(their_out)
    summed = (mine_out.astype(F32) + other_out.astype(F32)).astype(BF16)
    back = lax.all_to_all(
        summed.reshape(experts, SLOTS, packed),
        ("req", "z"),
        split_axis=0,
        concat_axis=0,
        tiled=True,
    ).reshape(experts * SLOTS, packed)
    return call(
        final_kernel,
        sds((own, width), BF16),
        [VMEM] * 3,
        flops=1 << 27,
        bytes_accessed=1 << 22,
    )(back, table, residual)


def solution(mesh):
    req_count, exp_count = mesh.devices.shape
    split = Mesh(
        mesh.devices.reshape(req_count, exp_count // CORES, CORES), ("req", "z", "core")
    )
    exp = ("z", "core")
    everywhere = ("req", "z", "core")
    in_specs = (
        P("req", None),
        P(),
        P(None, None, exp),
        P(exp, None),
        P("req", exp, None),
        P("req", exp, None),
        P("req"),
        P("req", None),
        P(),
        P(),
        P(everywhere, None),
        P(everywhere, None, None),
        P(everywhere, None, None),
    )
    return jax.shard_map(
        per_device,
        mesh=split,
        in_specs=in_specs,
        out_specs=P(everywhere, None),
        check_vma=False,
    )
```

```python
import functools

import jax
import jax.numpy as jnp
from jax import lax
from jax.experimental import pallas as pl
from jax.experimental.pallas import tpu as pltpu
from jax.sharding import Mesh
from jax.sharding import PartitionSpec as P

HEAD_DIM = 128
EXP_SPLIT = 2
CORES = 2
CAP = 6
SLOTS = 8

EPSILON = 1e-05
NEGATIVE = -1e30
F32 = jnp.float32
BF16 = jnp.bfloat16
VMEM = pltpu.VMEM
SMEM = pltpu.SMEM
HBM = pltpu.HBM


def dot(a, b):
    return jnp.dot(a, b, preferred_element_type=F32)


def dot_t(a, b):
    return lax.dot_general(a, b, (((1,), (1,)), ((), ())), preferred_element_type=F32)


def iota(shape, axis):
    return lax.broadcasted_iota(jnp.int32, shape, axis)


def call(body, out, in_spaces, scratch=(), flops=0, bytes_accessed=0, vmem=10 << 20):
    out_spec = jax.tree.map(lambda _: pl.BlockSpec(memory_space=VMEM), out)
    return pl.pallas_call(
        body,
        out_shape=out,
        in_specs=[pl.BlockSpec(memory_space=s) for s in in_spaces],
        out_specs=out_spec,
        scratch_shapes=list(scratch),
        compiler_params=pltpu.CompilerParams(vmem_limit_bytes=vmem),
        cost_estimate=pl.CostEstimate(
            flops=flops, bytes_accessed=bytes_accessed, transcendentals=0
        ),
    )


def sds(shape, dtype):
    return jax.ShapeDtypeStruct(shape, dtype)


def normed_rows(values, gain):
    inverse = lax.rsqrt(jnp.mean(values * values, axis=-1, keepdims=True) + EPSILON)
    return (values * inverse * gain).astype(BF16)


def query_kernel(x_hbm, g_ref, w_hbm, q_ref, x_ref, w_ref, sems):
    x_copy = pltpu.make_async_copy(x_hbm, x_ref, sems.at[0])
    w_copy = pltpu.make_async_copy(w_hbm.at[0], w_ref, sems.at[1])
    x_copy.start()
    w_copy.start()
    x_copy.wait()
    normed = normed_rows(x_ref[...].astype(F32), g_ref[...].astype(F32))
    w_copy.wait()
    q_ref[...] = dot(normed, w_ref[...]).astype(BF16)


def tree_kernel(
    scale, x_ref, g_ref, w_hbm, q_ref, up_ref, o_ref, lse_ref, turn, w_ref, sems
):
    tokens, width = q_ref.shape
    w_copies = [
        pltpu.make_async_copy(w_hbm.at[i + 1], w_ref.at[i], sems.at[i]) for i in range(2)
    ]
    for w_copy in w_copies:
        w_copy.start()
    normed = normed_rows(x_ref[...].astype(F32), g_ref[...].astype(F32))
    w_copies[0].wait()
    keys = dot(normed, w_ref[0]).astype(BF16)
    w_copies[1].wait()
    values = dot(normed, w_ref[1]).astype(BF16)
    row = iota((tokens, tokens), 0)
    column = iota((tokens, tokens), 1)
    reach = jnp.where((row == column) | (up_ref[...] == column), 1.0, 0.0)
    for _ in range(6):
        half = reach.astype(BF16)
        reach = jnp.minimum(dot(half, half), 1.0)
    visible = reach > 0.5
    lane = iota((tokens, 128), 1)
    stats = jnp.zeros((tokens, 128), F32)
    for h in range(width // HEAD_DIM):
        cut = slice(h * HEAD_DIM, (h + 1) * HEAD_DIM)
        scores = dot_t(q_ref[:, cut], keys[:, cut]) * scale
        scores = jnp.where(visible, scores, NEGATIVE)
        high = jnp.max(scores, axis=-1, keepdims=True)
        weights = jnp.where(visible, jnp.exp(scores - high), 0.0)
        total = jnp.sum(weights, axis=-1, keepdims=True)
        o_ref[:, cut] = dot(weights.astype(BF16), values[:, cut]) / total
        stats = jnp.where(lane == h, high + jnp.log(total), stats)
    turn[0:tokens, :] = stats
    lse_ref[...] = jnp.transpose(turn[...])[0:8, :]


def page_kernel(scale, tree, kept, meta_ref, *refs):
    pieces, (k_hbm, v_hbm) = refs[:4], refs[4:6]
    outs = refs[7:-5] if kept else refs[6:-5]
    s_all, p_all, k_ref, v_ref, sems = refs[-5:]
    out_ref = outs[0]
    requests, page = k_hbm.shape[0], k_hbm.shape[1]
    width = pieces[0].shape[1]
    pair = 2 * tree
    lane = iota((tree, 128), 1)
    wide = iota((tree, width), 1) < HEAD_DIM
    first_at = 8 if kept else 12

    def copies(r, which):
        source, target = (k_hbm, k_ref) if which == 0 else (v_hbm, v_ref)
        found = []
        for i in range(len(pieces)):
            at = pl.ds(pl.multiple_of(meta_ref[first_at + i], width), width)
            found.append(
                pltpu.make_async_copy(
                    source.at[r, :, at], target.at[r, i], sems.at[which, r, i]
                )
            )
        return found

    for r in range(requests):

        @pl.when(meta_ref[r] > 0)
        def _():
            for which in range(2):
                for copy in copies(r, which):
                    copy.start()

    for r in range(requests):
        rows = slice(r * tree, (r + 1) * tree)
        live = meta_ref[r]

        @pl.when(live > 0)
        def _():
            for copy in copies(r, 0):
                copy.wait()
            for i, piece in enumerate(pieces):
                query = piece[rows, :]
                zero = jnp.zeros_like(query)
                both = jnp.concatenate(
                    [jnp.where(wide, query, zero), jnp.where(wide, zero, query)], axis=0
                )
                s_all[i * pair : (i + 1) * pair, :] = dot_t(both, k_ref[r, i])
            scores = s_all[...] * scale
            scores = jnp.where(iota(scores.shape, 1) < live, scores, NEGATIVE)
            high = jnp.max(scores, axis=-1, keepdims=True)
            weights = jnp.exp(scores - high)
            total = jnp.sum(weights, axis=-1, keepdims=True)
            p_all[...] = weights.astype(BF16)
            inverse = 1.0 / total
            lse = high + jnp.log(total)
            first = lse.astype(BF16).astype(F32)
            second = (lse - first).astype(BF16).astype(F32)
            third = lse - first - second
            stats = jnp.zeros((tree, 128), F32)
            for copy in copies(r, 1):
                copy.wait()
            for i in range(len(pieces)):
                summed = dot(p_all[i * pair : (i + 1) * pair, :], v_ref[r, i])
                for h in range(2):
                    own = slice(i * pair + h * tree, i * pair + (h + 1) * tree)
                    cut = slice(h * HEAD_DIM, (h + 1) * HEAD_DIM)
                    value = summed[h * tree : (h + 1) * tree, cut] * inverse[own]
                    out_ref[2 * i + h, rows, :] = value.astype(out_ref.dtype)
                    if kept:
                        stats = jnp.where(lane == i * 8 + h, lse[own], stats)
                    else:
                        for j, part in enumerate((first, second, third)):
                            stats = jnp.where(lane == i * 8 + 2 * j + h, part[own], stats)
            if kept:
                outs[1][rows, :] = stats
            else:
                out_ref[8, rows, :] = stats.astype(BF16)

        @pl.when(live <= 0)
        def _():
            for i in range(8):
                out_ref[i, rows, :] = jnp.zeros((tree, HEAD_DIM), out_ref.dtype)
            empty = jnp.where(lane % 8 < 2, NEGATIVE, 0.0)
            if kept:
                outs[1][rows, :] = empty
            else:
                out_ref[8, rows, :] = empty.astype(BF16)


def merge_kernel(other_ref, kept_ref, lse_ref, *refs):
    outs, turn = refs[:-1], refs[-1]
    tokens = lse_ref.shape[0]
    sent = other_ref[8].astype(F32)
    other = sent + pltpu.roll(sent, 126, 1) + pltpu.roll(sent, 124, 1)
    kept = lse_ref[...]
    high = jnp.maximum(other, kept)
    other, kept = jnp.exp(other - high), jnp.exp(kept - high)
    whole = other + kept
    inverse = 1.0 / whole
    other, kept = other * inverse, kept * inverse
    lse = jnp.where(iota(high.shape, 1) % 8 < 2, high + jnp.log(whole), 0.0)
    first = lse.astype(BF16).astype(F32)
    second = (lse - first).astype(BF16).astype(F32)
    third = lse - first - second
    turn[0:tokens, :] = first + pltpu.roll(second, 2, 1) + pltpu.roll(third, 4, 1)
    turn[tokens:, :] = jnp.zeros((turn.shape[0] - tokens, 128), F32)
    turned = jnp.transpose(turn[...])
    for i, out_ref in enumerate(outs):
        for h in range(2):
            at = i * 8 + h
            value = other[:, at : at + 1] * other_ref[2 * i + h].astype(F32)
            value = value + kept[:, at : at + 1] * kept_ref[2 * i + h]
            out_ref[0:tokens, h * HEAD_DIM : (h + 1) * HEAD_DIM] = value.astype(BF16)
        out_ref[tokens:, :] = turned[i * 8 : (i + 1) * 8, :].astype(BF16)


def out_kernel(meta_ref, *refs):
    parts = refs[:4]
    tree_o_ref, tree_lse_ref, w_ref, theirs_ref, ours_ref, turn, mixed = refs[4:]
    padded, width = parts[0].shape
    tokens = padded - 8
    heads = width // HEAD_DIM
    own = ours_ref.shape[0] // 4
    lses = []
    for part in parts:
        rows = part[tokens:, :].astype(F32)
        lses.append(rows[0:2] + rows[2:4] + rows[4:6])
    lses.append(tree_lse_ref[0:2, :])
    high = functools.reduce(jnp.maximum, lses)
    factors = [jnp.exp(value - high) for value in lses]
    whole = functools.reduce(lambda a, b: a + b, factors)
    for s, factor in enumerate(factors):
        turn[2 * s : 2 * s + 2, :] = factor / whole
    turned = jnp.transpose(turn[...])[0:tokens, :]
    for h in range(heads):
        cut = slice(h * HEAD_DIM, (h + 1) * HEAD_DIM)
        at = 2 * len(parts) + h
        total = turned[:, at : at + 1] * tree_o_ref[:, cut]
        for s, part in enumerate(parts):
            at = 2 * s + h
            total = total + turned[:, at : at + 1] * part[0:tokens, cut].astype(F32)
        mixed[:, cut] = total

    def rows_of(first_at):
        rows = [
            mixed[pl.ds(pl.multiple_of(meta_ref[first_at + i], 8), own), :] for i in range(4)
        ]
        return jnp.concatenate(rows, axis=0).astype(BF16)

    theirs_ref[...] = dot(rows_of(20), w_ref[...]).astype(BF16)
    ours_ref[...] = dot(rows_of(16), w_ref[...])


def fold_kernel(ours_ref, theirs_ref, *outs):
    own = outs[0].shape[0]
    for i, out_ref in enumerate(outs):
        rows = slice(i * own, (i + 1) * own)
        out_ref[...] = (ours_ref[rows, :] + theirs_ref[rows, :].astype(F32)).astype(out_ref.dtype)


def expert_of_row(rows, experts):
    return jnp.where(iota((rows, experts), 0) // SLOTS == iota((rows, experts), 1), 1.0, 0.0)


def place_kernel(routes_ref, place_ref):
    top, tokens = routes_ref.shape
    chunks, rows, _ = place_ref.shape
    experts = rows // SLOTS
    named = iota((experts, tokens), 0)
    chosen = jnp.zeros((experts, tokens), F32)
    for k in range(top):
        chosen = jnp.where(routes_ref[k : k + 1, :] == named, 1.0, chosen)
    source = iota((tokens, 2 * tokens), 0)
    target = iota((tokens, 2 * tokens), 1) % tokens
    chosen = chosen.astype(BF16)
    rank = dot(chosen, jnp.where(source < target, 1.0, 0.0).astype(BF16))
    both = dot(chosen, jnp.where(source == target, 1.0, 0.0).astype(BF16))
    rank = jnp.where(both > 0.5, rank, -1.0).astype(BF16)
    spread = dot(expert_of_row(rows, experts).astype(BF16), rank)
    slot = iota((rows, 2 * tokens), 0) % SLOTS
    is_tail = iota((rows, 2 * tokens), 1) >= tokens
    for j in range(chunks):
        wanted = jnp.where(is_tail, (slot - CAP) * chunks + j, slot)
        valid = is_tail == (slot >= CAP)
        hit = valid & (spread == wanted.astype(F32))
        place_ref[j] = jnp.where(hit, 1.0, 0.0).astype(BF16)


def residual_kernel(meta_ref, *refs):
    parts = refs[:4]
    x_ref, g_ref, place_ref, res_ref, normed_ref, out_ref = refs[4:]
    tokens, width = parts[0].shape
    chunks = place_ref.shape[0]
    cut = width // (chunks + 1)
    start = pl.multiple_of(meta_ref[16], 8)
    residual = x_ref[pl.ds(start, tokens), :].astype(F32)
    for part in parts:
        residual = residual + part[...].astype(F32)
    res_ref[...] = residual
    inverse = lax.rsqrt(jnp.mean(residual * residual, axis=-1, keepdims=True) + EPSILON)
    normed = residual * inverse * g_ref[...].astype(F32)
    normed_ref[...] = normed.astype(BF16)
    tail = normed[:, chunks * cut :]
    for j in range(chunks):
        pair = jnp.concatenate([normed[:, j * cut : (j + 1) * cut], tail], axis=0).astype(BF16)
        out_ref[:, j * cut : (j + 1) * cut] = dot(place_ref[j], pair).astype(BF16)


def gate_kernel(normed_ref, router_ref, routes_ref, table_ref):
    tokens, top = routes_ref.shape
    experts = router_ref.shape[0]
    chunks, _, rows = table_ref.shape
    logits = dot_t(normed_ref[...], router_ref[...])
    exponent = jnp.exp(logits)
    chances = exponent / jnp.sum(exponent, axis=-1, keepdims=True)
    named = iota((tokens, experts), 1)
    chosen = jnp.zeros((tokens, experts), F32)
    for k in range(top):
        chosen = jnp.where(routes_ref[:, k : k + 1] == named, 1.0, chosen)
    picked = chances * chosen
    gates = picked / jnp.sum(picked, axis=-1, keepdims=True)
    earlier = jnp.where(iota((tokens, tokens), 0) > iota((tokens, tokens), 1), 1.0, 0.0)
    rank = dot(earlier.astype(BF16), chosen.astype(BF16))
    rank = jnp.where(chosen > 0.5, rank, -1.0).astype(BF16)
    first = gates.astype(BF16)
    second = (gates - first.astype(F32)).astype(BF16)
    home = iota((experts, rows), 0) == iota((experts, rows), 1) // SLOTS
    home = jnp.where(home, 1.0, 0.0).astype(BF16)
    rank, first, second = dot(rank, home), dot(first, home), dot(second, home)
    slot = iota((tokens, rows), 1) % SLOTS
    main = (slot < CAP) & (rank == slot.astype(F32))
    for j in range(chunks):
        tail = (slot >= CAP) & (rank == ((slot - CAP) * chunks + j).astype(F32))
        table_ref[j] = jnp.concatenate(
            [
                jnp.where(main, first, 0.0),
                jnp.where(main, second, 0.0),
                jnp.where(tail, first, 0.0),
                jnp.where(tail, second, 0.0),
            ],
            axis=0,
        ).astype(BF16)


def expert_kernel(first_row, x_ref, gate_up_ref, down_ref, *refs):
    out_ref = refs[-1]
    block, packed = out_ref.shape
    width, both = gate_up_ref.shape
    units = both // 2
    cut = width - packed
    chunks = packed // cut
    a = iota((block, block), 0)
    b = iota((block, block), 1)
    same = a // SLOTS == b // SLOTS
    slot_a, slot_b = a % SLOTS, b % SLOTS
    unpack, pack = [], []
    for k in range(chunks):
        hit = same & (slot_a < CAP) & (slot_b >= CAP) & (slot_a == (slot_b - CAP) * chunks + k)
        unpack.append(jnp.where(hit, 1.0, 0.0).astype(BF16))
        hit = same & (slot_b < CAP) & (slot_a >= CAP) & (slot_b == (slot_a - CAP) * chunks + k)
        pack.append(jnp.where(hit, 1.0, 0.0).astype(BF16))
    is_tail = iota((block, cut), 0) % SLOTS >= CAP
    span = slice(first_row, first_row + block)
    tail = dot(unpack[0], x_ref[span, 0:cut])
    for k in range(1, chunks):
        tail = tail + dot(unpack[k], x_ref[span, k * cut : (k + 1) * cut])
    up = dot(x_ref[span, :], gate_up_ref[0:packed, :])
    up = up + dot(tail.astype(BF16), gate_up_ref[packed:, :])
    gate = up[:, :units]
    hidden = (gate / (1.0 + jnp.exp(-gate)) * up[:, units:]).astype(BF16)
    last = dot(hidden, down_ref[:, packed:]).astype(BF16)
    for k in range(chunks):
        main = dot(hidden, down_ref[:, k * cut : (k + 1) * cut])
        out_ref[:, k * cut : (k + 1) * cut] = jnp.where(
            is_tail, dot(pack[k], last), main
        ).astype(BF16)


def add_kernel(*refs):
    out_ref = refs[-1]
    at = 0
    for first, second in zip(refs[0:-1:2], refs[1:-1:2]):
        rows = first.shape[0]
        total = first[...].astype(F32) + second[...].astype(F32)
        out_ref[at : at + rows, :] = total.astype(BF16)
        at += rows


def final_kernel(back_ref, table_ref, res_ref, out_ref):
    tokens, width = res_ref.shape
    chunks = table_ref.shape[0]
    cut = width // (chunks + 1)
    tail = res_ref[:, chunks * cut :]
    for j in range(chunks):
        span = slice(j * cut, (j + 1) * cut)
        sums = dot(table_ref[j], back_ref[:, span])
        main = sums[0:tokens] + sums[tokens : 2 * tokens]
        out_ref[:, span] = (res_ref[:, span] + main).astype(BF16)
        tail = tail + (sums[2 * tokens : 3 * tokens] + sums[3 * tokens :])
    out_ref[:, chunks * cut :] = tail.astype(BF16)


def per_device(
    hidden,
    gain_attn,
    w_qkv,
    w_out,
    cache_keys,
    cache_values,
    cache_lengths,
    parents,
    gain_moe,
    w_router,
    routes,
    w_gate_up,
    w_down,
):
    z_count = lax.axis_size("z")
    exp_count = z_count * CORES
    z_index = lax.axis_index("z")
    core = lax.axis_index("core")
    exp_index = z_index * CORES + core
    tokens, width = hidden.shape
    requests, tree = parents.shape
    page = cache_keys.shape[1]
    local_width = w_qkv.shape[2]
    scale = HEAD_DIM ** (-0.5)
    own = tokens // exp_count
    experts = w_router.shape[1]
    packed = width * CAP // SLOTS
    chunks = packed // (width - packed)
    padded = tokens + 8

    gain_a = gain_attn.reshape(1, width)
    gain_m = gain_moe.reshape(1, width)
    w_three = pltpu.with_memory_space_constraint(jnp.transpose(w_qkv, (1, 0, 2)), HBM)
    cache_keys = pltpu.with_memory_space_constraint(cache_keys, HBM)
    cache_values = pltpu.with_memory_space_constraint(cache_values, HBM)

    query = call(
        query_kernel,
        sds((tokens, local_width), BF16),
        [HBM, VMEM, HBM],
        [
            pltpu.VMEM((tokens, width), BF16),
            pltpu.VMEM((width, local_width), BF16),
            pltpu.SemaphoreType.DMA((2,)),
        ],
        flops=2 * tokens * width * local_width,
        bytes_accessed=2 * width * (tokens + local_width),
    )(pltpu.with_memory_space_constraint(hidden, HBM), gain_a, w_three)

    def over_z(value, step):
        return lax.ppermute(value, "z", [(i, (i + step) % z_count) for i in range(z_count)])

    def over_core(value):
        return lax.ppermute(value, "core", [(0, 1), (1, 0)])

    steps = range(1, z_count)
    pieces = [query] + [over_z(query, step) for step in steps]
    other_pieces = [over_core(piece) for piece in pieces]
    homes = jnp.bitwise_and(z_index - jnp.arange(z_count), z_count - 1) * CORES
    homes = jnp.stack([homes + core, homes + 1 - core])
    meta = jnp.concatenate(
        [
            cache_lengths - exp_index * page,
            jnp.zeros((8 - requests,), jnp.int32),
            (homes * local_width).reshape(-1),
            (homes * own).reshape(-1),
        ]
    ).astype(jnp.int32)

    up = (parents + tree * jnp.arange(requests, dtype=jnp.int32)[:, None]).reshape(tokens, 1)
    tree_o, tree_lse = call(
        functools.partial(tree_kernel, scale),
        (sds((tokens, local_width), F32), sds((8, 256), F32)),
        [VMEM, VMEM, HBM, VMEM, VMEM],
        [
            pltpu.VMEM((256, 128), F32),
            pltpu.VMEM((2, width, local_width), BF16),
            pltpu.SemaphoreType.DMA((2,)),
        ],
        flops=4 * tokens * width * local_width,
        bytes_accessed=2 * width * (tokens + 2 * local_width),
    )(hidden, gain_a, w_three, query, up)

    place = call(
        place_kernel,
        sds((chunks, experts * SLOTS, 2 * own), BF16),
        [VMEM],
        flops=1 << 22,
        bytes_accessed=1 << 18,
    )(routes.T)

    scratch = [
        pltpu.VMEM((z_count * 2 * tree, page), F32),
        pltpu.VMEM((z_count * 2 * tree, page), BF16),
        pltpu.VMEM((requests, z_count, page, local_width), BF16),
        pltpu.VMEM((requests, z_count, page, local_width), BF16),
        pltpu.SemaphoreType.DMA((2, requests, z_count)),
    ]
    heads = 2 * z_count
    for_other = call(
        functools.partial(page_kernel, scale, tree, False),
        sds((heads + 1, tokens, HEAD_DIM), BF16),
        [SMEM] + [VMEM] * 4 + [HBM] * 2,
        scratch,
        flops=2 * tokens * page * width,
        bytes_accessed=2 * requests * page * width,
        vmem=20 << 20,
    )(meta, *other_pieces, cache_keys, cache_values)
    from_other = over_core(for_other)
    kept, kept_lse = call(
        functools.partial(page_kernel, scale, tree, True),
        (sds((heads, tokens, HEAD_DIM), F32), sds((tokens, 128), F32)),
        [SMEM] + [VMEM] * 4 + [HBM] * 2 + [pl.ANY],
        scratch,
        flops=2 * tokens * page * width,
        bytes_accessed=2 * requests * page * width,
        vmem=20 << 20,
    )(meta, *pieces, cache_keys, cache_values, for_other)
    merged = call(
        merge_kernel,
        tuple(sds((padded, local_width), BF16) for _ in range(z_count)),
        [VMEM] * 3,
        [pltpu.VMEM((256, 128), F32)],
        bytes_accessed=1 << 20,
    )(from_other, kept, kept_lse)
    arrived = [merged[0]] + [over_z(merged[step], -step) for step in steps]
    theirs, ours = call(
        out_kernel,
        (sds((z_count * own, width), BF16), sds((z_count * own, width), F32)),
        [SMEM] + [VMEM] * 7,
        [pltpu.VMEM((128, 256), F32), pltpu.VMEM((tokens, local_width), F32)],
        flops=2 * tokens * width * local_width,
        bytes_accessed=2 * width * (tokens + local_width),
    )(meta, *arrived, tree_o, tree_lse, w_out)
    folded = call(
        fold_kernel,
        tuple(sds((own, width), BF16 if step else F32) for step in range(z_count)),
        [VMEM] * 2,
        bytes_accessed=1 << 20,
    )(ours, over_core(theirs))
    mixed = [folded[0]] + [over_z(folded[step], -step) for step in steps]

    residual, normed, outgoing = call(
        residual_kernel,
        (
            sds((own, width), F32),
            sds((own, width), BF16),
            sds((experts * SLOTS, packed), BF16),
        ),
        [SMEM] + [VMEM] * 7,
        flops=1 << 27,
        bytes_accessed=1 << 22,
    )(meta, *mixed, hidden, gain_m, place)
    rows = lax.all_to_all(
        outgoing.reshape(experts, SLOTS, packed),
        ("req", "z"),
        split_axis=0,
        concat_axis=0,
        tiled=True,
    ).reshape(experts * SLOTS, packed)
    table = call(
        gate_kernel,
        sds((chunks, 4 * own, experts * SLOTS), BF16),
        [VMEM] * 3,
        flops=1 << 24,
        bytes_accessed=1 << 19,
    )(normed, w_router.T, routes)

    block = experts * SLOTS // 2

    def expert(values, half, after=None):
        extra = [] if after is None else [after]
        return call(
            functools.partial(expert_kernel, half * block),
            sds((block, packed), BF16),
            [VMEM] * 3 + [pl.ANY] * len(extra),
            flops=6 * block * width * w_down.shape[1],
            bytes_accessed=6 * width * w_down.shape[1],
            vmem=20 << 20,
        )(values, w_gate_up[0], w_down[0], *extra)

    theirs = over_core(rows)
    mine_0 = expert(rows, 0)
    theirs_0 = expert(theirs, 0, mine_0)
    theirs_1 = expert(theirs, 1, theirs_0)
    mine_1 = expert(rows, 1, theirs_1)
    summed = call(
        add_kernel,
        sds((experts * SLOTS, packed), BF16),
        [VMEM] * 4,
        bytes_accessed=1 << 22,
    )(mine_0, over_core(theirs_0), mine_1, over_core(theirs_1))
    back = lax.all_to_all(
        summed.reshape(experts, SLOTS, packed),
        ("req", "z"),
        split_axis=0,
        concat_axis=0,
        tiled=True,
    ).reshape(experts * SLOTS, packed)
    return call(
        final_kernel,
        sds((own, width), BF16),
        [VMEM] * 3,
        flops=1 << 27,
        bytes_accessed=1 << 22,
    )(back, table, residual)


def solution(mesh):
    req_count, exp_count = mesh.devices.shape
    split = Mesh(
        mesh.devices.reshape(req_count, exp_count // CORES, CORES), ("req", "z", "core")
    )
    exp = ("z", "core")
    everywhere = ("req", "z", "core")
    in_specs = (
        P("req", None),
        P(),
        P(None, None, exp),
        P(exp, None),
        P("req", exp, None),
        P("req", exp, None),
        P("req"),
        P("req", None),
        P(),
        P(),
        P(everywhere, None),
        P(everywhere, None, None),
        P(everywhere, None, None),
    )
    return jax.shard_map(
        per_device,
        mesh=split,
        in_specs=in_specs,
        out_specs=P(everywhere, None),
        check_vma=False,
    )
```

```python
import functools

import jax
import jax.numpy as jnp
from jax import lax
from jax.experimental import pallas as pl
from jax.experimental.pallas import tpu as pltpu
from jax.sharding import Mesh
from jax.sharding import PartitionSpec as P

HEAD_DIM = 128
EXP_SPLIT = 2
CORES = 2
CAP = 6
SLOTS = 8

EPSILON = 1e-05
NEGATIVE = -1e30
F32 = jnp.float32
BF16 = jnp.bfloat16
VMEM = pltpu.VMEM
SMEM = pltpu.SMEM
HBM = pltpu.HBM


def dot(a, b):
    return jnp.dot(a, b, preferred_element_type=F32)


def dot_t(a, b):
    return lax.dot_general(a, b, (((1,), (1,)), ((), ())), preferred_element_type=F32)


def iota(shape, axis):
    return lax.broadcasted_iota(jnp.int32, shape, axis)


def call(body, out, in_spaces, scratch=(), flops=0, bytes_accessed=0, vmem=10 << 20, aliases={}):
    out_spec = jax.tree.map(lambda _: pl.BlockSpec(memory_space=VMEM), out)
    return pl.pallas_call(
        body,
        out_shape=out,
        in_specs=[pl.BlockSpec(memory_space=s) for s in in_spaces],
        out_specs=out_spec,
        scratch_shapes=list(scratch),
        input_output_aliases=aliases,
        compiler_params=pltpu.CompilerParams(vmem_limit_bytes=vmem),
        cost_estimate=pl.CostEstimate(
            flops=flops, bytes_accessed=bytes_accessed, transcendentals=0
        ),
    )


def sds(shape, dtype):
    return jax.ShapeDtypeStruct(shape, dtype)


def normed_rows(values, gain):
    inverse = lax.rsqrt(jnp.mean(values * values, axis=-1, keepdims=True) + EPSILON)
    return (values * inverse * gain).astype(BF16)


def query_kernel(x_hbm, g_ref, w_hbm, q_ref, x_ref, w_ref, sems):
    x_copy = pltpu.make_async_copy(x_hbm, x_ref, sems.at[0])
    w_copy = pltpu.make_async_copy(w_hbm.at[0], w_ref, sems.at[1])
    x_copy.start()
    w_copy.start()
    x_copy.wait()
    normed = normed_rows(x_ref[...].astype(F32), g_ref[...].astype(F32).reshape(1, -1))
    w_copy.wait()
    q_ref[...] = dot(normed, w_ref[...]).astype(BF16)


def tree_kernel(scale, x_ref, g_ref, w_hbm, q_ref, up_ref, k_hbm, v_hbm, *refs):
    o_ref, lse_ref, k_ref, v_ref, turn, w_ref, sems = refs
    tokens, width = q_ref.shape
    w_copies = [
        pltpu.make_async_copy(w_hbm.at[i + 1], w_ref.at[i], sems.at[i]) for i in range(2)
    ]
    for w_copy in w_copies:
        w_copy.start()
    k_copy = pltpu.make_async_copy(k_hbm, k_ref, sems.at[2])
    v_copy = pltpu.make_async_copy(v_hbm, v_ref, sems.at[3])
    k_copy.start()
    v_copy.start()
    normed = normed_rows(x_ref[...].astype(F32), g_ref[...].astype(F32).reshape(1, -1))
    w_copies[0].wait()
    keys = dot(normed, w_ref[0]).astype(BF16)
    w_copies[1].wait()
    values = dot(normed, w_ref[1]).astype(BF16)
    row = iota((tokens, tokens), 0)
    column = iota((tokens, tokens), 1)
    reach = jnp.where((row == column) | (up_ref[...] == column), 1.0, 0.0)
    for _ in range(6):
        half = reach.astype(BF16)
        reach = jnp.minimum(dot(half, half), 1.0)
    visible = reach > 0.5
    lane = iota((tokens, 128), 1)
    stats = jnp.zeros((tokens, 128), F32)
    for h in range(width // HEAD_DIM):
        cut = slice(h * HEAD_DIM, (h + 1) * HEAD_DIM)
        scores = dot_t(q_ref[:, cut], keys[:, cut]) * scale
        scores = jnp.where(visible, scores, NEGATIVE)
        high = jnp.max(scores, axis=-1, keepdims=True)
        weights = jnp.where(visible, jnp.exp(scores - high), 0.0)
        total = jnp.sum(weights, axis=-1, keepdims=True)
        o_ref[:, cut] = dot(weights.astype(BF16), values[:, cut]) / total
        stats = jnp.where(lane == h, high + jnp.log(total), stats)
    turn[0:tokens, :] = stats
    lse_ref[...] = jnp.transpose(turn[...])[0:8, :]
    k_copy.wait()
    v_copy.wait()


def page_kernel(scale, tree, kept, meta_ref, *refs):
    pieces, (k_ref, v_ref) = refs[:4], refs[4:6]
    outs = refs[7:-2] if kept else refs[6:-2]
    s_all, p_all = refs[-2:]
    out_ref = outs[0]
    requests, page = k_ref.shape[0], k_ref.shape[1]
    width = pieces[0].shape[1]
    pair = 2 * tree
    lane = iota((tree, 128), 1)
    wide = iota((tree, width), 1) < HEAD_DIM
    first_at = 8 if kept else 12

    def columns(i):
        return pl.ds(pl.multiple_of(meta_ref[first_at + i], width), width)

    for r in range(requests):
        rows = slice(r * tree, (r + 1) * tree)
        live = meta_ref[r]

        @pl.when(live > 0)
        def _():
            for i, piece in enumerate(pieces):
                query = piece[rows, :]
                zero = jnp.zeros_like(query)
                both = jnp.concatenate(
                    [jnp.where(wide, query, zero), jnp.where(wide, zero, query)], axis=0
                )
                s_all[i * pair : (i + 1) * pair, :] = dot_t(both, k_ref[r, :, columns(i)])
            scores = s_all[...] * scale
            scores = jnp.where(iota(scores.shape, 1) < live, scores, NEGATIVE)
            high = jnp.max(scores, axis=-1, keepdims=True)
            weights = jnp.exp(scores - high)
            total = jnp.sum(weights, axis=-1, keepdims=True)
            p_all[...] = weights.astype(BF16)
            inverse = 1.0 / total
            lse = high + jnp.log(total)
            first = lse.astype(BF16).astype(F32)
            second = (lse - first).astype(BF16).astype(F32)
            third = lse - first - second
            stats = jnp.zeros((tree, 128), F32)
            for i in range(len(pieces)):
                summed = dot(p_all[i * pair : (i + 1) * pair, :], v_ref[r, :, columns(i)])
                for h in range(2):
                    own = slice(i * pair + h * tree, i * pair + (h + 1) * tree)
                    cut = slice(h * HEAD_DIM, (h + 1) * HEAD_DIM)
                    value = summed[h * tree : (h + 1) * tree, cut] * inverse[own]
                    out_ref[2 * i + h, rows, :] = value.astype(out_ref.dtype)
                    if kept:
                        stats = jnp.where(lane == i * 8 + h, lse[own], stats)
                    else:
                        for j, part in enumerate((first, second, third)):
                            stats = jnp.where(lane == i * 8 + 2 * j + h, part[own], stats)
            if kept:
                outs[1][rows, :] = stats
            else:
                out_ref[8, rows, :] = stats.astype(BF16)

        @pl.when(live <= 0)
        def _():
            for i in range(8):
                out_ref[i, rows, :] = jnp.zeros((tree, HEAD_DIM), out_ref.dtype)
            empty = jnp.where(lane % 8 < 2, NEGATIVE, 0.0)
            if kept:
                outs[1][rows, :] = empty
            else:
                out_ref[8, rows, :] = empty.astype(BF16)


def merge_kernel(other_ref, kept_ref, lse_ref, *refs):
    outs, turn = refs[:-1], refs[-1]
    tokens = lse_ref.shape[0]
    sent = other_ref[8].astype(F32)
    other = sent + pltpu.roll(sent, 126, 1) + pltpu.roll(sent, 124, 1)
    kept = lse_ref[...]
    high = jnp.maximum(other, kept)
    other, kept = jnp.exp(other - high), jnp.exp(kept - high)
    whole = other + kept
    inverse = 1.0 / whole
    other, kept = other * inverse, kept * inverse
    lse = jnp.where(iota(high.shape, 1) % 8 < 2, high + jnp.log(whole), 0.0)
    first = lse.astype(BF16).astype(F32)
    second = (lse - first).astype(BF16).astype(F32)
    third = lse - first - second
    turn[0:tokens, :] = first + pltpu.roll(second, 2, 1) + pltpu.roll(third, 4, 1)
    turn[tokens:, :] = jnp.zeros((turn.shape[0] - tokens, 128), F32)
    turned = jnp.transpose(turn[...])
    for i, out_ref in enumerate(outs):
        for h in range(2):
            at = i * 8 + h
            value = other[:, at : at + 1] * other_ref[2 * i + h].astype(F32)
            value = value + kept[:, at : at + 1] * kept_ref[2 * i + h]
            out_ref[0:tokens, h * HEAD_DIM : (h + 1) * HEAD_DIM] = value.astype(BF16)
        out_ref[tokens:, :] = turned[i * 8 : (i + 1) * 8, :].astype(BF16)


def out_kernel(meta_ref, *refs):
    parts = refs[:4]
    tree_o_ref, tree_lse_ref, w_ref, theirs_ref, ours_ref, turn, mixed = refs[4:]
    padded, width = parts[0].shape
    tokens = padded - 8
    heads = width // HEAD_DIM
    own = ours_ref.shape[0] // 4
    lses = []
    for part in parts:
        rows = part[tokens:, :].astype(F32)
        lses.append(rows[0:2] + rows[2:4] + rows[4:6])
    lses.append(tree_lse_ref[0:2, :])
    high = functools.reduce(jnp.maximum, lses)
    factors = [jnp.exp(value - high) for value in lses]
    whole = functools.reduce(lambda a, b: a + b, factors)
    for s, factor in enumerate(factors):
        turn[2 * s : 2 * s + 2, :] = factor / whole
    turned = jnp.transpose(turn[...])[0:tokens, :]
    for h in range(heads):
        cut = slice(h * HEAD_DIM, (h + 1) * HEAD_DIM)
        at = 2 * len(parts) + h
        total = turned[:, at : at + 1] * tree_o_ref[:, cut]
        for s, part in enumerate(parts):
            at = 2 * s + h
            total = total + turned[:, at : at + 1] * part[0:tokens, cut].astype(F32)
        mixed[:, cut] = total

    def rows_of(first_at):
        rows = [
            mixed[pl.ds(pl.multiple_of(meta_ref[first_at + i], 8), own), :] for i in range(4)
        ]
        return jnp.concatenate(rows, axis=0).astype(BF16)

    theirs_ref[...] = dot(rows_of(20), w_ref[...]).astype(BF16)
    ours_ref[...] = dot(rows_of(16), w_ref[...])


def fold_kernel(ours_ref, theirs_ref, *outs):
    own = outs[0].shape[0]
    for i, out_ref in enumerate(outs):
        rows = slice(i * own, (i + 1) * own)
        out_ref[...] = (ours_ref[rows, :] + theirs_ref[rows, :].astype(F32)).astype(out_ref.dtype)


def expert_of_row(rows, experts):
    return jnp.where(iota((rows, experts), 0) // SLOTS == iota((rows, experts), 1), 1.0, 0.0)


def place_kernel(routes_ref, after_ref, up_hbm, down_hbm, *refs):
    place_ref, pack_ref, up_ref, down_ref, sems = refs
    del after_ref
    up_copy = pltpu.make_async_copy(up_hbm, up_ref, sems.at[0])
    down_copy = pltpu.make_async_copy(down_hbm, down_ref, sems.at[1])
    up_copy.start()
    down_copy.start()
    block = pack_ref.shape[1]
    a = iota((block, block), 0)
    b = iota((block, block), 1)
    same = a // SLOTS == b // SLOTS
    slot_a, slot_b = a % SLOTS, b % SLOTS
    chunks = place_ref.shape[0]
    for k in range(chunks):
        hit = same & (slot_a < CAP) & (slot_b >= CAP) & (slot_a == (slot_b - CAP) * chunks + k)
        pack_ref[k] = jnp.where(hit, 1.0, 0.0).astype(BF16)
        hit = same & (slot_b < CAP) & (slot_a >= CAP) & (slot_b == (slot_a - CAP) * chunks + k)
        pack_ref[chunks + k] = jnp.where(hit, 1.0, 0.0).astype(BF16)
    top, tokens = routes_ref.shape
    chunks, rows, _ = place_ref.shape
    experts = rows // SLOTS
    named = iota((experts, tokens), 0)
    chosen = jnp.zeros((experts, tokens), F32)
    for k in range(top):
        chosen = jnp.where(routes_ref[k : k + 1, :] == named, 1.0, chosen)
    source = iota((tokens, 2 * tokens), 0)
    target = iota((tokens, 2 * tokens), 1) % tokens
    chosen = chosen.astype(BF16)
    rank = dot(chosen, jnp.where(source < target, 1.0, 0.0).astype(BF16))
    both = dot(chosen, jnp.where(source == target, 1.0, 0.0).astype(BF16))
    rank = jnp.where(both > 0.5, rank, -1.0).astype(BF16)
    spread = dot(expert_of_row(rows, experts).astype(BF16), rank)
    slot = iota((rows, 2 * tokens), 0) % SLOTS
    is_tail = iota((rows, 2 * tokens), 1) >= tokens
    for j in range(chunks):
        wanted = jnp.where(is_tail, (slot - CAP) * chunks + j, slot)
        valid = is_tail == (slot >= CAP)
        hit = valid & (spread == wanted.astype(F32))
        place_ref[j] = jnp.where(hit, 1.0, 0.0).astype(BF16)
    up_copy.wait()
    down_copy.wait()


def residual_kernel(meta_ref, *refs):
    parts = refs[:4]
    x_ref, g_ref, place_ref, res_ref, normed_ref, out_ref = refs[4:]
    tokens, width = parts[0].shape
    chunks = place_ref.shape[0]
    cut = width // (chunks + 1)
    start = pl.multiple_of(meta_ref[16], 8)
    residual = x_ref[pl.ds(start, tokens), :].astype(F32)
    for part in parts:
        residual = residual + part[...].astype(F32)
    res_ref[...] = residual
    inverse = lax.rsqrt(jnp.mean(residual * residual, axis=-1, keepdims=True) + EPSILON)
    normed = residual * inverse * g_ref[...].astype(F32).reshape(1, -1)
    normed_ref[...] = normed.astype(BF16)
    tail = normed[:, chunks * cut :]
    for j in range(chunks):
        pair = jnp.concatenate([normed[:, j * cut : (j + 1) * cut], tail], axis=0).astype(BF16)
        out_ref[:, j * cut : (j + 1) * cut] = dot(place_ref[j], pair).astype(BF16)


def gate_kernel(normed_ref, router_ref, routes_ref, after_ref, table_ref):
    del after_ref
    top, tokens = routes_ref.shape
    experts = router_ref.shape[0]
    chunks, _, rows = table_ref.shape
    logits = dot_t(normed_ref[...], router_ref[...])
    exponent = jnp.exp(logits)
    chances = exponent / jnp.sum(exponent, axis=-1, keepdims=True)
    named = iota((experts, tokens), 0)
    chosen = jnp.zeros((experts, tokens), F32)
    for k in range(top):
        chosen = jnp.where(routes_ref[k : k + 1, :] == named, 1.0, chosen)
    same = jnp.where(iota((tokens, tokens), 0) == iota((tokens, tokens), 1), 1.0, 0.0)
    chosen = dot_t(same.astype(BF16), chosen.astype(BF16))
    picked = chances * chosen
    gates = picked / jnp.sum(picked, axis=-1, keepdims=True)
    earlier = jnp.where(iota((tokens, tokens), 0) > iota((tokens, tokens), 1), 1.0, 0.0)
    rank = dot(earlier.astype(BF16), chosen.astype(BF16))
    rank = jnp.where(chosen > 0.5, rank, -1.0).astype(BF16)
    first = gates.astype(BF16)
    second = (gates - first.astype(F32)).astype(BF16)
    home = iota((experts, rows), 0) == iota((experts, rows), 1) // SLOTS
    home = jnp.where(home, 1.0, 0.0).astype(BF16)
    rank, first, second = dot(rank, home), dot(first, home), dot(second, home)
    slot = iota((tokens, rows), 1) % SLOTS
    main = (slot < CAP) & (rank == slot.astype(F32))
    for j in range(chunks):
        tail = (slot >= CAP) & (rank == ((slot - CAP) * chunks + j).astype(F32))
        table_ref[j] = jnp.concatenate(
            [
                jnp.where(main, first, 0.0),
                jnp.where(main, second, 0.0),
                jnp.where(tail, first, 0.0),
                jnp.where(tail, second, 0.0),
            ],
            axis=0,
        ).astype(BF16)


def expert_kernel(first_row, x_ref, gate_up_ref, down_ref, pack_ref, *refs):
    out_ref = refs[-1]
    block = pack_ref.shape[1]
    packed = x_ref.shape[1]
    width, both = gate_up_ref.shape
    units = both // 2
    cut = width - packed
    chunks = packed // cut
    unpack = [pack_ref[k] for k in range(chunks)]
    pack = [pack_ref[chunks + k] for k in range(chunks)]
    is_tail = iota((block, cut), 0) % SLOTS >= CAP
    span = slice(first_row, first_row + block)
    tail = dot(unpack[0], x_ref[span, 0:cut])
    for k in range(1, chunks):
        tail = tail + dot(unpack[k], x_ref[span, k * cut : (k + 1) * cut])
    up = dot(x_ref[span, :], gate_up_ref[0:packed, :])
    up = up + dot(tail.astype(BF16), gate_up_ref[packed:, :])
    gate = up[:, :units]
    hidden = (gate / (1.0 + jnp.exp(-gate)) * up[:, units:]).astype(BF16)
    last = dot(hidden, down_ref[:, packed:]).astype(BF16)
    last_call = out_ref.shape[0] > block
    if last_call:
        own_ref, other_ref = refs[0], refs[1]
        total = own_ref[...].astype(F32) + other_ref[...].astype(F32)
        out_ref[0:block, :] = total.astype(BF16)
    at = block if last_call else 0
    for k in range(chunks):
        main = dot(hidden, down_ref[:, k * cut : (k + 1) * cut])
        out_ref[at : at + block, k * cut : (k + 1) * cut] = jnp.where(
            is_tail, dot(pack[k], last), main
        ).astype(BF16)


def add_kernel(values_ref, other_ref, out_ref):
    at = out_ref.shape[0] - other_ref.shape[0]
    total = values_ref[at:, :].astype(F32) + other_ref[...].astype(F32)
    out_ref[at:, :] = total.astype(BF16)


def final_kernel(back_ref, table_ref, res_ref, out_ref):
    tokens, width = res_ref.shape
    chunks = table_ref.shape[0]
    cut = width // (chunks + 1)
    tail = res_ref[:, chunks * cut :]
    for j in range(chunks):
        span = slice(j * cut, (j + 1) * cut)
        sums = dot(table_ref[j], back_ref[:, span])
        main = sums[0:tokens] + sums[tokens : 2 * tokens]
        out_ref[:, span] = (res_ref[:, span] + main).astype(BF16)
        tail = tail + (sums[2 * tokens : 3 * tokens] + sums[3 * tokens :])
    out_ref[:, chunks * cut :] = tail.astype(BF16)


def per_device(
    hidden,
    gain_attn,
    w_qkv,
    w_out,
    cache_keys,
    cache_values,
    cache_lengths,
    parents,
    gain_moe,
    w_router,
    routes,
    w_gate_up,
    w_down,
):
    z_count = lax.axis_size("z")
    exp_count = z_count * CORES
    z_index = lax.axis_index("z")
    core = lax.axis_index("core")
    exp_index = z_index * CORES + core
    tokens, width = hidden.shape
    requests, tree = parents.shape
    page = cache_keys.shape[1]
    local_width = w_qkv.shape[2]
    scale = HEAD_DIM ** (-0.5)
    own = tokens // exp_count
    experts = w_router.shape[1]
    packed = width * CAP // SLOTS
    chunks = packed // (width - packed)
    padded = tokens + 8

    w_three = pltpu.with_memory_space_constraint(jnp.transpose(w_qkv, (1, 0, 2)), HBM)
    cache_keys = pltpu.with_memory_space_constraint(cache_keys, HBM)
    cache_values = pltpu.with_memory_space_constraint(cache_values, HBM)

    query = call(
        query_kernel,
        sds((tokens, local_width), BF16),
        [HBM, VMEM, HBM],
        [
            pltpu.VMEM((tokens, width), BF16),
            pltpu.VMEM((width, local_width), BF16),
            pltpu.SemaphoreType.DMA((2,)),
        ],
        flops=2 * tokens * width * local_width,
        bytes_accessed=2 * width * (tokens + local_width),
    )(pltpu.with_memory_space_constraint(hidden, HBM), gain_attn, w_three)

    def over_z(value, step):
        return lax.ppermute(value, "z", [(i, (i + step) % z_count) for i in range(z_count)])

    def over_core(value):
        return lax.ppermute(value, "core", [(0, 1), (1, 0)])

    steps = range(1, z_count)
    pieces = [query] + [over_z(query, step) for step in steps]
    other_pieces = [over_core(piece) for piece in pieces]
    homes = jnp.bitwise_and(z_index - jnp.arange(z_count), z_count - 1) * CORES
    homes = jnp.stack([homes + core, homes + 1 - core])
    meta = jnp.concatenate(
        [
            cache_lengths - exp_index * page,
            jnp.zeros((8 - requests,), jnp.int32),
            (homes * local_width).reshape(-1),
            (homes * own).reshape(-1),
        ]
    ).astype(jnp.int32)

    up = (parents + tree * jnp.arange(requests, dtype=jnp.int32)[:, None]).reshape(tokens, 1)
    tree_o, tree_lse, keys, values = call(
        functools.partial(tree_kernel, scale),
        (
            sds((tokens, local_width), F32),
            sds((8, 256), F32),
            sds(cache_keys.shape, BF16),
            sds(cache_values.shape, BF16),
        ),
        [VMEM, VMEM, HBM, VMEM, VMEM, HBM, HBM],
        [
            pltpu.VMEM((256, 128), F32),
            pltpu.VMEM((2, width, local_width), BF16),
            pltpu.SemaphoreType.DMA((4,)),
        ],
        flops=4 * tokens * width * local_width,
        bytes_accessed=4 * requests * page * width,
        vmem=16 << 20,
    )(hidden, gain_attn, w_three, query, up, cache_keys, cache_values)

    scratch = [
        pltpu.VMEM((z_count * 2 * tree, page), F32),
        pltpu.VMEM((z_count * 2 * tree, page), BF16),
    ]
    heads = 2 * z_count
    for_other = call(
        functools.partial(page_kernel, scale, tree, False),
        sds((heads + 1, tokens, HEAD_DIM), BF16),
        [SMEM] + [VMEM] * 6,
        scratch,
        flops=2 * tokens * page * width,
        bytes_accessed=2 * requests * page * width,
        vmem=20 << 20,
    )(meta, *other_pieces, keys, values)
    from_other = over_core(for_other)
    kept, kept_lse = call(
        functools.partial(page_kernel, scale, tree, True),
        (sds((heads, tokens, HEAD_DIM), F32), sds((tokens, 128), F32)),
        [SMEM] + [VMEM] * 6 + [pl.ANY],
        scratch,
        flops=2 * tokens * page * width,
        bytes_accessed=2 * requests * page * width,
        vmem=20 << 20,
    )(meta, *pieces, keys, values, for_other)
    merged = call(
        merge_kernel,
        tuple(sds((padded, local_width), BF16) for _ in range(z_count)),
        [VMEM] * 3,
        [pltpu.VMEM((256, 128), F32)],
        bytes_accessed=1 << 20,
    )(from_other, kept, kept_lse)
    arrived = [merged[0]] + [over_z(merged[step], -step) for step in steps]
    block = experts * SLOTS // 2
    place, pack, gate_up, down = call(
        place_kernel,
        (
            sds((chunks, experts * SLOTS, 2 * own), BF16),
            sds((2 * chunks, block, block), BF16),
            sds(w_gate_up.shape[1:], BF16),
            sds(w_down.shape[1:], BF16),
        ),
        [VMEM, pl.ANY, HBM, HBM],
        [pltpu.SemaphoreType.DMA((2,))],
        flops=1 << 24,
        bytes_accessed=1 << 23,
        vmem=16 << 20,
    )(
        routes.T,
        merged[0],
        pltpu.with_memory_space_constraint(w_gate_up[0], HBM),
        pltpu.with_memory_space_constraint(w_down[0], HBM),
    )
    theirs, ours = call(
        out_kernel,
        (sds((z_count * own, width), BF16), sds((z_count * own, width), F32)),
        [SMEM] + [VMEM] * 7,
        [pltpu.VMEM((128, 256), F32), pltpu.VMEM((tokens, local_width), F32)],
        flops=2 * tokens * width * local_width,
        bytes_accessed=2 * width * (tokens + local_width),
    )(meta, *arrived, tree_o, tree_lse, w_out)
    folded = call(
        fold_kernel,
        tuple(sds((own, width), BF16 if step else F32) for step in range(z_count)),
        [VMEM] * 2,
        bytes_accessed=1 << 20,
    )(ours, over_core(theirs))
    mixed = [folded[0]] + [over_z(folded[step], -step) for step in steps]

    residual, normed, outgoing = call(
        residual_kernel,
        (
            sds((own, width), F32),
            sds((own, width), BF16),
            sds((experts * SLOTS, packed), BF16),
        ),
        [SMEM] + [VMEM] * 7,
        flops=1 << 27,
        bytes_accessed=1 << 22,
    )(meta, *mixed, hidden, gain_moe, place)
    rows = lax.all_to_all(
        outgoing.reshape(experts, SLOTS, packed),
        ("req", "z"),
        split_axis=0,
        concat_axis=0,
        tiled=True,
    ).reshape(experts * SLOTS, packed)

    def expert(values, half, extra, extra_spaces, out_rows):
        return call(
            functools.partial(expert_kernel, half * block),
            sds((out_rows, packed), BF16),
            [VMEM] * 4 + extra_spaces,
            flops=6 * block * width * w_down.shape[1],
            bytes_accessed=6 * width * w_down.shape[1],
            vmem=20 << 20,
        )(values, gate_up, down, pack, *extra)

    theirs = over_core(rows)
    mine_0 = expert(rows, 0, [], [], block)
    table = call(
        gate_kernel,
        sds((chunks, 4 * own, experts * SLOTS), BF16),
        [VMEM] * 3 + [pl.ANY],
        flops=1 << 24,
        bytes_accessed=1 << 19,
    )(normed, w_router.T, routes.T, mine_0)
    theirs_0 = expert(theirs, 0, [table], [pl.ANY], block)
    theirs_1 = expert(theirs, 1, [theirs_0], [pl.ANY], block)
    summed = expert(
        rows, 1, [mine_0, over_core(theirs_0), theirs_1], [VMEM, VMEM, pl.ANY], 2 * block
    )
    summed = call(
        add_kernel,
        sds((2 * block, packed), BF16),
        [VMEM] * 2,
        bytes_accessed=1 << 21,
        aliases={0: 0},
    )(summed, over_core(theirs_1))
    back = lax.all_to_all(
        summed.reshape(experts, SLOTS, packed),
        ("req", "z"),
        split_axis=0,
        concat_axis=0,
        tiled=True,
    ).reshape(experts * SLOTS, packed)
    return call(
        final_kernel,
        sds((own, width), BF16),
        [VMEM] * 3,
        flops=1 << 27,
        bytes_accessed=1 << 22,
    )(back, table, residual)


def solution(mesh):
    req_count, exp_count = mesh.devices.shape
    split = Mesh(
        mesh.devices.reshape(req_count, exp_count // CORES, CORES), ("req", "z", "core")
    )
    exp = ("z", "core")
    everywhere = ("req", "z", "core")
    in_specs = (
        P("req", None),
        P(),
        P(None, None, exp),
        P(exp, None),
        P("req", exp, None),
        P("req", exp, None),
        P("req"),
        P("req", None),
        P(),
        P(),
        P(everywhere, None),
        P(everywhere, None, None),
        P(everywhere, None, None),
    )
    return jax.shard_map(
        per_device,
        mesh=split,
        in_specs=in_specs,
        out_specs=P(everywhere, None),
        check_vma=False,
    )
```

```python
import functools

import jax
import jax.numpy as jnp
from jax import lax
from jax.experimental import pallas as pl
from jax.experimental.pallas import tpu as pltpu
from jax.sharding import Mesh
from jax.sharding import PartitionSpec as P

HEAD_DIM = 128
EXP_SPLIT = 2
CORES = 2
CAP = 6
SLOTS = 8

EPSILON = 1e-05
NEGATIVE = -1e30
F32 = jnp.float32
BF16 = jnp.bfloat16
VMEM = pltpu.VMEM
SMEM = pltpu.SMEM
HBM = pltpu.HBM


def dot(a, b):
    return jnp.dot(a, b, preferred_element_type=F32)


def dot_t(a, b):
    return lax.dot_general(a, b, (((1,), (1,)), ((), ())), preferred_element_type=F32)


def iota(shape, axis):
    return lax.broadcasted_iota(jnp.int32, shape, axis)


def call(body, out, in_spaces, scratch=(), flops=0, bytes_accessed=0, vmem=10 << 20, aliases={}):
    out_spec = jax.tree.map(lambda _: pl.BlockSpec(memory_space=VMEM), out)
    return pl.pallas_call(
        body,
        out_shape=out,
        in_specs=[pl.BlockSpec(memory_space=s) for s in in_spaces],
        out_specs=out_spec,
        scratch_shapes=list(scratch),
        input_output_aliases=aliases,
        compiler_params=pltpu.CompilerParams(vmem_limit_bytes=vmem),
        cost_estimate=pl.CostEstimate(
            flops=flops, bytes_accessed=bytes_accessed, transcendentals=0
        ),
    )


def sds(shape, dtype):
    return jax.ShapeDtypeStruct(shape, dtype)


def normed_rows(values, gain):
    inverse = lax.rsqrt(jnp.mean(values * values, axis=-1, keepdims=True) + EPSILON)
    return (values * inverse * gain).astype(BF16)


def query_kernel(x_hbm, g_hbm, w_hbm, q_ref, x_ref, g_ref, w_ref, sems):
    x_copy = pltpu.make_async_copy(x_hbm, x_ref, sems.at[0])
    w_copy = pltpu.make_async_copy(w_hbm.at[0], w_ref, sems.at[1])
    g_copy = pltpu.make_async_copy(g_hbm, g_ref, sems.at[2])
    x_copy.start()
    g_copy.start()
    w_copy.start()
    g_copy.wait()
    x_copy.wait()
    normed = normed_rows(x_ref[...].astype(F32), g_ref[...].astype(F32).reshape(1, -1))
    w_copy.wait()
    q_ref[...] = dot(normed, w_ref[...]).astype(BF16)


def load_kernel(k_hbm, v_hbm, after_ref, k_ref, v_ref, sems):
    del after_ref
    k_copy = pltpu.make_async_copy(k_hbm, k_ref, sems.at[0])
    v_copy = pltpu.make_async_copy(v_hbm, v_ref, sems.at[1])
    k_copy.start()
    v_copy.start()
    k_copy.wait()
    v_copy.wait()


def tree_kernel(scale, x_ref, g_ref, w_hbm, q_ref, up_ref, *refs):
    o_ref, lse_ref, turn, w_ref, sems = refs
    tokens, width = q_ref.shape
    w_copies = [
        pltpu.make_async_copy(w_hbm.at[i + 1], w_ref.at[i], sems.at[i]) for i in range(2)
    ]
    for w_copy in w_copies:
        w_copy.start()
    normed = normed_rows(x_ref[...].astype(F32), g_ref[...].astype(F32).reshape(1, -1))
    w_copies[0].wait()
    keys = dot(normed, w_ref[0]).astype(BF16)
    w_copies[1].wait()
    values = dot(normed, w_ref[1]).astype(BF16)
    requests, tree = up_ref.shape
    spread = iota((tree, tokens), 0) == iota((tree, tokens), 1) % tree
    wide = dot(up_ref[...].astype(BF16), jnp.where(spread, 1.0, 0.0).astype(BF16))
    home = iota((requests, tokens), 1) // tree
    wide = jnp.where(iota((requests, tokens), 0) == home, wide + (home * tree).astype(F32), 0.0)
    parent = jnp.sum(wide, axis=0, keepdims=True)
    row = iota((tokens, tokens), 0)
    same = row == iota((tokens, tokens), 1)
    reach = jnp.where(same | (row.astype(F32) == parent), 1.0, 0.0)
    for _ in range(6):
        half = reach.astype(BF16)
        reach = jnp.minimum(dot(half, half), 1.0)
    visible = dot_t(jnp.where(same, 1.0, 0.0).astype(BF16), reach.astype(BF16)) > 0.5
    lane = iota((tokens, 128), 1)
    stats = jnp.zeros((tokens, 128), F32)
    for h in range(width // HEAD_DIM):
        cut = slice(h * HEAD_DIM, (h + 1) * HEAD_DIM)
        scores = dot_t(q_ref[:, cut], keys[:, cut]) * scale
        scores = jnp.where(visible, scores, NEGATIVE)
        high = jnp.max(scores, axis=-1, keepdims=True)
        weights = jnp.where(visible, jnp.exp(scores - high), 0.0)
        total = jnp.sum(weights, axis=-1, keepdims=True)
        o_ref[:, cut] = dot(weights.astype(BF16), values[:, cut]) / total
        stats = jnp.where(lane == h, high + jnp.log(total), stats)
    turn[0:tokens, :] = stats
    lse_ref[...] = jnp.transpose(turn[...])[0:8, :]


def page_kernel(scale, tree, kept, meta_ref, *refs):
    pieces, (k_ref, v_ref) = refs[:4], refs[4:6]
    outs = refs[7:-2] if kept else refs[6:-2]
    s_all, p_all = refs[-2:]
    out_ref = outs[0]
    requests, page = k_ref.shape[0], k_ref.shape[1]
    width = pieces[0].shape[1]
    pair = 2 * tree
    lane = iota((tree, 128), 1)
    wide = iota((tree, width), 1) < HEAD_DIM
    first_at = 8 if kept else 12

    def columns(i):
        return pl.ds(pl.multiple_of(meta_ref[first_at + i], width), width)

    for r in range(requests):
        rows = slice(r * tree, (r + 1) * tree)
        live = meta_ref[r]

        @pl.when(live > 0)
        def _():
            for i, piece in enumerate(pieces):
                query = piece[rows, :]
                zero = jnp.zeros_like(query)
                both = jnp.concatenate(
                    [jnp.where(wide, query, zero), jnp.where(wide, zero, query)], axis=0
                )
                s_all[i * pair : (i + 1) * pair, :] = dot_t(both, k_ref[r, :, columns(i)])
            scores = s_all[...] * scale
            scores = jnp.where(iota(scores.shape, 1) < live, scores, NEGATIVE)
            high = jnp.max(scores, axis=-1, keepdims=True)
            weights = jnp.exp(scores - high)
            total = jnp.sum(weights, axis=-1, keepdims=True)
            p_all[...] = weights.astype(BF16)
            inverse = 1.0 / total
            lse = high + jnp.log(total)
            first = lse.astype(BF16).astype(F32)
            second = (lse - first).astype(BF16).astype(F32)
            third = lse - first - second
            stats = jnp.zeros((tree, 128), F32)
            for i in range(len(pieces)):
                summed = dot(p_all[i * pair : (i + 1) * pair, :], v_ref[r, :, columns(i)])
                for h in range(2):
                    own = slice(i * pair + h * tree, i * pair + (h + 1) * tree)
                    cut = slice(h * HEAD_DIM, (h + 1) * HEAD_DIM)
                    value = summed[h * tree : (h + 1) * tree, cut] * inverse[own]
                    out_ref[2 * i + h, rows, :] = value.astype(out_ref.dtype)
                    if kept:
                        stats = jnp.where(lane == i * 8 + h, lse[own], stats)
                    else:
                        for j, part in enumerate((first, second, third)):
                            stats = jnp.where(lane == i * 8 + 2 * j + h, part[own], stats)
            if kept:
                outs[1][rows, :] = stats
            else:
                out_ref[8, rows, :] = stats.astype(BF16)

        @pl.when(live <= 0)
        def _():
            for i in range(8):
                out_ref[i, rows, :] = jnp.zeros((tree, HEAD_DIM), out_ref.dtype)
            empty = jnp.where(lane % 8 < 2, NEGATIVE, 0.0)
            if kept:
                outs[1][rows, :] = empty
            else:
                out_ref[8, rows, :] = empty.astype(BF16)


def merge_kernel(other_ref, kept_ref, lse_ref, *refs):
    outs, turn = refs[:-1], refs[-1]
    tokens = lse_ref.shape[0]
    sent = other_ref[8].astype(F32)
    other = sent + pltpu.roll(sent, 126, 1) + pltpu.roll(sent, 124, 1)
    kept = lse_ref[...]
    high = jnp.maximum(other, kept)
    other, kept = jnp.exp(other - high), jnp.exp(kept - high)
    whole = other + kept
    inverse = 1.0 / whole
    other, kept = other * inverse, kept * inverse
    lse = jnp.where(iota(high.shape, 1) % 8 < 2, high + jnp.log(whole), 0.0)
    first = lse.astype(BF16).astype(F32)
    second = (lse - first).astype(BF16).astype(F32)
    third = lse - first - second
    turn[0:tokens, :] = first + pltpu.roll(second, 2, 1) + pltpu.roll(third, 4, 1)
    turn[tokens:, :] = jnp.zeros((turn.shape[0] - tokens, 128), F32)
    turned = jnp.transpose(turn[...])
    for i, out_ref in enumerate(outs):
        for h in range(2):
            at = i * 8 + h
            value = other[:, at : at + 1] * other_ref[2 * i + h].astype(F32)
            value = value + kept[:, at : at + 1] * kept_ref[2 * i + h]
            out_ref[0:tokens, h * HEAD_DIM : (h + 1) * HEAD_DIM] = value.astype(BF16)
        out_ref[tokens:, :] = turned[i * 8 : (i + 1) * 8, :].astype(BF16)


def out_kernel(meta_ref, *refs):
    parts = refs[:4]
    tree_o_ref, tree_lse_ref, w_ref, theirs_ref, ours_ref, turn, mixed = refs[4:]
    padded, width = parts[0].shape
    tokens = padded - 8
    heads = width // HEAD_DIM
    own = ours_ref.shape[0] // 4
    lses = []
    for part in parts:
        rows = part[tokens:, :].astype(F32)
        lses.append(rows[0:2] + rows[2:4] + rows[4:6])
    lses.append(tree_lse_ref[0:2, :])
    high = functools.reduce(jnp.maximum, lses)
    factors = [jnp.exp(value - high) for value in lses]
    whole = functools.reduce(lambda a, b: a + b, factors)
    for s, factor in enumerate(factors):
        turn[2 * s : 2 * s + 2, :] = factor / whole
    turned = jnp.transpose(turn[...])[0:tokens, :]
    for h in range(heads):
        cut = slice(h * HEAD_DIM, (h + 1) * HEAD_DIM)
        at = 2 * len(parts) + h
        total = turned[:, at : at + 1] * tree_o_ref[:, cut]
        for s, part in enumerate(parts):
            at = 2 * s + h
            total = total + turned[:, at : at + 1] * part[0:tokens, cut].astype(F32)
        mixed[:, cut] = total

    def rows_of(first_at):
        rows = [
            mixed[pl.ds(pl.multiple_of(meta_ref[first_at + i], 8), own), :] for i in range(4)
        ]
        return jnp.concatenate(rows, axis=0).astype(BF16)

    theirs_ref[...] = dot(rows_of(20), w_ref[...]).astype(BF16)
    ours_ref[...] = dot(rows_of(16), w_ref[...])


def fold_kernel(ours_ref, theirs_ref, *outs):
    own = outs[0].shape[0]
    for i, out_ref in enumerate(outs):
        rows = slice(i * own, (i + 1) * own)
        out_ref[...] = (ours_ref[rows, :] + theirs_ref[rows, :].astype(F32)).astype(out_ref.dtype)


def expert_of_row(rows, experts):
    return jnp.where(iota((rows, experts), 0) // SLOTS == iota((rows, experts), 1), 1.0, 0.0)


def window_kernel(scale, tree_inputs, routes_ref, up_hbm, down_hbm, after_ref, *refs):
    tree_refs, place_refs, (up_ref, down_ref), scratch = refs[:2], refs[2:5], refs[5:7], refs[7:]
    del after_ref
    up_copy = pltpu.make_async_copy(up_hbm, up_ref, scratch[3].at[0])
    down_copy = pltpu.make_async_copy(down_hbm, down_ref, scratch[3].at[1])
    up_copy.start()
    down_copy.start()
    tree_kernel(scale, *tree_inputs, *tree_refs, *scratch[:3])
    place_kernel(routes_ref, *place_refs)
    up_copy.wait()
    down_copy.wait()


def place_kernel(routes_ref, place_ref, gather_ref, scatter_ref):
    chunks = place_ref.shape[0]
    _, real, block = gather_ref.shape
    row, column = iota((real, block), 0), iota((real, block), 1)
    base, slot = row // CAP * SLOTS, row % CAP
    gather_ref[0] = jnp.where(column == base + slot, 1.0, 0.0).astype(BF16)
    for k in range(chunks):
        hit = (column == base + CAP + slot // chunks) & (slot % chunks == k)
        gather_ref[1 + k] = jnp.where(hit, 1.0, 0.0).astype(BF16)
    row, column = iota((block, 2 * real), 0), iota((block, 2 * real), 1)
    is_tail = column >= real
    column = column - jnp.where(is_tail, real, 0)
    base, slot = column // CAP * SLOTS, column % CAP
    for k in range(chunks):
        main = (row == base + slot) & jnp.logical_not(is_tail)
        tail = (row == base + CAP + slot // chunks) & (slot % chunks == k) & is_tail
        scatter_ref[k] = jnp.where(main | tail, 1.0, 0.0).astype(BF16)
    top, tokens = routes_ref.shape
    chunks, rows, _ = place_ref.shape
    experts = rows // SLOTS
    named = iota((experts, tokens), 0)
    chosen = jnp.zeros((experts, tokens), F32)
    for k in range(top):
        chosen = jnp.where(routes_ref[k : k + 1, :] == named, 1.0, chosen)
    source = iota((tokens, 2 * tokens), 0)
    target = iota((tokens, 2 * tokens), 1) % tokens
    chosen = chosen.astype(BF16)
    rank = dot(chosen, jnp.where(source < target, 1.0, 0.0).astype(BF16))
    both = dot(chosen, jnp.where(source == target, 1.0, 0.0).astype(BF16))
    rank = jnp.where(both > 0.5, rank, -1.0).astype(BF16)
    spread = dot(expert_of_row(rows, experts).astype(BF16), rank)
    slot = iota((rows, 2 * tokens), 0) % SLOTS
    is_tail = iota((rows, 2 * tokens), 1) >= tokens
    for j in range(chunks):
        wanted = jnp.where(is_tail, (slot - CAP) * chunks + j, slot)
        valid = is_tail == (slot >= CAP)
        hit = valid & (spread == wanted.astype(F32))
        place_ref[j] = jnp.where(hit, 1.0, 0.0).astype(BF16)


def residual_kernel(meta_ref, *refs):
    parts = refs[:4]
    x_ref, g_ref, place_ref, res_ref, normed_ref, out_ref = refs[4:]
    tokens, width = parts[0].shape
    chunks = place_ref.shape[0]
    cut = width // (chunks + 1)
    start = pl.multiple_of(meta_ref[16], 8)
    residual = x_ref[pl.ds(start, tokens), :].astype(F32)
    for part in parts:
        residual = residual + part[...].astype(F32)
    res_ref[...] = residual
    inverse = lax.rsqrt(jnp.mean(residual * residual, axis=-1, keepdims=True) + EPSILON)
    normed = residual * inverse * g_ref[...].astype(F32).reshape(1, -1)
    normed_ref[...] = normed.astype(BF16)
    tail = normed[:, chunks * cut :]
    for j in range(chunks):
        pair = jnp.concatenate([normed[:, j * cut : (j + 1) * cut], tail], axis=0).astype(BF16)
        out_ref[:, j * cut : (j + 1) * cut] = dot(place_ref[j], pair).astype(BF16)


def gate_kernel(normed_ref, router_ref, routes_ref, table_ref):
    top, tokens = routes_ref.shape
    experts = router_ref.shape[0]
    chunks, _, rows = table_ref.shape
    logits = dot_t(normed_ref[...], router_ref[...])
    exponent = jnp.exp(logits)
    chances = exponent / jnp.sum(exponent, axis=-1, keepdims=True)
    named = iota((experts, tokens), 0)
    chosen = jnp.zeros((experts, tokens), F32)
    for k in range(top):
        chosen = jnp.where(routes_ref[k : k + 1, :] == named, 1.0, chosen)
    same = jnp.where(iota((tokens, tokens), 0) == iota((tokens, tokens), 1), 1.0, 0.0)
    chosen = dot_t(same.astype(BF16), chosen.astype(BF16))
    picked = chances * chosen
    gates = picked / jnp.sum(picked, axis=-1, keepdims=True)
    earlier = jnp.where(iota((tokens, tokens), 0) > iota((tokens, tokens), 1), 1.0, 0.0)
    rank = dot(earlier.astype(BF16), chosen.astype(BF16))
    rank = jnp.where(chosen > 0.5, rank, -1.0).astype(BF16)
    first = gates.astype(BF16)
    second = (gates - first.astype(F32)).astype(BF16)
    home = iota((experts, rows), 0) == iota((experts, rows), 1) // SLOTS
    home = jnp.where(home, 1.0, 0.0).astype(BF16)
    rank, first, second = dot(rank, home), dot(first, home), dot(second, home)
    slot = iota((tokens, rows), 1) % SLOTS
    main = (slot < CAP) & (rank == slot.astype(F32))
    for j in range(chunks):
        tail = (slot >= CAP) & (rank == ((slot - CAP) * chunks + j).astype(F32))
        table_ref[j] = jnp.concatenate(
            [
                jnp.where(main, first, 0.0),
                jnp.where(main, second, 0.0),
                jnp.where(tail, first, 0.0),
                jnp.where(tail, second, 0.0),
            ],
            axis=0,
        ).astype(BF16)


def expert_kernel(
    x_ref,
    up_ref,
    down_ref,
    other_up_ref,
    other_down_ref,
    gather_ref,
    scatter_ref,
    normed_ref,
    router_ref,
    routes_ref,
    out_ref,
    table_ref,
):
    gate_kernel(normed_ref, router_ref, routes_ref, table_ref)
    rows, packed = x_ref.shape
    width, both = up_ref.shape
    units = both // 2
    cut = width - packed
    chunks = packed // cut
    _, real, block = gather_ref.shape
    mains, tails = [], []
    for at in range(0, rows, block):
        span = slice(at, at + block)
        mains.append(dot(gather_ref[0], x_ref[span, :]).astype(BF16))
        tail = dot(gather_ref[1], x_ref[span, 0:cut])
        for k in range(1, chunks):
            tail = tail + dot(gather_ref[1 + k], x_ref[span, k * cut : (k + 1) * cut])
        tails.append(tail.astype(BF16))
    main, tail = jnp.concatenate(mains, axis=0), jnp.concatenate(tails, axis=0)
    hidden = []
    for weights in (up_ref, other_up_ref):
        parts = []
        for at in range(0, units, units // 2):
            gate_cut = slice(at, at + units // 2)
            up_cut = slice(units + at, units + at + units // 2)
            gate = dot(main, weights[0:packed, gate_cut]) + dot(tail, weights[packed:, gate_cut])
            up = dot(main, weights[0:packed, up_cut]) + dot(tail, weights[packed:, up_cut])
            parts.append((gate / (1.0 + jnp.exp(-gate)) * up).astype(BF16))
        hidden.append(jnp.concatenate(parts, axis=1))

    def result(columns):
        first = dot(hidden[0], down_ref[:, columns]).astype(BF16).astype(F32)
        second = dot(hidden[1], other_down_ref[:, columns]).astype(BF16).astype(F32)
        return (first + second).astype(BF16)

    last = result(slice(packed, width))
    for k in range(chunks):
        columns = slice(k * cut, (k + 1) * cut)
        value = result(columns)
        for i in range(rows // block):
            own = slice(i * real, (i + 1) * real)
            pair = jnp.concatenate([value[own], last[own]], axis=0)
            out_ref[i * block : (i + 1) * block, columns] = dot(scatter_ref[k], pair).astype(
                BF16
            )


def final_kernel(back_ref, table_ref, res_ref, out_ref):
    tokens, width = res_ref.shape
    chunks = table_ref.shape[0]
    cut = width // (chunks + 1)
    tail = res_ref[:, chunks * cut :]
    for j in range(chunks):
        span = slice(j * cut, (j + 1) * cut)
        sums = dot(table_ref[j], back_ref[:, span])
        main = sums[0:tokens] + sums[tokens : 2 * tokens]
        out_ref[:, span] = (res_ref[:, span] + main).astype(BF16)
        tail = tail + (sums[2 * tokens : 3 * tokens] + sums[3 * tokens :])
    out_ref[:, chunks * cut :] = tail.astype(BF16)


def per_device(
    hidden,
    gain_attn,
    w_qkv,
    w_out,
    cache_keys,
    cache_values,
    cache_lengths,
    parents,
    gain_moe,
    w_router,
    routes,
    w_gate_up,
    w_down,
):
    z_count = lax.axis_size("z")
    exp_count = z_count * CORES
    z_index = lax.axis_index("z")
    core = lax.axis_index("core")
    exp_index = z_index * CORES + core
    tokens, width = hidden.shape
    requests, tree = parents.shape
    page = cache_keys.shape[1]
    local_width = w_qkv.shape[2]
    scale = HEAD_DIM ** (-0.5)
    own = tokens // exp_count
    experts = w_router.shape[1]
    packed = width * CAP // SLOTS
    chunks = packed // (width - packed)
    padded = tokens + 8

    w_three = pltpu.with_memory_space_constraint(jnp.transpose(w_qkv, (1, 0, 2)), HBM)
    cache_keys = pltpu.with_memory_space_constraint(cache_keys, HBM)
    cache_values = pltpu.with_memory_space_constraint(cache_values, HBM)

    query = call(
        query_kernel,
        sds((tokens, local_width), BF16),
        [HBM, HBM, HBM],
        [
            pltpu.VMEM((tokens, width), BF16),
            pltpu.VMEM((width,), BF16),
            pltpu.VMEM((width, local_width), BF16),
            pltpu.SemaphoreType.DMA((3,)),
        ],
        flops=2 * tokens * width * local_width,
        bytes_accessed=2 * width * (tokens + local_width),
    )(
        pltpu.with_memory_space_constraint(hidden, HBM),
        pltpu.with_memory_space_constraint(gain_attn, HBM),
        w_three,
    )

    def over_z(value, step):
        return lax.ppermute(value, "z", [(i, (i + step) % z_count) for i in range(z_count)])

    def over_core(value):
        return lax.ppermute(value, "core", [(0, 1), (1, 0)])

    steps = range(1, z_count)
    pieces = [query] + [over_z(query, step) for step in steps]
    other_pieces = [over_core(piece) for piece in pieces]
    homes = jnp.bitwise_and(z_index - jnp.arange(z_count), z_count - 1) * CORES
    homes = jnp.stack([homes + core, homes + 1 - core])
    meta = jnp.concatenate(
        [
            cache_lengths - exp_index * page,
            jnp.zeros((8 - requests,), jnp.int32),
            (homes * local_width).reshape(-1),
            (homes * own).reshape(-1),
        ]
    ).astype(jnp.int32)

    keys, values = call(
        load_kernel,
        (sds(cache_keys.shape, BF16), sds(cache_values.shape, BF16)),
        [HBM, HBM, pl.ANY],
        [pltpu.SemaphoreType.DMA((2,))],
        bytes_accessed=4 * requests * page * width,
        vmem=16 << 20,
    )(cache_keys, cache_values, query)

    scratch = [
        pltpu.VMEM((z_count * 2 * tree, page), F32),
        pltpu.VMEM((z_count * 2 * tree, page), BF16),
    ]
    heads = 2 * z_count
    for_other = call(
        functools.partial(page_kernel, scale, tree, False),
        sds((heads + 1, tokens, HEAD_DIM), BF16),
        [SMEM] + [VMEM] * 6,
        scratch,
        flops=2 * tokens * page * width,
        bytes_accessed=2 * requests * page * width,
        vmem=20 << 20,
    )(meta, *other_pieces, keys, values)
    from_other = over_core(for_other)
    kept, kept_lse = call(
        functools.partial(page_kernel, scale, tree, True),
        (sds((heads, tokens, HEAD_DIM), F32), sds((tokens, 128), F32)),
        [SMEM] + [VMEM] * 6 + [pl.ANY],
        scratch,
        flops=2 * tokens * page * width,
        bytes_accessed=2 * requests * page * width,
        vmem=20 << 20,
    )(meta, *pieces, keys, values, for_other)
    merged = call(
        merge_kernel,
        tuple(sds((padded, local_width), BF16) for _ in range(z_count)),
        [VMEM] * 3,
        [pltpu.VMEM((256, 128), F32)],
        bytes_accessed=1 << 20,
    )(from_other, kept, kept_lse)
    arrived = [merged[0]] + [over_z(merged[step], -step) for step in steps]

    block = experts * SLOTS // 2
    real = block // SLOTS * CAP

    def body(x_ref, g_ref, w_hbm, q_ref, up_ref, *refs):
        window_kernel(scale, (x_ref, g_ref, w_hbm, q_ref, up_ref), *refs)

    tree_o, tree_lse, place, gather, scatter, gate_up, down = call(
        body,
        (
            sds((tokens, local_width), F32),
            sds((8, 256), F32),
            sds((chunks, experts * SLOTS, 2 * own), BF16),
            sds((1 + chunks, real, block), BF16),
            sds((chunks, block, 2 * real), BF16),
            sds(w_gate_up.shape[1:], BF16),
            sds(w_down.shape[1:], BF16),
        ),
        [VMEM, VMEM, HBM, VMEM, VMEM, VMEM, HBM, HBM, pl.ANY],
        [
            pltpu.VMEM((256, 128), F32),
            pltpu.VMEM((2, width, local_width), BF16),
            pltpu.SemaphoreType.DMA((2,)),
            pltpu.SemaphoreType.DMA((2,)),
        ],
        flops=4 * tokens * width * local_width,
        bytes_accessed=2 * width * (tokens + 2 * local_width) + (1 << 23),
        vmem=24 << 20,
    )(
        hidden,
        gain_attn,
        w_three,
        query,
        parents,
        routes.T,
        pltpu.with_memory_space_constraint(w_gate_up[0], HBM),
        pltpu.with_memory_space_constraint(w_down[0], HBM),
        merged[0],
    )

    theirs, ours = call(
        out_kernel,
        (sds((z_count * own, width), BF16), sds((z_count * own, width), F32)),
        [SMEM] + [VMEM] * 7,
        [pltpu.VMEM((128, 256), F32), pltpu.VMEM((tokens, local_width), F32)],
        flops=2 * tokens * width * local_width,
        bytes_accessed=2 * width * (tokens + local_width),
    )(meta, *arrived, tree_o, tree_lse, w_out)
    folded = call(
        fold_kernel,
        tuple(sds((own, width), BF16 if step else F32) for step in range(z_count)),
        [VMEM] * 2,
        bytes_accessed=1 << 20,
    )(ours, over_core(theirs))
    first_fold, far_up, far_down = lax.optimization_barrier(
        (folded[0], w_gate_up[0], w_down[0])
    )
    other_gate_up, other_down = over_core(far_up), over_core(far_down)
    mixed = [first_fold] + [over_z(folded[step], -step) for step in steps]

    residual, normed, outgoing = call(
        residual_kernel,
        (
            sds((own, width), F32),
            sds((own, width), BF16),
            sds((experts * SLOTS, packed), BF16),
        ),
        [SMEM] + [VMEM] * 7,
        flops=1 << 27,
        bytes_accessed=1 << 22,
    )(meta, *mixed, hidden, gain_moe, place)
    rows = lax.all_to_all(
        outgoing.reshape(experts, SLOTS, packed),
        ("req", "z"),
        split_axis=0,
        concat_axis=0,
        tiled=True,
    ).reshape(experts * SLOTS, packed)

    summed, table = call(
        expert_kernel,
        (
            sds((experts * SLOTS, packed), BF16),
            sds((chunks, 4 * own, experts * SLOTS), BF16),
        ),
        [VMEM] * 10,
        flops=12 * experts * CAP * width * w_down.shape[1],
        bytes_accessed=12 * width * w_down.shape[1],
        vmem=24 << 20,
    )(
        rows,
        gate_up,
        down,
        other_gate_up,
        other_down,
        gather,
        scatter,
        normed,
        w_router.T,
        routes.T,
    )
    back = lax.all_to_all(
        summed.reshape(experts, SLOTS, packed),
        ("req", "z"),
        split_axis=0,
        concat_axis=0,
        tiled=True,
    ).reshape(experts * SLOTS, packed)
    return call(
        final_kernel,
        sds((own, width), BF16),
        [VMEM] * 3,
        flops=1 << 27,
        bytes_accessed=1 << 22,
    )(back, table, residual)


def solution(mesh):
    req_count, exp_count = mesh.devices.shape
    split = Mesh(
        mesh.devices.reshape(req_count, exp_count // CORES, CORES), ("req", "z", "core")
    )
    exp = ("z", "core")
    everywhere = ("req", "z", "core")
    in_specs = (
        P("req", None),
        P(),
        P(None, None, exp),
        P(exp, None),
        P("req", exp, None),
        P("req", exp, None),
        P("req"),
        P("req", None),
        P(),
        P(),
        P(everywhere, None),
        P(everywhere, None, None),
        P(everywhere, None, None),
    )
    return jax.shard_map(
        per_device,
        mesh=split,
        in_specs=in_specs,
        out_specs=P(everywhere, None),
        check_vma=False,
    )
```

```python
import functools

import jax
import jax.numpy as jnp
from jax import lax
from jax.experimental import pallas as pl
from jax.experimental.pallas import tpu as pltpu
from jax.sharding import Mesh
from jax.sharding import PartitionSpec as P

HEAD_DIM = 128
EXP_SPLIT = 2
CORES = 2
CAP = 6
SLOTS = 8

EPSILON = 1e-05
NEGATIVE = -1e30
F32 = jnp.float32
BF16 = jnp.bfloat16
VMEM = pltpu.VMEM
SMEM = pltpu.SMEM
HBM = pltpu.HBM


def dot(a, b):
    return jnp.dot(a, b, preferred_element_type=F32)


def dot_t(a, b):
    return lax.dot_general(a, b, (((1,), (1,)), ((), ())), preferred_element_type=F32)


def iota(shape, axis):
    return lax.broadcasted_iota(jnp.int32, shape, axis)


def call(body, out, in_spaces, scratch=(), flops=0, bytes_accessed=0, vmem=10 << 20, aliases={}):
    out_spec = jax.tree.map(lambda _: pl.BlockSpec(memory_space=VMEM), out)
    return pl.pallas_call(
        body,
        out_shape=out,
        in_specs=[pl.BlockSpec(memory_space=s) for s in in_spaces],
        out_specs=out_spec,
        scratch_shapes=list(scratch),
        input_output_aliases=aliases,
        compiler_params=pltpu.CompilerParams(vmem_limit_bytes=vmem),
        cost_estimate=pl.CostEstimate(
            flops=flops, bytes_accessed=bytes_accessed, transcendentals=0
        ),
    )


def sds(shape, dtype):
    return jax.ShapeDtypeStruct(shape, dtype)


def normed_rows(values, gain):
    inverse = lax.rsqrt(jnp.mean(values * values, axis=-1, keepdims=True) + EPSILON)
    return (values * inverse * gain).astype(BF16)


def query_kernel(x_hbm, g_hbm, w_hbm, q_ref, x_ref, g_ref, w_ref, sems):
    x_copy = pltpu.make_async_copy(x_hbm, x_ref, sems.at[0])
    w_copy = pltpu.make_async_copy(w_hbm.at[0], w_ref, sems.at[1])
    g_copy = pltpu.make_async_copy(g_hbm, g_ref, sems.at[2])
    x_copy.start()
    g_copy.start()
    w_copy.start()
    g_copy.wait()
    x_copy.wait()
    normed = normed_rows(x_ref[...].astype(F32), g_ref[...].astype(F32).reshape(1, -1))
    w_copy.wait()
    q_ref[...] = dot(normed, w_ref[...]).astype(BF16)


def load_kernel(k_hbm, after_ref, k_ref, sem):
    del after_ref
    k_copy = pltpu.make_async_copy(k_hbm, k_ref, sem)
    k_copy.start()
    k_copy.wait()


def tree_kernel(scale, x_ref, g_ref, w_hbm, q_ref, up_ref, after_ref, *refs):
    o_ref, lse_ref, turn, w_ref, sems = refs
    del after_ref
    tokens, width = q_ref.shape
    w_copies = [
        pltpu.make_async_copy(w_hbm.at[i + 1], w_ref.at[i], sems.at[i]) for i in range(2)
    ]
    for w_copy in w_copies:
        w_copy.start()
    normed = normed_rows(x_ref[...].astype(F32), g_ref[...].astype(F32).reshape(1, -1))
    w_copies[0].wait()
    keys = dot(normed, w_ref[0]).astype(BF16)
    w_copies[1].wait()
    values = dot(normed, w_ref[1]).astype(BF16)
    requests, tree = up_ref.shape
    spread = iota((tree, tokens), 0) == iota((tree, tokens), 1) % tree
    wide = dot(up_ref[...].astype(BF16), jnp.where(spread, 1.0, 0.0).astype(BF16))
    home = iota((requests, tokens), 1) // tree
    wide = jnp.where(iota((requests, tokens), 0) == home, wide + (home * tree).astype(F32), 0.0)
    parent = jnp.sum(wide, axis=0, keepdims=True)
    row = iota((tokens, tokens), 0)
    same = row == iota((tokens, tokens), 1)
    reach = jnp.where(same | (row.astype(F32) == parent), 1.0, 0.0)
    for _ in range(6):
        half = reach.astype(BF16)
        reach = jnp.minimum(dot(half, half), 1.0)
    visible = dot_t(jnp.where(same, 1.0, 0.0).astype(BF16), reach.astype(BF16)) > 0.5
    lane = iota((tokens, 128), 1)
    stats = jnp.zeros((tokens, 128), F32)
    for h in range(width // HEAD_DIM):
        cut = slice(h * HEAD_DIM, (h + 1) * HEAD_DIM)
        scores = dot_t(q_ref[:, cut], keys[:, cut]) * scale
        scores = jnp.where(visible, scores, NEGATIVE)
        high = jnp.max(scores, axis=-1, keepdims=True)
        weights = jnp.where(visible, jnp.exp(scores - high), 0.0)
        total = jnp.sum(weights, axis=-1, keepdims=True)
        o_ref[:, cut] = dot(weights.astype(BF16), values[:, cut]) / total
        stats = jnp.where(lane == h, high + jnp.log(total), stats)
    turn[0:tokens, :] = stats
    lse_ref[...] = jnp.transpose(turn[...])[0:8, :]


def page_kernel(scale, tree, kept, meta_ref, *refs):
    pieces, (k_ref, v_ref) = refs[:4], refs[4:6]
    outs = refs[7:-2] if kept else refs[6:-3]
    s_all, p_all = refs[-2:] if kept else refs[-3:-1]
    out_ref = outs[0]
    if not kept:
        v_hbm, v_ref, sems = v_ref, outs[1], refs[-1]
        loads = [
            pltpu.make_async_copy(v_hbm.at[r], v_ref.at[r], sems.at[r])
            for r in range(v_hbm.shape[0])
        ]
        for load in loads:
            load.start()
    requests, page = k_ref.shape[0], k_ref.shape[1]
    width = pieces[0].shape[1]
    pair = 2 * tree
    lane = iota((tree, 128), 1)
    wide = iota((tree, width), 1) < HEAD_DIM
    first_at = 8 if kept else 12

    def columns(i):
        return pl.ds(pl.multiple_of(meta_ref[first_at + i], width), width)

    for r in range(requests):
        rows = slice(r * tree, (r + 1) * tree)
        live = meta_ref[r]
        if not kept:
            loads[r].wait()

        @pl.when(live > 0)
        def _():
            for i, piece in enumerate(pieces):
                query = piece[rows, :]
                zero = jnp.zeros_like(query)
                both = jnp.concatenate(
                    [jnp.where(wide, query, zero), jnp.where(wide, zero, query)], axis=0
                )
                s_all[i * pair : (i + 1) * pair, :] = dot_t(both, k_ref[r, :, columns(i)])
            scores = s_all[...] * scale
            scores = jnp.where(iota(scores.shape, 1) < live, scores, NEGATIVE)
            high = jnp.max(scores, axis=-1, keepdims=True)
            weights = jnp.exp(scores - high)
            total = jnp.sum(weights, axis=-1, keepdims=True)
            p_all[...] = weights.astype(BF16)
            inverse = 1.0 / total
            lse = high + jnp.log(total)
            first = lse.astype(BF16).astype(F32)
            second = (lse - first).astype(BF16).astype(F32)
            third = lse - first - second
            stats = jnp.zeros((tree, 128), F32)
            for i in range(len(pieces)):
                summed = dot(p_all[i * pair : (i + 1) * pair, :], v_ref[r, :, columns(i)])
                for h in range(2):
                    own = slice(i * pair + h * tree, i * pair + (h + 1) * tree)
                    cut = slice(h * HEAD_DIM, (h + 1) * HEAD_DIM)
                    value = summed[h * tree : (h + 1) * tree, cut] * inverse[own]
                    out_ref[2 * i + h, rows, :] = value.astype(out_ref.dtype)
                    if kept:
                        stats = jnp.where(lane == i * 8 + h, lse[own], stats)
                    else:
                        for j, part in enumerate((first, second, third)):
                            stats = jnp.where(lane == i * 8 + 2 * j + h, part[own], stats)
            if kept:
                outs[1][rows, :] = stats
            else:
                out_ref[8, rows, :] = stats.astype(BF16)

        @pl.when(live <= 0)
        def _():
            for i in range(8):
                out_ref[i, rows, :] = jnp.zeros((tree, HEAD_DIM), out_ref.dtype)
            empty = jnp.where(lane % 8 < 2, NEGATIVE, 0.0)
            if kept:
                outs[1][rows, :] = empty
            else:
                out_ref[8, rows, :] = empty.astype(BF16)


def merge_kernel(other_ref, kept_ref, lse_ref, *refs):
    outs, turn = refs[:-1], refs[-1]
    tokens = lse_ref.shape[0]
    sent = other_ref[8].astype(F32)
    other = sent + pltpu.roll(sent, 126, 1) + pltpu.roll(sent, 124, 1)
    kept = lse_ref[...]
    high = jnp.maximum(other, kept)
    other, kept = jnp.exp(other - high), jnp.exp(kept - high)
    whole = other + kept
    inverse = 1.0 / whole
    other, kept = other * inverse, kept * inverse
    lse = jnp.where(iota(high.shape, 1) % 8 < 2, high + jnp.log(whole), 0.0)
    first = lse.astype(BF16).astype(F32)
    second = (lse - first).astype(BF16).astype(F32)
    third = lse - first - second
    turn[0:tokens, :] = first + pltpu.roll(second, 2, 1) + pltpu.roll(third, 4, 1)
    turn[tokens:, :] = jnp.zeros((turn.shape[0] - tokens, 128), F32)
    turned = jnp.transpose(turn[...])
    for i, out_ref in enumerate(outs):
        for h in range(2):
            at = i * 8 + h
            value = other[:, at : at + 1] * other_ref[2 * i + h].astype(F32)
            value = value + kept[:, at : at + 1] * kept_ref[2 * i + h]
            out_ref[0:tokens, h * HEAD_DIM : (h + 1) * HEAD_DIM] = value.astype(BF16)
        out_ref[tokens:, :] = turned[i * 8 : (i + 1) * 8, :].astype(BF16)


def out_kernel(meta_ref, *refs):
    parts = refs[:4]
    tree_o_ref, tree_lse_ref, w_ref, theirs_ref, ours_ref, turn, mixed = refs[4:]
    padded, width = parts[0].shape
    tokens = padded - 8
    heads = width // HEAD_DIM
    own = ours_ref.shape[0] // 4
    lses = []
    for part in parts:
        rows = part[tokens:, :].astype(F32)
        lses.append(rows[0:2] + rows[2:4] + rows[4:6])
    lses.append(tree_lse_ref[0:2, :])
    high = functools.reduce(jnp.maximum, lses)
    factors = [jnp.exp(value - high) for value in lses]
    whole = functools.reduce(lambda a, b: a + b, factors)
    for s, factor in enumerate(factors):
        turn[2 * s : 2 * s + 2, :] = factor / whole
    turned = jnp.transpose(turn[...])[0:tokens, :]
    for h in range(heads):
        cut = slice(h * HEAD_DIM, (h + 1) * HEAD_DIM)
        at = 2 * len(parts) + h
        total = turned[:, at : at + 1] * tree_o_ref[:, cut]
        for s, part in enumerate(parts):
            at = 2 * s + h
            total = total + turned[:, at : at + 1] * part[0:tokens, cut].astype(F32)
        mixed[:, cut] = total

    def rows_of(first_at):
        rows = [
            mixed[pl.ds(pl.multiple_of(meta_ref[first_at + i], 8), own), :] for i in range(4)
        ]
        return jnp.concatenate(rows, axis=0).astype(BF16)

    theirs_ref[...] = dot(rows_of(20), w_ref[...]).astype(BF16)
    ours_ref[...] = dot(rows_of(16), w_ref[...])


def fold_kernel(ours_ref, theirs_ref, *outs):
    own = outs[0].shape[0]
    for i, out_ref in enumerate(outs):
        rows = slice(i * own, (i + 1) * own)
        out_ref[...] = (ours_ref[rows, :] + theirs_ref[rows, :].astype(F32)).astype(out_ref.dtype)


def expert_of_row(rows, experts):
    return jnp.where(iota((rows, experts), 0) // SLOTS == iota((rows, experts), 1), 1.0, 0.0)


def table_kernel(routes_ref, up_hbm, down_hbm, after_ref, *refs):
    place_refs, (weights_ref, sems) = refs[:3], refs[3:]
    del after_ref
    depth, both = up_hbm.shape
    units = down_hbm.shape[0]
    copies = [pltpu.make_async_copy(up_hbm, weights_ref.at[0:depth], sems.at[0])]
    for i in range(down_hbm.shape[1] // both):
        at = depth + i * units
        copies.append(
            pltpu.make_async_copy(
                down_hbm.at[:, i * both : (i + 1) * both],
                weights_ref.at[at : at + units],
                sems.at[1 + i],
            )
        )
    for copy in copies:
        copy.start()
    place_kernel(routes_ref, *place_refs)
    for copy in copies:
        copy.wait()


def place_kernel(routes_ref, place_ref, gather_ref, scatter_ref):
    chunks = place_ref.shape[0]
    _, real, block = gather_ref.shape
    row, column = iota((real, block), 0), iota((real, block), 1)
    base, slot = row // CAP * SLOTS, row % CAP
    gather_ref[0] = jnp.where(column == base + slot, 1.0, 0.0).astype(BF16)
    for k in range(chunks):
        hit = (column == base + CAP + slot // chunks) & (slot % chunks == k)
        gather_ref[1 + k] = jnp.where(hit, 1.0, 0.0).astype(BF16)
    row, column = iota((block, 2 * real), 0), iota((block, 2 * real), 1)
    is_tail = column >= real
    column = column - jnp.where(is_tail, real, 0)
    base, slot = column // CAP * SLOTS, column % CAP
    for k in range(chunks):
        main = (row == base + slot) & jnp.logical_not(is_tail)
        tail = (row == base + CAP + slot // chunks) & (slot % chunks == k) & is_tail
        scatter_ref[k] = jnp.where(main | tail, 1.0, 0.0).astype(BF16)
    top, tokens = routes_ref.shape
    chunks, rows, _ = place_ref.shape
    experts = rows // SLOTS
    named = iota((experts, tokens), 0)
    chosen = jnp.zeros((experts, tokens), F32)
    for k in range(top):
        chosen = jnp.where(routes_ref[k : k + 1, :] == named, 1.0, chosen)
    source = iota((tokens, 2 * tokens), 0)
    target = iota((tokens, 2 * tokens), 1) % tokens
    chosen = chosen.astype(BF16)
    rank = dot(chosen, jnp.where(source < target, 1.0, 0.0).astype(BF16))
    both = dot(chosen, jnp.where(source == target, 1.0, 0.0).astype(BF16))
    rank = jnp.where(both > 0.5, rank, -1.0).astype(BF16)
    spread = dot(expert_of_row(rows, experts).astype(BF16), rank)
    slot = iota((rows, 2 * tokens), 0) % SLOTS
    is_tail = iota((rows, 2 * tokens), 1) >= tokens
    for j in range(chunks):
        wanted = jnp.where(is_tail, (slot - CAP) * chunks + j, slot)
        valid = is_tail == (slot >= CAP)
        hit = valid & (spread == wanted.astype(F32))
        place_ref[j] = jnp.where(hit, 1.0, 0.0).astype(BF16)


def residual_kernel(meta_ref, *refs):
    parts = refs[:4]
    x_ref, g_ref, place_ref, res_ref, normed_ref, out_ref = refs[4:]
    tokens, width = parts[0].shape
    chunks = place_ref.shape[0]
    cut = width // (chunks + 1)
    start = pl.multiple_of(meta_ref[16], 8)
    residual = x_ref[pl.ds(start, tokens), :].astype(F32)
    for part in parts:
        residual = residual + part[...].astype(F32)
    res_ref[...] = residual
    inverse = lax.rsqrt(jnp.mean(residual * residual, axis=-1, keepdims=True) + EPSILON)
    normed = residual * inverse * g_ref[...].astype(F32).reshape(1, -1)
    normed_ref[...] = normed.astype(BF16)
    tail = normed[:, chunks * cut :]
    for j in range(chunks):
        pair = jnp.concatenate([normed[:, j * cut : (j + 1) * cut], tail], axis=0).astype(BF16)
        out_ref[:, j * cut : (j + 1) * cut] = dot(place_ref[j], pair).astype(BF16)


def gate_kernel(normed_ref, router_ref, routes_ref, table_ref):
    top, tokens = routes_ref.shape
    experts = router_ref.shape[0]
    chunks, _, rows = table_ref.shape
    logits = dot_t(normed_ref[...], router_ref[...])
    exponent = jnp.exp(logits)
    chances = exponent / jnp.sum(exponent, axis=-1, keepdims=True)
    named = iota((experts, tokens), 0)
    chosen = jnp.zeros((experts, tokens), F32)
    for k in range(top):
        chosen = jnp.where(routes_ref[k : k + 1, :] == named, 1.0, chosen)
    same = jnp.where(iota((tokens, tokens), 0) == iota((tokens, tokens), 1), 1.0, 0.0)
    chosen = dot_t(same.astype(BF16), chosen.astype(BF16))
    picked = chances * chosen
    gates = picked / jnp.sum(picked, axis=-1, keepdims=True)
    earlier = jnp.where(iota((tokens, tokens), 0) > iota((tokens, tokens), 1), 1.0, 0.0)
    rank = dot(earlier.astype(BF16), chosen.astype(BF16))
    rank = jnp.where(chosen > 0.5, rank, -1.0).astype(BF16)
    first = gates.astype(BF16)
    second = (gates - first.astype(F32)).astype(BF16)
    home = iota((experts, rows), 0) == iota((experts, rows), 1) // SLOTS
    home = jnp.where(home, 1.0, 0.0).astype(BF16)
    rank, first, second = dot(rank, home), dot(first, home), dot(second, home)
    slot = iota((tokens, rows), 1) % SLOTS
    main = (slot < CAP) & (rank == slot.astype(F32))
    for j in range(chunks):
        tail = (slot >= CAP) & (rank == ((slot - CAP) * chunks + j).astype(F32))
        table_ref[j] = jnp.concatenate(
            [
                jnp.where(main, first, 0.0),
                jnp.where(main, second, 0.0),
                jnp.where(tail, first, 0.0),
                jnp.where(tail, second, 0.0),
            ],
            axis=0,
        ).astype(BF16)


def expert_kernel(
    x_ref,
    weights_ref,
    other_ref,
    gather_ref,
    scatter_ref,
    normed_ref,
    router_ref,
    routes_ref,
    out_ref,
    table_ref,
):
    gate_kernel(normed_ref, router_ref, routes_ref, table_ref)
    rows, packed = x_ref.shape
    width = normed_ref.shape[1]
    both = weights_ref.shape[1]
    units = both // 2
    cut = width - packed
    chunks = packed // cut
    _, real, block = gather_ref.shape
    mains, tails = [], []
    for at in range(0, rows, block):
        span = slice(at, at + block)
        mains.append(dot(gather_ref[0], x_ref[span, :]).astype(BF16))
        tail = dot(gather_ref[1], x_ref[span, 0:cut])
        for k in range(1, chunks):
            tail = tail + dot(gather_ref[1 + k], x_ref[span, k * cut : (k + 1) * cut])
        tails.append(tail.astype(BF16))
    main, tail = jnp.concatenate(mains, axis=0), jnp.concatenate(tails, axis=0)
    hidden = []
    for weights in (weights_ref, other_ref):
        parts = []
        for at in range(0, units, units // 2):
            gate_cut = slice(at, at + units // 2)
            up_cut = slice(units + at, units + at + units // 2)
            gate = dot(main, weights[0:packed, gate_cut]) + dot(tail, weights[packed:width, gate_cut])
            up = dot(main, weights[0:packed, up_cut]) + dot(tail, weights[packed:width, up_cut])
            parts.append((gate / (1.0 + jnp.exp(-gate)) * up).astype(BF16))
        hidden.append(jnp.concatenate(parts, axis=1))

    def result(k):
        at = width + k * cut // both * units
        rows, columns = slice(at, at + units), slice(k * cut % both, k * cut % both + cut)
        first = dot(hidden[0], weights_ref[rows, columns]).astype(BF16).astype(F32)
        second = dot(hidden[1], other_ref[rows, columns]).astype(BF16).astype(F32)
        return (first + second).astype(BF16)

    last = result(chunks)
    for k in range(chunks):
        columns = slice(k * cut, (k + 1) * cut)
        value = result(k)
        for i in range(rows // block):
            own = slice(i * real, (i + 1) * real)
            pair = jnp.concatenate([value[own], last[own]], axis=0)
            out_ref[i * block : (i + 1) * block, columns] = dot(scatter_ref[k], pair).astype(
                BF16
            )


def final_kernel(back_ref, table_ref, res_ref, out_ref):
    tokens, width = res_ref.shape
    chunks = table_ref.shape[0]
    cut = width // (chunks + 1)
    tail = res_ref[:, chunks * cut :]
    for j in range(chunks):
        span = slice(j * cut, (j + 1) * cut)
        sums = dot(table_ref[j], back_ref[:, span])
        main = sums[0:tokens] + sums[tokens : 2 * tokens]
        out_ref[:, span] = (res_ref[:, span] + main).astype(BF16)
        tail = tail + (sums[2 * tokens : 3 * tokens] + sums[3 * tokens :])
    out_ref[:, chunks * cut :] = tail.astype(BF16)


def per_device(
    hidden,
    gain_attn,
    w_qkv,
    w_out,
    cache_keys,
    cache_values,
    cache_lengths,
    parents,
    gain_moe,
    w_router,
    routes,
    w_gate_up,
    w_down,
):
    z_count = lax.axis_size("z")
    exp_count = z_count * CORES
    z_index = lax.axis_index("z")
    core = lax.axis_index("core")
    exp_index = z_index * CORES + core
    tokens, width = hidden.shape
    requests, tree = parents.shape
    page = cache_keys.shape[1]
    local_width = w_qkv.shape[2]
    scale = HEAD_DIM ** (-0.5)
    own = tokens // exp_count
    experts = w_router.shape[1]
    packed = width * CAP // SLOTS
    chunks = packed // (width - packed)
    padded = tokens + 8

    w_three = pltpu.with_memory_space_constraint(jnp.transpose(w_qkv, (1, 0, 2)), HBM)
    cache_keys = pltpu.with_memory_space_constraint(cache_keys, HBM)
    cache_values = pltpu.with_memory_space_constraint(cache_values, HBM)

    query = call(
        query_kernel,
        sds((tokens, local_width), BF16),
        [HBM, HBM, HBM],
        [
            pltpu.VMEM((tokens, width), BF16),
            pltpu.VMEM((width,), BF16),
            pltpu.VMEM((width, local_width), BF16),
            pltpu.SemaphoreType.DMA((3,)),
        ],
        flops=2 * tokens * width * local_width,
        bytes_accessed=2 * width * (tokens + local_width),
    )(
        pltpu.with_memory_space_constraint(hidden, HBM),
        pltpu.with_memory_space_constraint(gain_attn, HBM),
        w_three,
    )

    def over_z(value, step):
        return lax.ppermute(value, "z", [(i, (i + step) % z_count) for i in range(z_count)])

    def over_core(value):
        return lax.ppermute(value, "core", [(0, 1), (1, 0)])

    steps = range(1, z_count)
    pieces = [query] + [over_z(query, step) for step in steps]
    other_pieces = [over_core(piece) for piece in pieces]
    homes = jnp.bitwise_and(z_index - jnp.arange(z_count), z_count - 1) * CORES
    homes = jnp.stack([homes + core, homes + 1 - core])
    meta = jnp.concatenate(
        [
            cache_lengths - exp_index * page,
            jnp.zeros((8 - requests,), jnp.int32),
            (homes * local_width).reshape(-1),
            (homes * own).reshape(-1),
        ]
    ).astype(jnp.int32)

    keys = call(
        load_kernel,
        sds(cache_keys.shape, BF16),
        [HBM, pl.ANY],
        [pltpu.SemaphoreType.DMA],
        bytes_accessed=2 * requests * page * width,
    )(cache_keys, query)

    scratch = [
        pltpu.VMEM((z_count * 2 * tree, page), F32),
        pltpu.VMEM((z_count * 2 * tree, page), BF16),
    ]
    heads = 2 * z_count
    for_other, values = call(
        functools.partial(page_kernel, scale, tree, False),
        (sds((heads + 1, tokens, HEAD_DIM), BF16), sds(cache_values.shape, BF16)),
        [SMEM] + [VMEM] * 5 + [HBM],
        scratch + [pltpu.SemaphoreType.DMA((requests,))],
        flops=2 * tokens * page * width,
        bytes_accessed=2 * requests * page * width,
        vmem=20 << 20,
    )(meta, *other_pieces, keys, cache_values)
    from_other = over_core(for_other)
    kept, kept_lse = call(
        functools.partial(page_kernel, scale, tree, True),
        (sds((heads, tokens, HEAD_DIM), F32), sds((tokens, 128), F32)),
        [SMEM] + [VMEM] * 6 + [pl.ANY],
        scratch,
        flops=2 * tokens * page * width,
        bytes_accessed=2 * requests * page * width,
        vmem=20 << 20,
    )(meta, *pieces, keys, values, for_other)
    merged = call(
        merge_kernel,
        tuple(sds((padded, local_width), BF16) for _ in range(z_count)),
        [VMEM] * 3,
        [pltpu.VMEM((256, 128), F32)],
        bytes_accessed=1 << 20,
    )(from_other, kept, kept_lse)
    arrived = [merged[0]] + [over_z(merged[step], -step) for step in steps]

    tree_o, tree_lse = call(
        functools.partial(tree_kernel, scale),
        (sds((tokens, local_width), F32), sds((8, 256), F32)),
        [VMEM, VMEM, HBM, VMEM, VMEM, pl.ANY],
        [
            pltpu.VMEM((256, 128), F32),
            pltpu.VMEM((2, width, local_width), BF16),
            pltpu.SemaphoreType.DMA((2,)),
        ],
        flops=4 * tokens * width * local_width,
        bytes_accessed=2 * width * (tokens + 2 * local_width),
    )(hidden, gain_attn, w_three, query, parents, merged[0])
    theirs, ours = call(
        out_kernel,
        (sds((z_count * own, width), BF16), sds((z_count * own, width), F32)),
        [SMEM] + [VMEM] * 7,
        [pltpu.VMEM((128, 256), F32), pltpu.VMEM((tokens, local_width), F32)],
        flops=2 * tokens * width * local_width,
        bytes_accessed=2 * width * (tokens + local_width),
    )(meta, *arrived, tree_o, tree_lse, w_out)
    folded = call(
        fold_kernel,
        tuple(sds((own, width), BF16 if step else F32) for step in range(z_count)),
        [VMEM] * 2,
        bytes_accessed=1 << 20,
    )(ours, over_core(theirs))
    mixed = [folded[0]] + [over_z(folded[step], -step) for step in steps]
    block = experts * SLOTS // 2
    real = block // SLOTS * CAP
    weight_rows = width + width * w_down.shape[1] // w_gate_up.shape[2]
    place, gather, scatter, weights = call(
        table_kernel,
        (
            sds((chunks, experts * SLOTS, 2 * own), BF16),
            sds((1 + chunks, real, block), BF16),
            sds((chunks, block, 2 * real), BF16),
            sds((weight_rows, w_gate_up.shape[2]), BF16),
        ),
        [VMEM, HBM, HBM, pl.ANY],
        [pltpu.SemaphoreType.DMA((1 + width // w_gate_up.shape[2],))],
        flops=1 << 24,
        bytes_accessed=1 << 23,
        vmem=16 << 20,
    )(
        routes.T,
        pltpu.with_memory_space_constraint(w_gate_up[0], HBM),
        pltpu.with_memory_space_constraint(w_down[0], HBM),
        folded[0],
    )
    *mixed, weights = lax.optimization_barrier((*mixed, weights))
    other_weights = over_core(weights)

    residual, normed, outgoing = call(
        residual_kernel,
        (
            sds((own, width), F32),
            sds((own, width), BF16),
            sds((experts * SLOTS, packed), BF16),
        ),
        [SMEM] + [VMEM] * 7,
        flops=1 << 27,
        bytes_accessed=1 << 22,
    )(meta, *mixed, hidden, gain_moe, place)
    rows = lax.all_to_all(
        outgoing.reshape(experts, SLOTS, packed),
        ("req", "z"),
        split_axis=0,
        concat_axis=0,
        tiled=True,
    ).reshape(experts * SLOTS, packed)

    summed, table = call(
        expert_kernel,
        (
            sds((experts * SLOTS, packed), BF16),
            sds((chunks, 4 * own, experts * SLOTS), BF16),
        ),
        [VMEM] * 8,
        flops=12 * experts * CAP * width * w_down.shape[1],
        bytes_accessed=12 * width * w_down.shape[1],
        vmem=24 << 20,
    )(
        rows,
        weights,
        other_weights,
        gather,
        scatter,
        normed,
        w_router.T,
        routes.T,
    )
    back = lax.all_to_all(
        summed.reshape(experts, SLOTS, packed),
        ("req", "z"),
        split_axis=0,
        concat_axis=0,
        tiled=True,
    ).reshape(experts * SLOTS, packed)
    return call(
        final_kernel,
        sds((own, width), BF16),
        [VMEM] * 3,
        flops=1 << 27,
        bytes_accessed=1 << 22,
    )(back, table, residual)


def solution(mesh):
    req_count, exp_count = mesh.devices.shape
    split = Mesh(
        mesh.devices.reshape(req_count, exp_count // CORES, CORES), ("req", "z", "core")
    )
    exp = ("z", "core")
    everywhere = ("req", "z", "core")
    in_specs = (
        P("req", None),
        P(),
        P(None, None, exp),
        P(exp, None),
        P("req", exp, None),
        P("req", exp, None),
        P("req"),
        P("req", None),
        P(),
        P(),
        P(everywhere, None),
        P(everywhere, None, None),
        P(everywhere, None, None),
    )
    return jax.shard_map(
        per_device,
        mesh=split,
        in_specs=in_specs,
        out_specs=P(everywhere, None),
        check_vma=False,
    )
```

```python
import functools

import jax
import jax.numpy as jnp
from jax import lax
from jax.experimental import pallas as pl
from jax.experimental.pallas import tpu as pltpu
from jax.sharding import Mesh
from jax.sharding import PartitionSpec as P

HEAD_DIM = 128
EXP_SPLIT = 2
CORES = 2
CAP = 6
SLOTS = 8

EPSILON = 1e-05
NEGATIVE = -1e30
F32 = jnp.float32
BF16 = jnp.bfloat16
VMEM = pltpu.VMEM
SMEM = pltpu.SMEM
HBM = pltpu.HBM


def dot(a, b):
    return jnp.dot(a, b, preferred_element_type=F32)


def dot_t(a, b):
    return lax.dot_general(a, b, (((1,), (1,)), ((), ())), preferred_element_type=F32)


def iota(shape, axis):
    return lax.broadcasted_iota(jnp.int32, shape, axis)


def call(body, out, in_spaces, scratch=(), flops=0, bytes_accessed=0, vmem=10 << 20, aliases={}):
    out_spec = jax.tree.map(lambda _: pl.BlockSpec(memory_space=VMEM), out)
    return pl.pallas_call(
        body,
        out_shape=out,
        in_specs=[pl.BlockSpec(memory_space=s) for s in in_spaces],
        out_specs=out_spec,
        scratch_shapes=list(scratch),
        input_output_aliases=aliases,
        compiler_params=pltpu.CompilerParams(vmem_limit_bytes=vmem),
        cost_estimate=pl.CostEstimate(
            flops=flops, bytes_accessed=bytes_accessed, transcendentals=0
        ),
    )


def sds(shape, dtype):
    return jax.ShapeDtypeStruct(shape, dtype)


def homes(count, other):
    z, core = lax.axis_index("z"), lax.axis_index("core")
    core = 1 - core if other else core
    return [lax.rem(z + count - i, count) * CORES + core for i in range(count)]


def normed_rows(values, gain):
    inverse = lax.rsqrt(jnp.mean(values * values, axis=-1, keepdims=True) + EPSILON)
    return (values * inverse * gain).astype(BF16)


def query_kernel(x_hbm, g_hbm, w_hbm, q_ref, x_ref, g_ref, w_ref, sems):
    half = x_ref.shape[0] // 2
    rows = [slice(0, half), slice(half, 2 * half)]
    g_copy = pltpu.make_async_copy(g_hbm, g_ref, sems.at[0])
    x_copies = [
        pltpu.make_async_copy(x_hbm.at[rows[i]], x_ref.at[rows[i]], sems.at[1 + i])
        for i in range(2)
    ]
    w_copy = pltpu.make_async_copy(w_hbm.at[0], w_ref, sems.at[3])
    g_copy.start()
    for copy in x_copies:
        copy.start()
    w_copy.start()
    g_copy.wait()
    gain = g_ref[...].astype(F32).reshape(1, -1)
    normed = []
    for copy, cut in zip(x_copies, rows):
        copy.wait()
        normed.append(normed_rows(x_ref[cut, :].astype(F32), gain))
    w_copy.wait()
    for values, cut in zip(normed, rows):
        q_ref[cut, :] = dot(values, w_ref[...]).astype(BF16)


def load_kernel(k_hbm, v_hbm, after_ref, k_ref, v_ref, sems):
    del after_ref
    copies = [
        pltpu.make_async_copy(k_hbm, k_ref, sems.at[0]),
        pltpu.make_async_copy(v_hbm, v_ref, sems.at[1]),
    ]
    for copy in copies:
        copy.start()
    for copy in copies:
        copy.wait()


def tree_kernel(scale, x_ref, g_ref, w_hbm, q_ref, up_ref, after_ref, *refs):
    o_ref, lse_ref, turn, w_ref, sems = refs
    del after_ref
    tokens, width = q_ref.shape
    w_copies = [
        pltpu.make_async_copy(w_hbm.at[i + 1], w_ref.at[i], sems.at[i]) for i in range(2)
    ]
    for w_copy in w_copies:
        w_copy.start()
    normed = normed_rows(x_ref[...].astype(F32), g_ref[...].astype(F32).reshape(1, -1))
    w_copies[0].wait()
    keys = dot(normed, w_ref[0]).astype(BF16)
    w_copies[1].wait()
    values = dot(normed, w_ref[1]).astype(BF16)
    requests, tree = up_ref.shape
    spread = iota((tree, tokens), 0) == iota((tree, tokens), 1) % tree
    wide = dot(up_ref[...].astype(BF16), jnp.where(spread, 1.0, 0.0).astype(BF16))
    home = iota((requests, tokens), 1) // tree
    wide = jnp.where(iota((requests, tokens), 0) == home, wide + (home * tree).astype(F32), 0.0)
    parent = jnp.sum(wide, axis=0, keepdims=True)
    row = iota((tokens, tokens), 0)
    same = row == iota((tokens, tokens), 1)
    reach = jnp.where(same | (row.astype(F32) == parent), 1.0, 0.0)
    for _ in range(6):
        half = reach.astype(BF16)
        reach = jnp.minimum(dot(half, half), 1.0)
    visible = dot_t(jnp.where(same, 1.0, 0.0).astype(BF16), reach.astype(BF16)) > 0.5
    lane = iota((tokens, 128), 1)
    stats = jnp.zeros((tokens, 128), F32)
    for h in range(width // HEAD_DIM):
        cut = slice(h * HEAD_DIM, (h + 1) * HEAD_DIM)
        scores = dot_t(q_ref[:, cut], keys[:, cut]) * scale
        scores = jnp.where(visible, scores, NEGATIVE)
        high = jnp.max(scores, axis=-1, keepdims=True)
        weights = jnp.where(visible, jnp.exp(scores - high), 0.0)
        total = jnp.sum(weights, axis=-1, keepdims=True)
        o_ref[:, cut] = dot(weights.astype(BF16), values[:, cut]) / total
        stats = jnp.where(lane == h, high + jnp.log(total), stats)
    turn[0:tokens, :] = stats
    lse_ref[...] = jnp.transpose(turn[...])[0:8, :]


def page_kernel(scale, tree, kept, lengths_ref, *refs):
    pieces, (k_ref, v_ref) = refs[:4], refs[4:6]
    outs = refs[7:-2] if kept else refs[6:-2]
    s_all, p_all = refs[-2:]
    out_ref = outs[0]
    requests, page = k_ref.shape[0], k_ref.shape[1]
    width = pieces[0].shape[1]
    pair = 2 * tree
    lane = iota((tree, 128), 1)
    wide = iota((tree, width), 1) < HEAD_DIM
    owners = homes(len(pieces), not kept)
    start = (lax.axis_index("z") * CORES + lax.axis_index("core")) * page

    def columns(i):
        return pl.ds(pl.multiple_of(owners[i] * width, width), width)

    for r in range(requests):
        rows = slice(r * tree, (r + 1) * tree)
        live = lengths_ref[r] - start

        @pl.when(live > 0)
        def _():
            for i, piece in enumerate(pieces):
                query = piece[rows, :]
                zero = jnp.zeros_like(query)
                both = jnp.concatenate(
                    [jnp.where(wide, query, zero), jnp.where(wide, zero, query)], axis=0
                )
                s_all[i * pair : (i + 1) * pair, :] = dot_t(both, k_ref[r, :, columns(i)])
            scores = s_all[...] * scale
            scores = jnp.where(iota(scores.shape, 1) < live, scores, NEGATIVE)
            high = jnp.max(scores, axis=-1, keepdims=True)
            weights = jnp.exp(scores - high)
            total = jnp.sum(weights, axis=-1, keepdims=True)
            p_all[...] = weights.astype(BF16)
            inverse = 1.0 / total
            lse = high + jnp.log(total)
            first = lse.astype(BF16).astype(F32)
            second = (lse - first).astype(BF16).astype(F32)
            third = lse - first - second
            stats = jnp.zeros((tree, 128), F32)
            for i in range(len(pieces)):
                summed = dot(p_all[i * pair : (i + 1) * pair, :], v_ref[r, :, columns(i)])
                for h in range(2):
                    own = slice(i * pair + h * tree, i * pair + (h + 1) * tree)
                    cut = slice(h * HEAD_DIM, (h + 1) * HEAD_DIM)
                    value = summed[h * tree : (h + 1) * tree, cut] * inverse[own]
                    out_ref[2 * i + h, rows, :] = value.astype(out_ref.dtype)
                    if kept:
                        stats = jnp.where(lane == i * 8 + h, lse[own], stats)
                    else:
                        for j, part in enumerate((first, second, third)):
                            stats = jnp.where(lane == i * 8 + 2 * j + h, part[own], stats)
            if kept:
                outs[1][rows, :] = stats
            else:
                out_ref[8, rows, :] = stats.astype(BF16)

        @pl.when(live <= 0)
        def _():
            for i in range(8):
                out_ref[i, rows, :] = jnp.zeros((tree, HEAD_DIM), out_ref.dtype)
            empty = jnp.where(lane % 8 < 2, NEGATIVE, 0.0)
            if kept:
                outs[1][rows, :] = empty
            else:
                out_ref[8, rows, :] = empty.astype(BF16)


def merge_kernel(other_ref, kept_ref, lse_ref, *refs):
    outs, turn = refs[:-1], refs[-1]
    tokens = lse_ref.shape[0]
    sent = other_ref[8].astype(F32)
    other = sent + pltpu.roll(sent, 126, 1) + pltpu.roll(sent, 124, 1)
    kept = lse_ref[...]
    high = jnp.maximum(other, kept)
    other, kept = jnp.exp(other - high), jnp.exp(kept - high)
    whole = other + kept
    inverse = 1.0 / whole
    other, kept = other * inverse, kept * inverse
    lse = jnp.where(iota(high.shape, 1) % 8 < 2, high + jnp.log(whole), 0.0)
    first = lse.astype(BF16).astype(F32)
    second = (lse - first).astype(BF16).astype(F32)
    third = lse - first - second
    turn[0:tokens, :] = first + pltpu.roll(second, 2, 1) + pltpu.roll(third, 4, 1)
    turn[tokens:, :] = jnp.zeros((turn.shape[0] - tokens, 128), F32)
    turned = jnp.transpose(turn[...])
    for i, out_ref in enumerate(outs):
        for h in range(2):
            at = i * 8 + h
            value = other[:, at : at + 1] * other_ref[2 * i + h].astype(F32)
            value = value + kept[:, at : at + 1] * kept_ref[2 * i + h]
            out_ref[0:tokens, h * HEAD_DIM : (h + 1) * HEAD_DIM] = value.astype(BF16)
        out_ref[tokens:, :] = turned[i * 8 : (i + 1) * 8, :].astype(BF16)


def out_kernel(*refs):
    parts = refs[:4]
    tree_o_ref, tree_lse_ref, w_ref, theirs_ref, ours_ref, turn, mixed = refs[4:]
    padded, width = parts[0].shape
    tokens = padded - 8
    heads = width // HEAD_DIM
    own = ours_ref.shape[0] // 4
    lses = []
    for part in parts:
        rows = part[tokens:, :].astype(F32)
        lses.append(rows[0:2] + rows[2:4] + rows[4:6])
    lses.append(tree_lse_ref[0:2, :])
    high = functools.reduce(jnp.maximum, lses)
    factors = [jnp.exp(value - high) for value in lses]
    whole = functools.reduce(lambda a, b: a + b, factors)
    for s, factor in enumerate(factors):
        turn[2 * s : 2 * s + 2, :] = factor / whole
    turned = jnp.transpose(turn[...])[0:tokens, :]
    for h in range(heads):
        cut = slice(h * HEAD_DIM, (h + 1) * HEAD_DIM)
        at = 2 * len(parts) + h
        total = turned[:, at : at + 1] * tree_o_ref[:, cut]
        for s, part in enumerate(parts):
            at = 2 * s + h
            total = total + turned[:, at : at + 1] * part[0:tokens, cut].astype(F32)
        mixed[:, cut] = total

    def rows_of(other):
        rows = [
            mixed[pl.ds(pl.multiple_of(owner * own, 8), own), :]
            for owner in homes(len(parts), other)
        ]
        return jnp.concatenate(rows, axis=0).astype(BF16)

    theirs_ref[...] = dot(rows_of(True), w_ref[...]).astype(BF16)
    ours_ref[...] = dot(rows_of(False), w_ref[...])


def fold_kernel(ours_ref, theirs_ref, *outs):
    own = outs[0].shape[0]
    for i, out_ref in enumerate(outs):
        rows = slice(i * own, (i + 1) * own)
        out_ref[...] = (ours_ref[rows, :] + theirs_ref[rows, :].astype(F32)).astype(out_ref.dtype)


def expert_of_row(rows, experts):
    return jnp.where(iota((rows, experts), 0) // SLOTS == iota((rows, experts), 1), 1.0, 0.0)


def table_kernel(routes_ref, up_hbm, down_hbm, after_ref, *refs):
    place_refs, (weights_ref, sems) = refs[:3], refs[3:]
    del after_ref
    depth, both = up_hbm.shape
    units = down_hbm.shape[0]
    copies = [pltpu.make_async_copy(up_hbm, weights_ref.at[0:depth], sems.at[0])]
    for i in range(down_hbm.shape[1] // both):
        at = depth + i * units
        copies.append(
            pltpu.make_async_copy(
                down_hbm.at[:, i * both : (i + 1) * both],
                weights_ref.at[at : at + units],
                sems.at[1 + i],
            )
        )
    for copy in copies:
        copy.start()
    place_kernel(routes_ref, *place_refs)
    for copy in copies:
        copy.wait()


def place_kernel(routes_ref, place_ref, gather_ref, scatter_ref):
    chunks = place_ref.shape[0]
    _, real, block = gather_ref.shape
    row, column = iota((real, block), 0), iota((real, block), 1)
    base, slot = row // CAP * SLOTS, row % CAP
    gather_ref[0] = jnp.where(column == base + slot, 1.0, 0.0).astype(BF16)
    for k in range(chunks):
        hit = (column == base + CAP + slot // chunks) & (slot % chunks == k)
        gather_ref[1 + k] = jnp.where(hit, 1.0, 0.0).astype(BF16)
    row, column = iota((block, 2 * real), 0), iota((block, 2 * real), 1)
    is_tail = column >= real
    column = column - jnp.where(is_tail, real, 0)
    base, slot = column // CAP * SLOTS, column % CAP
    for k in range(chunks):
        main = (row == base + slot) & jnp.logical_not(is_tail)
        tail = (row == base + CAP + slot // chunks) & (slot % chunks == k) & is_tail
        scatter_ref[k] = jnp.where(main | tail, 1.0, 0.0).astype(BF16)
    top, tokens = routes_ref.shape
    chunks, rows, _ = place_ref.shape
    experts = rows // SLOTS
    named = iota((experts, tokens), 0)
    chosen = jnp.zeros((experts, tokens), F32)
    for k in range(top):
        chosen = jnp.where(routes_ref[k : k + 1, :] == named, 1.0, chosen)
    source = iota((tokens, 2 * tokens), 0)
    target = iota((tokens, 2 * tokens), 1) % tokens
    chosen = chosen.astype(BF16)
    rank = dot(chosen, jnp.where(source < target, 1.0, 0.0).astype(BF16))
    both = dot(chosen, jnp.where(source == target, 1.0, 0.0).astype(BF16))
    rank = jnp.where(both > 0.5, rank, -1.0).astype(BF16)
    spread = dot(expert_of_row(rows, experts).astype(BF16), rank)
    slot = iota((rows, 2 * tokens), 0) % SLOTS
    is_tail = iota((rows, 2 * tokens), 1) >= tokens
    for j in range(chunks):
        wanted = jnp.where(is_tail, (slot - CAP) * chunks + j, slot)
        valid = is_tail == (slot >= CAP)
        hit = valid & (spread == wanted.astype(F32))
        place_ref[j] = jnp.where(hit, 1.0, 0.0).astype(BF16)


def residual_kernel(*refs):
    parts = refs[:4]
    x_ref, g_ref, place_ref, res_ref, normed_ref, out_ref = refs[4:]
    tokens, width = parts[0].shape
    chunks = place_ref.shape[0]
    cut = width // (chunks + 1)
    start = pl.multiple_of(homes(len(parts), False)[0] * tokens, 8)
    residual = x_ref[pl.ds(start, tokens), :].astype(F32)
    for part in parts:
        residual = residual + part[...].astype(F32)
    res_ref[...] = residual
    inverse = lax.rsqrt(jnp.mean(residual * residual, axis=-1, keepdims=True) + EPSILON)
    normed = residual * inverse * g_ref[...].astype(F32).reshape(1, -1)
    normed_ref[...] = normed.astype(BF16)
    tail = normed[:, chunks * cut :]
    for j in range(chunks):
        pair = jnp.concatenate([normed[:, j * cut : (j + 1) * cut], tail], axis=0).astype(BF16)
        out_ref[:, j * cut : (j + 1) * cut] = dot(place_ref[j], pair).astype(BF16)


def gate_kernel(normed_ref, router_ref, routes_ref, table_ref):
    top, tokens = routes_ref.shape
    experts = router_ref.shape[0]
    chunks, _, rows = table_ref.shape
    logits = dot_t(normed_ref[...], router_ref[...])
    exponent = jnp.exp(logits)
    chances = exponent / jnp.sum(exponent, axis=-1, keepdims=True)
    named = iota((experts, tokens), 0)
    chosen = jnp.zeros((experts, tokens), F32)
    for k in range(top):
        chosen = jnp.where(routes_ref[k : k + 1, :] == named, 1.0, chosen)
    same = jnp.where(iota((tokens, tokens), 0) == iota((tokens, tokens), 1), 1.0, 0.0)
    chosen = dot_t(same.astype(BF16), chosen.astype(BF16))
    picked = chances * chosen
    gates = picked / jnp.sum(picked, axis=-1, keepdims=True)
    earlier = jnp.where(iota((tokens, tokens), 0) > iota((tokens, tokens), 1), 1.0, 0.0)
    rank = dot(earlier.astype(BF16), chosen.astype(BF16))
    rank = jnp.where(chosen > 0.5, rank, -1.0).astype(BF16)
    first = gates.astype(BF16)
    second = (gates - first.astype(F32)).astype(BF16)
    home = iota((experts, rows), 0) == iota((experts, rows), 1) // SLOTS
    home = jnp.where(home, 1.0, 0.0).astype(BF16)
    rank, first, second = dot(rank, home), dot(first, home), dot(second, home)
    slot = iota((tokens, rows), 1) % SLOTS
    main = (slot < CAP) & (rank == slot.astype(F32))
    for j in range(chunks):
        tail = (slot >= CAP) & (rank == ((slot - CAP) * chunks + j).astype(F32))
        table_ref[j] = jnp.concatenate(
            [
                jnp.where(main, first, 0.0),
                jnp.where(main, second, 0.0),
                jnp.where(tail, first, 0.0),
                jnp.where(tail, second, 0.0),
            ],
            axis=0,
        ).astype(BF16)


def expert_kernel(
    x_ref,
    weights_ref,
    other_ref,
    gather_ref,
    scatter_ref,
    normed_ref,
    router_ref,
    routes_ref,
    out_ref,
    table_ref,
):
    gate_kernel(normed_ref, router_ref, routes_ref, table_ref)
    rows, packed = x_ref.shape
    width = normed_ref.shape[1]
    both = weights_ref.shape[1]
    units = both // 2
    cut = width - packed
    chunks = packed // cut
    _, real, block = gather_ref.shape
    mains, tails = [], []
    for at in range(0, rows, block):
        span = slice(at, at + block)
        mains.append(dot(gather_ref[0], x_ref[span, :]).astype(BF16))
        tail = dot(gather_ref[1], x_ref[span, 0:cut])
        for k in range(1, chunks):
            tail = tail + dot(gather_ref[1 + k], x_ref[span, k * cut : (k + 1) * cut])
        tails.append(tail.astype(BF16))
    main, tail = jnp.concatenate(mains, axis=0), jnp.concatenate(tails, axis=0)
    hidden = []
    for weights in (weights_ref, other_ref):
        parts = []
        for at in range(0, units, units // 2):
            gate_cut = slice(at, at + units // 2)
            up_cut = slice(units + at, units + at + units // 2)
            gate = dot(main, weights[0:packed, gate_cut]) + dot(tail, weights[packed:width, gate_cut])
            up = dot(main, weights[0:packed, up_cut]) + dot(tail, weights[packed:width, up_cut])
            parts.append((gate / (1.0 + jnp.exp(-gate)) * up).astype(BF16))
        hidden.append(jnp.concatenate(parts, axis=1))

    def result(k):
        at = width + k * cut // both * units
        rows, columns = slice(at, at + units), slice(k * cut % both, k * cut % both + cut)
        first = dot(hidden[0], weights_ref[rows, columns]).astype(BF16).astype(F32)
        second = dot(hidden[1], other_ref[rows, columns]).astype(BF16).astype(F32)
        return (first + second).astype(BF16)

    last = result(chunks)
    for k in range(chunks):
        columns = slice(k * cut, (k + 1) * cut)
        value = result(k)
        for i in range(rows // block):
            own = slice(i * real, (i + 1) * real)
            pair = jnp.concatenate([value[own], last[own]], axis=0)
            out_ref[i * block : (i + 1) * block, columns] = dot(scatter_ref[k], pair).astype(
                BF16
            )


def final_kernel(back_ref, table_ref, res_ref, out_ref):
    tokens, width = res_ref.shape
    chunks = table_ref.shape[0]
    cut = width // (chunks + 1)
    tail = res_ref[:, chunks * cut :]
    for j in range(chunks):
        span = slice(j * cut, (j + 1) * cut)
        sums = dot(table_ref[j], back_ref[:, span])
        main = sums[0:tokens] + sums[tokens : 2 * tokens]
        out_ref[:, span] = (res_ref[:, span] + main).astype(BF16)
        tail = tail + (sums[2 * tokens : 3 * tokens] + sums[3 * tokens :])
    out_ref[:, chunks * cut :] = tail.astype(BF16)


def per_device(
    hidden,
    gain_attn,
    w_qkv,
    w_out,
    cache_keys,
    cache_values,
    cache_lengths,
    parents,
    gain_moe,
    w_router,
    routes,
    w_gate_up,
    w_down,
):
    z_count = lax.axis_size("z")
    exp_count = z_count * CORES
    tokens, width = hidden.shape
    requests, tree = parents.shape
    page = cache_keys.shape[1]
    local_width = w_qkv.shape[2]
    scale = HEAD_DIM ** (-0.5)
    own = tokens // exp_count
    experts = w_router.shape[1]
    packed = width * CAP // SLOTS
    chunks = packed // (width - packed)
    padded = tokens + 8

    w_three = pltpu.with_memory_space_constraint(jnp.transpose(w_qkv, (1, 0, 2)), HBM)
    cache_keys = pltpu.with_memory_space_constraint(cache_keys, HBM)
    cache_values = pltpu.with_memory_space_constraint(cache_values, HBM)

    query = call(
        query_kernel,
        sds((tokens, local_width), BF16),
        [HBM, HBM, HBM],
        [
            pltpu.VMEM((tokens, width), BF16),
            pltpu.VMEM((width,), BF16),
            pltpu.VMEM((width, local_width), BF16),
            pltpu.SemaphoreType.DMA((4,)),
        ],
        flops=2 * tokens * width * local_width,
        bytes_accessed=2 * width * (tokens + local_width),
    )(
        pltpu.with_memory_space_constraint(hidden, HBM),
        pltpu.with_memory_space_constraint(gain_attn, HBM),
        w_three,
    )

    def over_z(value, step):
        return lax.ppermute(value, "z", [(i, (i + step) % z_count) for i in range(z_count)])

    def over_core(value):
        return lax.ppermute(value, "core", [(0, 1), (1, 0)])

    steps = range(1, z_count)
    pieces = [query] + [over_z(query, step) for step in steps]
    keys, values = call(
        load_kernel,
        (sds(cache_keys.shape, BF16), sds(cache_values.shape, BF16)),
        [HBM, HBM, pl.ANY],
        [pltpu.SemaphoreType.DMA((2,))],
        bytes_accessed=4 * requests * page * width,
        vmem=16 << 20,
    )(cache_keys, cache_values, query)
    pieces[1:], keys = lax.optimization_barrier((pieces[1:], keys))
    other_pieces = [over_core(piece) for piece in pieces]

    scratch = [
        pltpu.VMEM((z_count * 2 * tree, page), F32),
        pltpu.VMEM((z_count * 2 * tree, page), BF16),
    ]
    heads = 2 * z_count
    for_other = call(
        functools.partial(page_kernel, scale, tree, False),
        sds((heads + 1, tokens, HEAD_DIM), BF16),
        [SMEM] + [VMEM] * 6,
        scratch,
        flops=2 * tokens * page * width,
        bytes_accessed=2 * requests * page * width,
        vmem=20 << 20,
    )(cache_lengths, *other_pieces, keys, values)
    from_other = over_core(for_other)
    kept, kept_lse = call(
        functools.partial(page_kernel, scale, tree, True),
        (sds((heads, tokens, HEAD_DIM), F32), sds((tokens, 128), F32)),
        [SMEM] + [VMEM] * 6 + [pl.ANY],
        scratch,
        flops=2 * tokens * page * width,
        bytes_accessed=2 * requests * page * width,
        vmem=20 << 20,
    )(cache_lengths, *pieces, keys, values, for_other)
    merged = call(
        merge_kernel,
        tuple(sds((padded, local_width), BF16) for _ in range(z_count)),
        [VMEM] * 3,
        [pltpu.VMEM((256, 128), F32)],
        bytes_accessed=1 << 20,
    )(from_other, kept, kept_lse)
    arrived = [merged[0]] + [over_z(merged[step], -step) for step in steps]

    tree_o, tree_lse = call(
        functools.partial(tree_kernel, scale),
        (sds((tokens, local_width), F32), sds((8, 256), F32)),
        [VMEM, VMEM, HBM, VMEM, VMEM, pl.ANY],
        [
            pltpu.VMEM((256, 128), F32),
            pltpu.VMEM((2, width, local_width), BF16),
            pltpu.SemaphoreType.DMA((2,)),
        ],
        flops=4 * tokens * width * local_width,
        bytes_accessed=2 * width * (tokens + 2 * local_width),
    )(hidden, gain_attn, w_three, query, parents, merged[0])
    theirs, ours = call(
        out_kernel,
        (sds((z_count * own, width), BF16), sds((z_count * own, width), F32)),
        [VMEM] * 7,
        [pltpu.VMEM((128, 256), F32), pltpu.VMEM((tokens, local_width), F32)],
        flops=2 * tokens * width * local_width,
        bytes_accessed=2 * width * (tokens + local_width),
    )(*arrived, tree_o, tree_lse, w_out)
    folded = call(
        fold_kernel,
        tuple(sds((own, width), BF16 if step else F32) for step in range(z_count)),
        [VMEM] * 2,
        bytes_accessed=1 << 20,
    )(ours, over_core(theirs))
    mixed = [folded[0]] + [over_z(folded[step], -step) for step in steps]
    block = experts * SLOTS // 2
    real = block // SLOTS * CAP
    weight_rows = width + width * w_down.shape[1] // w_gate_up.shape[2]
    place, gather, scatter, weights = call(
        table_kernel,
        (
            sds((chunks, experts * SLOTS, 2 * own), BF16),
            sds((1 + chunks, real, block), BF16),
            sds((chunks, block, 2 * real), BF16),
            sds((weight_rows, w_gate_up.shape[2]), BF16),
        ),
        [VMEM, HBM, HBM, pl.ANY],
        [pltpu.SemaphoreType.DMA((1 + width // w_gate_up.shape[2],))],
        flops=1 << 24,
        bytes_accessed=1 << 23,
        vmem=16 << 20,
    )(
        routes.T,
        pltpu.with_memory_space_constraint(w_gate_up[0], HBM),
        pltpu.with_memory_space_constraint(w_down[0], HBM),
        folded[0],
    )
    *mixed, weights = lax.optimization_barrier((*mixed, weights))
    other_weights = over_core(weights)

    residual, normed, outgoing = call(
        residual_kernel,
        (
            sds((own, width), F32),
            sds((own, width), BF16),
            sds((experts * SLOTS, packed), BF16),
        ),
        [VMEM] * 7,
        flops=1 << 27,
        bytes_accessed=1 << 22,
    )(*mixed, hidden, gain_moe, place)
    rows = lax.all_to_all(
        outgoing.reshape(experts, SLOTS, packed),
        ("req", "z"),
        split_axis=0,
        concat_axis=0,
        tiled=True,
    ).reshape(experts * SLOTS, packed)

    summed, table = call(
        expert_kernel,
        (
            sds((experts * SLOTS, packed), BF16),
            sds((chunks, 4 * own, experts * SLOTS), BF16),
        ),
        [VMEM] * 8,
        flops=12 * experts * CAP * width * w_down.shape[1],
        bytes_accessed=12 * width * w_down.shape[1],
        vmem=24 << 20,
    )(
        rows,
        weights,
        other_weights,
        gather,
        scatter,
        normed,
        w_router.T,
        routes.T,
    )
    back = lax.all_to_all(
        summed.reshape(experts, SLOTS, packed),
        ("req", "z"),
        split_axis=0,
        concat_axis=0,
        tiled=True,
    ).reshape(experts * SLOTS, packed)
    return call(
        final_kernel,
        sds((own, width), BF16),
        [VMEM] * 3,
        flops=1 << 27,
        bytes_accessed=1 << 22,
    )(back, table, residual)


def solution(mesh):
    req_count, exp_count = mesh.devices.shape
    split = Mesh(
        mesh.devices.reshape(req_count, exp_count // CORES, CORES), ("req", "z", "core")
    )
    exp = ("z", "core")
    everywhere = ("req", "z", "core")
    in_specs = (
        P("req", None),
        P(),
        P(None, None, exp),
        P(exp, None),
        P("req", exp, None),
        P("req", exp, None),
        P("req"),
        P("req", None),
        P(),
        P(),
        P(everywhere, None),
        P(everywhere, None, None),
        P(everywhere, None, None),
    )
    return jax.shard_map(
        per_device,
        mesh=split,
        in_specs=in_specs,
        out_specs=P(everywhere, None),
        check_vma=False,
    )
```

```python
import functools

import jax
import jax.numpy as jnp
from jax import lax
from jax.experimental import pallas as pl
from jax.experimental.pallas import tpu as pltpu
from jax.sharding import Mesh
from jax.sharding import PartitionSpec as P

HEAD_DIM = 128
EXP_SPLIT = 2
CORES = 2
CAP = 6
SLOTS = 8

EPSILON = 1e-05
NEGATIVE = -1e30
F32 = jnp.float32
BF16 = jnp.bfloat16
VMEM = pltpu.VMEM
SMEM = pltpu.SMEM
HBM = pltpu.HBM


def dot(a, b):
    return jnp.dot(a, b, preferred_element_type=F32)


def dot_t(a, b):
    return lax.dot_general(a, b, (((1,), (1,)), ((), ())), preferred_element_type=F32)


def iota(shape, axis):
    return lax.broadcasted_iota(jnp.int32, shape, axis)


def call(body, out, in_spaces, scratch=(), flops=0, bytes_accessed=0, vmem=10 << 20, aliases={}):
    out_spec = jax.tree.map(lambda _: pl.BlockSpec(memory_space=VMEM), out)
    return pl.pallas_call(
        body,
        out_shape=out,
        in_specs=[pl.BlockSpec(memory_space=s) for s in in_spaces],
        out_specs=out_spec,
        scratch_shapes=list(scratch),
        input_output_aliases=aliases,
        compiler_params=pltpu.CompilerParams(vmem_limit_bytes=vmem),
        cost_estimate=pl.CostEstimate(
            flops=flops, bytes_accessed=bytes_accessed, transcendentals=0
        ),
    )


def sds(shape, dtype):
    return jax.ShapeDtypeStruct(shape, dtype)


def homes(count, other):
    z, core = lax.axis_index("z"), lax.axis_index("core")
    core = 1 - core if other else core
    return [lax.rem(z + count - i, count) * CORES + core for i in range(count)]


def normed_rows(values, gain):
    inverse = lax.rsqrt(jnp.mean(values * values, axis=-1, keepdims=True) + EPSILON)
    return (values * inverse * gain).astype(BF16)


def query_kernel(x_hbm, g_hbm, w_hbm, q_ref, x_ref, g_ref, w_ref, sems):
    x_copy = pltpu.make_async_copy(x_hbm, x_ref, sems.at[0])
    w_copy = pltpu.make_async_copy(w_hbm.at[0], w_ref, sems.at[1])
    g_copy = pltpu.make_async_copy(g_hbm, g_ref, sems.at[2])
    x_copy.start()
    g_copy.start()
    w_copy.start()
    g_copy.wait()
    x_copy.wait()
    normed = normed_rows(x_ref[...].astype(F32), g_ref[...].astype(F32).reshape(1, -1))
    w_copy.wait()
    q_ref[...] = dot(normed, w_ref[...]).astype(BF16)


def load_kernel(k_hbm, v_hbm, after_ref, k_ref, v_ref, sems):
    del after_ref
    copies = [
        pltpu.make_async_copy(k_hbm, k_ref, sems.at[0]),
        pltpu.make_async_copy(v_hbm, v_ref, sems.at[1]),
    ]
    for copy in copies:
        copy.start()
    for copy in copies:
        copy.wait()


def tree_kernel(scale, x_ref, g_ref, w_hbm, q_ref, up_ref, after_ref, *refs):
    o_ref, lse_ref, turn, w_ref, sems = refs
    del after_ref
    tokens, width = q_ref.shape
    w_copies = [
        pltpu.make_async_copy(w_hbm.at[i + 1], w_ref.at[i], sems.at[i]) for i in range(2)
    ]
    for w_copy in w_copies:
        w_copy.start()
    normed = normed_rows(x_ref[...].astype(F32), g_ref[...].astype(F32).reshape(1, -1))
    w_copies[0].wait()
    keys = dot(normed, w_ref[0]).astype(BF16)
    w_copies[1].wait()
    values = dot(normed, w_ref[1]).astype(BF16)
    requests, tree = up_ref.shape
    spread = iota((tree, tokens), 0) == iota((tree, tokens), 1) % tree
    wide = dot(up_ref[...].astype(BF16), jnp.where(spread, 1.0, 0.0).astype(BF16))
    home = iota((requests, tokens), 1) // tree
    wide = jnp.where(iota((requests, tokens), 0) == home, wide + (home * tree).astype(F32), 0.0)
    parent = jnp.sum(wide, axis=0, keepdims=True)
    row = iota((tokens, tokens), 0)
    same = row == iota((tokens, tokens), 1)
    reach = jnp.where(same | (row.astype(F32) == parent), 1.0, 0.0)
    for _ in range(6):
        half = reach.astype(BF16)
        reach = jnp.minimum(dot(half, half), 1.0)
    visible = dot_t(jnp.where(same, 1.0, 0.0).astype(BF16), reach.astype(BF16)) > 0.5
    lane = iota((tokens, 128), 1)
    stats = jnp.zeros((tokens, 128), F32)
    for h in range(width // HEAD_DIM):
        cut = slice(h * HEAD_DIM, (h + 1) * HEAD_DIM)
        scores = dot_t(q_ref[:, cut], keys[:, cut]) * scale
        scores = jnp.where(visible, scores, NEGATIVE)
        high = jnp.max(scores, axis=-1, keepdims=True)
        weights = jnp.where(visible, jnp.exp(scores - high), 0.0)
        total = jnp.sum(weights, axis=-1, keepdims=True)
        o_ref[:, cut] = dot(weights.astype(BF16), values[:, cut]) / total
        stats = jnp.where(lane == h, high + jnp.log(total), stats)
    turn[0:tokens, :] = stats
    lse_ref[...] = jnp.transpose(turn[...])[0:8, :]


def page_kernel(scale, tree, kept, lengths_ref, *refs):
    pieces, (k_ref, v_ref) = refs[:4], refs[4:6]
    outs = refs[7:-2] if kept else refs[6:-2]
    s_all, p_all = refs[-2:]
    out_ref = outs[0]
    requests, page = k_ref.shape[0], k_ref.shape[1]
    width = pieces[0].shape[1]
    pair = 2 * tree
    lane = iota((tree, 128), 1)
    wide = iota((tree, width), 1) < HEAD_DIM
    owners = homes(len(pieces), not kept)
    start = (lax.axis_index("z") * CORES + lax.axis_index("core")) * page
    lives = lengths_ref[...] - start

    def columns(i):
        return pl.ds(pl.multiple_of(owners[i] * width, width), width)

    for r in range(requests):
        rows = slice(r * tree, (r + 1) * tree)
        for i, piece in enumerate(pieces):
            query = piece[rows, :]
            zero = jnp.zeros_like(query)
            both = jnp.concatenate(
                [jnp.where(wide, query, zero), jnp.where(wide, zero, query)], axis=0
            )
            s_all[r, i * pair : (i + 1) * pair, :] = dot_t(both, k_ref[r, :, columns(i)])
    for r in range(requests):
        rows = slice(r * tree, (r + 1) * tree)
        scores = s_all[r] * scale
        scores = jnp.where(iota(scores.shape, 1) < lives[:, r : r + 1], scores, NEGATIVE)
        high = jnp.max(scores, axis=-1, keepdims=True)
        weights = jnp.exp(scores - high)
        total = jnp.sum(weights, axis=-1, keepdims=True)
        p_all[r] = weights.astype(BF16)
        inverse = 1.0 / total
        lse = high + jnp.log(total)
        first = lse.astype(BF16).astype(F32)
        second = (lse - first).astype(BF16).astype(F32)
        third = lse - first - second
        stats = jnp.zeros((tree, 128), F32)
        for i in range(len(pieces)):
            summed = dot(p_all[r, i * pair : (i + 1) * pair, :], v_ref[r, :, columns(i)])
            for h in range(2):
                own = slice(i * pair + h * tree, i * pair + (h + 1) * tree)
                cut = slice(h * HEAD_DIM, (h + 1) * HEAD_DIM)
                value = summed[h * tree : (h + 1) * tree, cut] * inverse[own]
                out_ref[2 * i + h, rows, :] = value.astype(out_ref.dtype)
                if kept:
                    stats = jnp.where(lane == i * 8 + h, lse[own], stats)
                else:
                    for j, part in enumerate((first, second, third)):
                        stats = jnp.where(lane == i * 8 + 2 * j + h, part[own], stats)
        if kept:
            outs[1][rows, :] = stats
        else:
            out_ref[8, rows, :] = stats.astype(BF16)


def merge_kernel(other_ref, kept_ref, lse_ref, *refs):
    outs, turn = refs[:-1], refs[-1]
    tokens = lse_ref.shape[0]
    sent = other_ref[8].astype(F32)
    other = sent + pltpu.roll(sent, 126, 1) + pltpu.roll(sent, 124, 1)
    kept = lse_ref[...]
    high = jnp.maximum(other, kept)
    other, kept = jnp.exp(other - high), jnp.exp(kept - high)
    whole = other + kept
    inverse = 1.0 / whole
    other, kept = other * inverse, kept * inverse
    lse = jnp.where(iota(high.shape, 1) % 8 < 2, high + jnp.log(whole), 0.0)
    first = lse.astype(BF16).astype(F32)
    second = (lse - first).astype(BF16).astype(F32)
    third = lse - first - second
    turn[0:tokens, :] = first + pltpu.roll(second, 2, 1) + pltpu.roll(third, 4, 1)
    turn[tokens:, :] = jnp.zeros((turn.shape[0] - tokens, 128), F32)
    turned = jnp.transpose(turn[...])
    for i, out_ref in enumerate(outs):
        for h in range(2):
            at = i * 8 + h
            value = other[:, at : at + 1] * other_ref[2 * i + h].astype(F32)
            value = value + kept[:, at : at + 1] * kept_ref[2 * i + h]
            out_ref[0:tokens, h * HEAD_DIM : (h + 1) * HEAD_DIM] = value.astype(BF16)
        out_ref[tokens:, :] = turned[i * 8 : (i + 1) * 8, :].astype(BF16)


def out_kernel(*refs):
    parts = refs[:4]
    tree_o_ref, tree_lse_ref, w_ref, theirs_ref, ours_ref, turn, mixed = refs[4:]
    padded, width = parts[0].shape
    tokens = padded - 8
    heads = width // HEAD_DIM
    own = ours_ref.shape[0] // 4
    lses = []
    for part in parts:
        rows = part[tokens:, :].astype(F32)
        lses.append(rows[0:2] + rows[2:4] + rows[4:6])
    lses.append(tree_lse_ref[0:2, :])
    high = functools.reduce(jnp.maximum, lses)
    factors = [jnp.exp(value - high) for value in lses]
    whole = functools.reduce(lambda a, b: a + b, factors)
    for s, factor in enumerate(factors):
        turn[2 * s : 2 * s + 2, :] = factor / whole
    turned = jnp.transpose(turn[...])[0:tokens, :]
    for h in range(heads):
        cut = slice(h * HEAD_DIM, (h + 1) * HEAD_DIM)
        at = 2 * len(parts) + h
        total = turned[:, at : at + 1] * tree_o_ref[:, cut]
        for s, part in enumerate(parts):
            at = 2 * s + h
            total = total + turned[:, at : at + 1] * part[0:tokens, cut].astype(F32)
        mixed[:, cut] = total

    def rows_of(other):
        rows = [
            mixed[pl.ds(pl.multiple_of(owner * own, 8), own), :]
            for owner in homes(len(parts), other)
        ]
        return jnp.concatenate(rows, axis=0).astype(BF16)

    theirs_ref[...] = dot(rows_of(True), w_ref[...]).astype(BF16)
    ours_ref[...] = dot(rows_of(False), w_ref[...])


def fold_kernel(ours_ref, theirs_ref, *outs):
    own = outs[0].shape[0]
    for i, out_ref in enumerate(outs):
        rows = slice(i * own, (i + 1) * own)
        out_ref[...] = (ours_ref[rows, :] + theirs_ref[rows, :].astype(F32)).astype(out_ref.dtype)


def expert_of_row(rows, experts):
    return jnp.where(iota((rows, experts), 0) // SLOTS == iota((rows, experts), 1), 1.0, 0.0)


def table_kernel(routes_ref, up_hbm, down_hbm, after_ref, *refs):
    place_refs, (weights_ref, sems) = refs[:3], refs[3:]
    del after_ref
    depth, both = up_hbm.shape
    units = down_hbm.shape[0]
    copies = [pltpu.make_async_copy(up_hbm, weights_ref.at[0:depth], sems.at[0])]
    for i in range(down_hbm.shape[1] // both):
        at = depth + i * units
        copies.append(
            pltpu.make_async_copy(
                down_hbm.at[:, i * both : (i + 1) * both],
                weights_ref.at[at : at + units],
                sems.at[1 + i],
            )
        )
    for copy in copies:
        copy.start()
    place_kernel(routes_ref, *place_refs)
    for copy in copies:
        copy.wait()


def place_kernel(routes_ref, place_ref, gather_ref, scatter_ref):
    chunks = place_ref.shape[0]
    _, real, block = gather_ref.shape
    row, column = iota((real, block), 0), iota((real, block), 1)
    base, slot = row // CAP * SLOTS, row % CAP
    gather_ref[0] = jnp.where(column == base + slot, 1.0, 0.0).astype(BF16)
    for k in range(chunks):
        hit = (column == base + CAP + slot // chunks) & (slot % chunks == k)
        gather_ref[1 + k] = jnp.where(hit, 1.0, 0.0).astype(BF16)
    row, column = iota((block, 2 * real), 0), iota((block, 2 * real), 1)
    is_tail = column >= real
    column = column - jnp.where(is_tail, real, 0)
    base, slot = column // CAP * SLOTS, column % CAP
    for k in range(chunks):
        main = (row == base + slot) & jnp.logical_not(is_tail)
        tail = (row == base + CAP + slot // chunks) & (slot % chunks == k) & is_tail
        scatter_ref[k] = jnp.where(main | tail, 1.0, 0.0).astype(BF16)
    top, tokens = routes_ref.shape
    chunks, rows, _ = place_ref.shape
    experts = rows // SLOTS
    named = iota((experts, tokens), 0)
    chosen = jnp.zeros((experts, tokens), F32)
    for k in range(top):
        chosen = jnp.where(routes_ref[k : k + 1, :] == named, 1.0, chosen)
    source = iota((tokens, 2 * tokens), 0)
    target = iota((tokens, 2 * tokens), 1) % tokens
    chosen = chosen.astype(BF16)
    rank = dot(chosen, jnp.where(source < target, 1.0, 0.0).astype(BF16))
    both = dot(chosen, jnp.where(source == target, 1.0, 0.0).astype(BF16))
    rank = jnp.where(both > 0.5, rank, -1.0).astype(BF16)
    spread = dot(expert_of_row(rows, experts).astype(BF16), rank)
    slot = iota((rows, 2 * tokens), 0) % SLOTS
    is_tail = iota((rows, 2 * tokens), 1) >= tokens
    for j in range(chunks):
        wanted = jnp.where(is_tail, (slot - CAP) * chunks + j, slot)
        valid = is_tail == (slot >= CAP)
        hit = valid & (spread == wanted.astype(F32))
        place_ref[j] = jnp.where(hit, 1.0, 0.0).astype(BF16)


def residual_kernel(*refs):
    parts = refs[:4]
    x_ref, g_ref, place_ref, res_ref, normed_ref, out_ref = refs[4:]
    tokens, width = parts[0].shape
    chunks = place_ref.shape[0]
    cut = width // (chunks + 1)
    start = pl.multiple_of(homes(len(parts), False)[0] * tokens, 8)
    residual = x_ref[pl.ds(start, tokens), :].astype(F32)
    for part in parts:
        residual = residual + part[...].astype(F32)
    res_ref[...] = residual
    inverse = lax.rsqrt(jnp.mean(residual * residual, axis=-1, keepdims=True) + EPSILON)
    normed = residual * inverse * g_ref[...].astype(F32).reshape(1, -1)
    normed_ref[...] = normed.astype(BF16)
    tail = normed[:, chunks * cut :]
    for j in range(chunks):
        pair = jnp.concatenate([normed[:, j * cut : (j + 1) * cut], tail], axis=0).astype(BF16)
        out_ref[:, j * cut : (j + 1) * cut] = dot(place_ref[j], pair).astype(BF16)


def gate_kernel(normed_ref, router_ref, routes_ref, table_ref):
    top, tokens = routes_ref.shape
    experts = router_ref.shape[0]
    chunks, _, rows = table_ref.shape
    logits = dot_t(normed_ref[...], router_ref[...])
    exponent = jnp.exp(logits)
    chances = exponent / jnp.sum(exponent, axis=-1, keepdims=True)
    named = iota((experts, tokens), 0)
    chosen = jnp.zeros((experts, tokens), F32)
    for k in range(top):
        chosen = jnp.where(routes_ref[k : k + 1, :] == named, 1.0, chosen)
    same = jnp.where(iota((tokens, tokens), 0) == iota((tokens, tokens), 1), 1.0, 0.0)
    chosen = dot_t(same.astype(BF16), chosen.astype(BF16))
    picked = chances * chosen
    gates = picked / jnp.sum(picked, axis=-1, keepdims=True)
    earlier = jnp.where(iota((tokens, tokens), 0) > iota((tokens, tokens), 1), 1.0, 0.0)
    rank = dot(earlier.astype(BF16), chosen.astype(BF16))
    rank = jnp.where(chosen > 0.5, rank, -1.0).astype(BF16)
    first = gates.astype(BF16)
    second = (gates - first.astype(F32)).astype(BF16)
    home = iota((experts, rows), 0) == iota((experts, rows), 1) // SLOTS
    home = jnp.where(home, 1.0, 0.0).astype(BF16)
    rank, first, second = dot(rank, home), dot(first, home), dot(second, home)
    slot = iota((tokens, rows), 1) % SLOTS
    main = (slot < CAP) & (rank == slot.astype(F32))
    for j in range(chunks):
        tail = (slot >= CAP) & (rank == ((slot - CAP) * chunks + j).astype(F32))
        table_ref[j] = jnp.concatenate(
            [
                jnp.where(main, first, 0.0),
                jnp.where(main, second, 0.0),
                jnp.where(tail, first, 0.0),
                jnp.where(tail, second, 0.0),
            ],
            axis=0,
        ).astype(BF16)


def expert_kernel(
    x_ref,
    weights_ref,
    other_ref,
    gather_ref,
    scatter_ref,
    normed_ref,
    router_ref,
    routes_ref,
    out_ref,
    table_ref,
):
    gate_kernel(normed_ref, router_ref, routes_ref, table_ref)
    rows, packed = x_ref.shape
    width = normed_ref.shape[1]
    both = weights_ref.shape[1]
    units = both // 2
    cut = width - packed
    chunks = packed // cut
    _, real, block = gather_ref.shape
    mains, tails = [], []
    for at in range(0, rows, block):
        span = slice(at, at + block)
        mains.append(dot(gather_ref[0], x_ref[span, :]).astype(BF16))
        tail = dot(gather_ref[1], x_ref[span, 0:cut])
        for k in range(1, chunks):
            tail = tail + dot(gather_ref[1 + k], x_ref[span, k * cut : (k + 1) * cut])
        tails.append(tail.astype(BF16))
    main, tail = jnp.concatenate(mains, axis=0), jnp.concatenate(tails, axis=0)
    hidden = []
    for weights in (weights_ref, other_ref):
        parts = []
        for at in range(0, units, units // 2):
            gate_cut = slice(at, at + units // 2)
            up_cut = slice(units + at, units + at + units // 2)
            gate = dot(main, weights[0:packed, gate_cut]) + dot(tail, weights[packed:width, gate_cut])
            up = dot(main, weights[0:packed, up_cut]) + dot(tail, weights[packed:width, up_cut])
            parts.append((gate / (1.0 + jnp.exp(-gate)) * up).astype(BF16))
        hidden.append(jnp.concatenate(parts, axis=1))

    def result(k):
        at = width + k * cut // both * units
        rows, columns = slice(at, at + units), slice(k * cut % both, k * cut % both + cut)
        first = dot(hidden[0], weights_ref[rows, columns]).astype(BF16).astype(F32)
        second = dot(hidden[1], other_ref[rows, columns]).astype(BF16).astype(F32)
        return (first + second).astype(BF16)

    last = result(chunks)
    for k in range(chunks):
        columns = slice(k * cut, (k + 1) * cut)
        value = result(k)
        for i in range(rows // block):
            own = slice(i * real, (i + 1) * real)
            pair = jnp.concatenate([value[own], last[own]], axis=0)
            out_ref[i * block : (i + 1) * block, columns] = dot(scatter_ref[k], pair).astype(
                BF16
            )


def final_kernel(back_ref, table_ref, res_ref, out_ref):
    tokens, width = res_ref.shape
    chunks = table_ref.shape[0]
    cut = width // (chunks + 1)
    tail = res_ref[:, chunks * cut :]
    for j in range(chunks):
        span = slice(j * cut, (j + 1) * cut)
        sums = dot(table_ref[j], back_ref[:, span])
        main = sums[0:tokens] + sums[tokens : 2 * tokens]
        out_ref[:, span] = (res_ref[:, span] + main).astype(BF16)
        tail = tail + (sums[2 * tokens : 3 * tokens] + sums[3 * tokens :])
    out_ref[:, chunks * cut :] = tail.astype(BF16)


def per_device(
    hidden,
    gain_attn,
    w_qkv,
    w_out,
    cache_keys,
    cache_values,
    cache_lengths,
    parents,
    gain_moe,
    w_router,
    routes,
    w_gate_up,
    w_down,
):
    z_count = lax.axis_size("z")
    exp_count = z_count * CORES
    tokens, width = hidden.shape
    requests, tree = parents.shape
    page = cache_keys.shape[1]
    local_width = w_qkv.shape[2]
    scale = HEAD_DIM ** (-0.5)
    own = tokens // exp_count
    experts = w_router.shape[1]
    packed = width * CAP // SLOTS
    chunks = packed // (width - packed)
    padded = tokens + 8

    w_three = pltpu.with_memory_space_constraint(jnp.transpose(w_qkv, (1, 0, 2)), HBM)
    cache_keys = pltpu.with_memory_space_constraint(cache_keys, HBM)
    cache_values = pltpu.with_memory_space_constraint(cache_values, HBM)

    query = call(
        query_kernel,
        sds((tokens, local_width), BF16),
        [HBM, HBM, HBM],
        [
            pltpu.VMEM((tokens, width), BF16),
            pltpu.VMEM((width,), BF16),
            pltpu.VMEM((width, local_width), BF16),
            pltpu.SemaphoreType.DMA((3,)),
        ],
        flops=2 * tokens * width * local_width,
        bytes_accessed=2 * width * (tokens + local_width),
    )(
        pltpu.with_memory_space_constraint(hidden, HBM),
        pltpu.with_memory_space_constraint(gain_attn, HBM),
        w_three,
    )

    def over_z(value, step):
        return lax.ppermute(value, "z", [(i, (i + step) % z_count) for i in range(z_count)])

    def over_core(value):
        return lax.ppermute(value, "core", [(0, 1), (1, 0)])

    steps = range(1, z_count)
    pieces = [query] + [over_z(query, step) for step in steps]
    keys, values = call(
        load_kernel,
        (sds(cache_keys.shape, BF16), sds(cache_values.shape, BF16)),
        [HBM, HBM, pl.ANY],
        [pltpu.SemaphoreType.DMA((2,))],
        bytes_accessed=4 * requests * page * width,
        vmem=16 << 20,
    )(cache_keys, cache_values, query)
    pieces[0], keys = lax.optimization_barrier((pieces[0], keys))
    other_pieces = [over_core(piece) for piece in pieces]

    scratch = [
        pltpu.VMEM((requests, z_count * 2 * tree, page), F32),
        pltpu.VMEM((requests, z_count * 2 * tree, page), BF16),
    ]
    heads = 2 * z_count
    lengths = cache_lengths.reshape(1, requests)
    for_other = call(
        functools.partial(page_kernel, scale, tree, False),
        sds((heads + 1, tokens, HEAD_DIM), BF16),
        [VMEM] * 7,
        scratch,
        flops=2 * tokens * page * width,
        bytes_accessed=2 * requests * page * width,
        vmem=20 << 20,
    )(lengths, *other_pieces, keys, values)
    from_other = over_core(for_other)
    kept, kept_lse = call(
        functools.partial(page_kernel, scale, tree, True),
        (sds((heads, tokens, HEAD_DIM), F32), sds((tokens, 128), F32)),
        [VMEM] * 7 + [pl.ANY],
        scratch,
        flops=2 * tokens * page * width,
        bytes_accessed=2 * requests * page * width,
        vmem=20 << 20,
    )(lengths, *pieces, keys, values, for_other)
    merged = call(
        merge_kernel,
        tuple(sds((padded, local_width), BF16) for _ in range(z_count)),
        [VMEM] * 3,
        [pltpu.VMEM((256, 128), F32)],
        bytes_accessed=1 << 20,
    )(from_other, kept, kept_lse)
    arrived = [merged[0]] + [over_z(merged[step], -step) for step in steps]

    tree_o, tree_lse = call(
        functools.partial(tree_kernel, scale),
        (sds((tokens, local_width), F32), sds((8, 256), F32)),
        [VMEM, VMEM, HBM, VMEM, VMEM, pl.ANY],
        [
            pltpu.VMEM((256, 128), F32),
            pltpu.VMEM((2, width, local_width), BF16),
            pltpu.SemaphoreType.DMA((2,)),
        ],
        flops=4 * tokens * width * local_width,
        bytes_accessed=2 * width * (tokens + 2 * local_width),
    )(hidden, gain_attn, w_three, query, parents, merged[0])
    theirs, ours = call(
        out_kernel,
        (sds((z_count * own, width), BF16), sds((z_count * own, width), F32)),
        [VMEM] * 7,
        [pltpu.VMEM((128, 256), F32), pltpu.VMEM((tokens, local_width), F32)],
        flops=2 * tokens * width * local_width,
        bytes_accessed=2 * width * (tokens + local_width),
    )(*arrived, tree_o, tree_lse, w_out)
    folded = call(
        fold_kernel,
        tuple(sds((own, width), BF16 if step else F32) for step in range(z_count)),
        [VMEM] * 2,
        bytes_accessed=1 << 20,
    )(ours, over_core(theirs))
    mixed = [folded[0]] + [over_z(folded[step], -step) for step in steps]
    block = experts * SLOTS // 2
    real = block // SLOTS * CAP
    weight_rows = width + width * w_down.shape[1] // w_gate_up.shape[2]
    place, gather, scatter, weights = call(
        table_kernel,
        (
            sds((chunks, experts * SLOTS, 2 * own), BF16),
            sds((1 + chunks, real, block), BF16),
            sds((chunks, block, 2 * real), BF16),
            sds((weight_rows, w_gate_up.shape[2]), BF16),
        ),
        [VMEM, HBM, HBM, pl.ANY],
        [pltpu.SemaphoreType.DMA((1 + width // w_gate_up.shape[2],))],
        flops=1 << 24,
        bytes_accessed=1 << 23,
        vmem=16 << 20,
    )(
        routes.T,
        pltpu.with_memory_space_constraint(w_gate_up[0], HBM),
        pltpu.with_memory_space_constraint(w_down[0], HBM),
        folded[0],
    )
    *mixed, weights = lax.optimization_barrier((*mixed, weights))
    other_weights = over_core(weights)

    residual, normed, outgoing = call(
        residual_kernel,
        (
            sds((own, width), F32),
            sds((own, width), BF16),
            sds((experts * SLOTS, packed), BF16),
        ),
        [VMEM] * 7,
        flops=1 << 27,
        bytes_accessed=1 << 22,
    )(*mixed, hidden, gain_moe, place)
    rows = lax.all_to_all(
        outgoing.reshape(experts, SLOTS, packed),
        ("req", "z"),
        split_axis=0,
        concat_axis=0,
        tiled=True,
    ).reshape(experts * SLOTS, packed)

    summed, table = call(
        expert_kernel,
        (
            sds((experts * SLOTS, packed), BF16),
            sds((chunks, 4 * own, experts * SLOTS), BF16),
        ),
        [VMEM] * 8,
        flops=12 * experts * CAP * width * w_down.shape[1],
        bytes_accessed=12 * width * w_down.shape[1],
        vmem=24 << 20,
    )(
        rows,
        weights,
        other_weights,
        gather,
        scatter,
        normed,
        w_router.T,
        routes.T,
    )
    back = lax.all_to_all(
        summed.reshape(experts, SLOTS, packed),
        ("req", "z"),
        split_axis=0,
        concat_axis=0,
        tiled=True,
    ).reshape(experts * SLOTS, packed)
    return call(
        final_kernel,
        sds((own, width), BF16),
        [VMEM] * 3,
        flops=1 << 27,
        bytes_accessed=1 << 22,
    )(back, table, residual)


def solution(mesh):
    req_count, exp_count = mesh.devices.shape
    split = Mesh(
        mesh.devices.reshape(req_count, exp_count // CORES, CORES), ("req", "z", "core")
    )
    exp = ("z", "core")
    everywhere = ("req", "z", "core")
    in_specs = (
        P("req", None),
        P(),
        P(None, None, exp),
        P(exp, None),
        P("req", exp, None),
        P("req", exp, None),
        P("req"),
        P("req", None),
        P(),
        P(),
        P(everywhere, None),
        P(everywhere, None, None),
        P(everywhere, None, None),
    )
    return jax.shard_map(
        per_device,
        mesh=split,
        in_specs=in_specs,
        out_specs=P(everywhere, None),
        check_vma=False,
    )
```

```python
import functools

import jax
import jax.numpy as jnp
from jax import lax
from jax.experimental import pallas as pl
from jax.experimental.pallas import tpu as pltpu
from jax.sharding import Mesh
from jax.sharding import PartitionSpec as P

HEAD_DIM = 128
EXP_SPLIT = 2
CORES = 2
CAP = 6
SLOTS = 8

EPSILON = 1e-05
NEGATIVE = -1e30
F32 = jnp.float32
BF16 = jnp.bfloat16
VMEM = pltpu.VMEM
SMEM = pltpu.SMEM
HBM = pltpu.HBM


def dot(a, b):
    return jnp.dot(a, b, preferred_element_type=F32)


def dot_t(a, b):
    return lax.dot_general(a, b, (((1,), (1,)), ((), ())), preferred_element_type=F32)


def iota(shape, axis):
    return lax.broadcasted_iota(jnp.int32, shape, axis)


def call(body, out, in_spaces, scratch=(), flops=0, bytes_accessed=0, vmem=10 << 20, aliases={}):
    out_spec = jax.tree.map(lambda _: pl.BlockSpec(memory_space=VMEM), out)
    return pl.pallas_call(
        body,
        out_shape=out,
        in_specs=[pl.BlockSpec(memory_space=s) for s in in_spaces],
        out_specs=out_spec,
        scratch_shapes=list(scratch),
        input_output_aliases=aliases,
        compiler_params=pltpu.CompilerParams(vmem_limit_bytes=vmem),
        cost_estimate=pl.CostEstimate(
            flops=flops, bytes_accessed=bytes_accessed, transcendentals=0
        ),
    )


def sds(shape, dtype):
    return jax.ShapeDtypeStruct(shape, dtype)


def homes(count, other):
    z, core = lax.axis_index("z"), lax.axis_index("core")
    core = 1 - core if other else core
    return [lax.rem(z + count - i, count) * CORES + core for i in range(count)]


def normed_rows(values, gain):
    inverse = lax.rsqrt(jnp.mean(values * values, axis=-1, keepdims=True) + EPSILON)
    return (values * inverse * gain).astype(BF16)


def query_kernel(x_hbm, g_hbm, w_hbm, q_ref, x_ref, g_ref, w_ref, sems):
    half = x_ref.shape[0] // 2
    rows = [slice(0, half), slice(half, 2 * half)]
    g_copy = pltpu.make_async_copy(g_hbm, g_ref, sems.at[0])
    x_copies = [
        pltpu.make_async_copy(x_hbm.at[rows[i]], x_ref.at[rows[i]], sems.at[1 + i])
        for i in range(2)
    ]
    w_copy = pltpu.make_async_copy(w_hbm.at[0], w_ref, sems.at[3])
    g_copy.start()
    for copy in x_copies:
        copy.start()
    g_copy.wait()
    gain = g_ref[...].astype(F32).reshape(1, -1)
    x_copies[0].wait()
    w_copy.start()
    first = normed_rows(x_ref[rows[0], :].astype(F32), gain)
    x_copies[1].wait()
    second = normed_rows(x_ref[rows[1], :].astype(F32), gain)
    w_copy.wait()
    q_ref[...] = dot(jnp.concatenate([first, second], axis=0), w_ref[...]).astype(BF16)


def load_kernel(source_hbm, after_ref, target_ref, sems):
    del after_ref
    copies = [
        pltpu.make_async_copy(source_hbm.at[r], target_ref.at[r], sems.at[r])
        for r in range(source_hbm.shape[0])
    ]
    for copy in copies:
        copy.start()
    for copy in copies:
        copy.wait()


def tree_kernel(scale, x_ref, g_ref, w_hbm, q_ref, up_ref, after_ref, *refs):
    o_ref, lse_ref, turn, w_ref, sems = refs
    del after_ref
    tokens, width = q_ref.shape
    w_copies = [
        pltpu.make_async_copy(w_hbm.at[i + 1], w_ref.at[i], sems.at[i]) for i in range(2)
    ]
    for w_copy in w_copies:
        w_copy.start()
    normed = normed_rows(x_ref[...].astype(F32), g_ref[...].astype(F32).reshape(1, -1))
    w_copies[0].wait()
    keys = dot(normed, w_ref[0]).astype(BF16)
    w_copies[1].wait()
    values = dot(normed, w_ref[1]).astype(BF16)
    requests, tree = up_ref.shape
    spread = iota((tree, tokens), 0) == iota((tree, tokens), 1) % tree
    wide = dot(up_ref[...].astype(BF16), jnp.where(spread, 1.0, 0.0).astype(BF16))
    home = iota((requests, tokens), 1) // tree
    wide = jnp.where(iota((requests, tokens), 0) == home, wide + (home * tree).astype(F32), 0.0)
    parent = jnp.sum(wide, axis=0, keepdims=True)
    row = iota((tokens, tokens), 0)
    same = row == iota((tokens, tokens), 1)
    reach = jnp.where(same | (row.astype(F32) == parent), 1.0, 0.0)
    for _ in range(6):
        half = reach.astype(BF16)
        reach = jnp.minimum(dot(half, half), 1.0)
    visible = dot_t(jnp.where(same, 1.0, 0.0).astype(BF16), reach.astype(BF16)) > 0.5
    lane = iota((tokens, 128), 1)
    stats = jnp.zeros((tokens, 128), F32)
    for h in range(width // HEAD_DIM):
        cut = slice(h * HEAD_DIM, (h + 1) * HEAD_DIM)
        scores = dot_t(q_ref[:, cut], keys[:, cut]) * scale
        scores = jnp.where(visible, scores, NEGATIVE)
        high = jnp.max(scores, axis=-1, keepdims=True)
        weights = jnp.where(visible, jnp.exp(scores - high), 0.0)
        total = jnp.sum(weights, axis=-1, keepdims=True)
        o_ref[:, cut] = dot(weights.astype(BF16), values[:, cut]) / total
        stats = jnp.where(lane == h, high + jnp.log(total), stats)
    turn[0:tokens, :] = stats
    lse_ref[...] = jnp.transpose(turn[...])[0:8, :]


def page_kernel(scale, tree, kept, lengths_ref, *refs):
    pieces, (k_ref, v_ref) = refs[:4], refs[4:6]
    outs = refs[7:-2] if kept else refs[6:-2]
    s_all, p_all = refs[-2:]
    out_ref = outs[0]
    requests, page = k_ref.shape[0], k_ref.shape[1]
    width = pieces[0].shape[1]
    pair = 2 * tree
    lane = iota((tree, 128), 1)
    wide = iota((tree, width), 1) < HEAD_DIM
    owners = homes(len(pieces), not kept)
    start = (lax.axis_index("z") * CORES + lax.axis_index("core")) * page
    lives = lengths_ref[...] - start

    def columns(i):
        return pl.ds(pl.multiple_of(owners[i] * width, width), width)

    for r in range(requests):
        rows = slice(r * tree, (r + 1) * tree)
        for i, piece in enumerate(pieces):
            query = piece[rows, :]
            zero = jnp.zeros_like(query)
            both = jnp.concatenate(
                [jnp.where(wide, query, zero), jnp.where(wide, zero, query)], axis=0
            )
            s_all[r, i * pair : (i + 1) * pair, :] = dot_t(both, k_ref[r, :, columns(i)])
    for r in range(requests):
        rows = slice(r * tree, (r + 1) * tree)
        scores = s_all[r] * scale
        scores = jnp.where(iota(scores.shape, 1) < lives[:, r : r + 1], scores, NEGATIVE)
        high = jnp.max(scores, axis=-1, keepdims=True)
        weights = jnp.exp(scores - high)
        total = jnp.sum(weights, axis=-1, keepdims=True)
        p_all[r] = weights.astype(BF16)
        inverse = 1.0 / total
        lse = high + jnp.log(total)
        first = lse.astype(BF16).astype(F32)
        second = (lse - first).astype(BF16).astype(F32)
        third = lse - first - second
        stats = jnp.zeros((tree, 128), F32)
        for i in range(len(pieces)):
            summed = dot(p_all[r, i * pair : (i + 1) * pair, :], v_ref[r, :, columns(i)])
            for h in range(2):
                own = slice(i * pair + h * tree, i * pair + (h + 1) * tree)
                cut = slice(h * HEAD_DIM, (h + 1) * HEAD_DIM)
                value = summed[h * tree : (h + 1) * tree, cut] * inverse[own]
                out_ref[2 * i + h, rows, :] = value.astype(out_ref.dtype)
                if kept:
                    stats = jnp.where(lane == i * 8 + h, lse[own], stats)
                else:
                    for j, part in enumerate((first, second, third)):
                        stats = jnp.where(lane == i * 8 + 2 * j + h, part[own], stats)
        if kept:
            outs[1][rows, :] = stats
        else:
            out_ref[8, rows, :] = stats.astype(BF16)


def merge_kernel(other_ref, kept_ref, lse_ref, *refs):
    outs, turn = refs[:-1], refs[-1]
    tokens = lse_ref.shape[0]
    sent = other_ref[8].astype(F32)
    other = sent + pltpu.roll(sent, 126, 1) + pltpu.roll(sent, 124, 1)
    kept = lse_ref[...]
    high = jnp.maximum(other, kept)
    other, kept = jnp.exp(other - high), jnp.exp(kept - high)
    whole = other + kept
    inverse = 1.0 / whole
    other, kept = other * inverse, kept * inverse
    lse = jnp.where(iota(high.shape, 1) % 8 < 2, high + jnp.log(whole), 0.0)
    first = lse.astype(BF16).astype(F32)
    second = (lse - first).astype(BF16).astype(F32)
    third = lse - first - second
    turn[0:tokens, :] = first + pltpu.roll(second, 2, 1) + pltpu.roll(third, 4, 1)
    turn[tokens:, :] = jnp.zeros((turn.shape[0] - tokens, 128), F32)
    turned = jnp.transpose(turn[...])
    for i, out_ref in enumerate(outs):
        for h in range(2):
            at = i * 8 + h
            value = other[:, at : at + 1] * other_ref[2 * i + h].astype(F32)
            value = value + kept[:, at : at + 1] * kept_ref[2 * i + h]
            out_ref[0:tokens, h * HEAD_DIM : (h + 1) * HEAD_DIM] = value.astype(BF16)
        out_ref[tokens:, :] = turned[i * 8 : (i + 1) * 8, :].astype(BF16)


def out_kernel(*refs):
    parts = refs[:4]
    tree_o_ref, tree_lse_ref, w_ref, theirs_ref, ours_ref, turn, mixed = refs[4:]
    padded, width = parts[0].shape
    tokens = padded - 8
    heads = width // HEAD_DIM
    own = ours_ref.shape[0] // 4
    lses = []
    for part in parts:
        rows = part[tokens:, :].astype(F32)
        lses.append(rows[0:2] + rows[2:4] + rows[4:6])
    lses.append(tree_lse_ref[0:2, :])
    high = functools.reduce(jnp.maximum, lses)
    factors = [jnp.exp(value - high) for value in lses]
    whole = functools.reduce(lambda a, b: a + b, factors)
    for s, factor in enumerate(factors):
        turn[2 * s : 2 * s + 2, :] = factor / whole
    turned = jnp.transpose(turn[...])[0:tokens, :]
    for h in range(heads):
        cut = slice(h * HEAD_DIM, (h + 1) * HEAD_DIM)
        at = 2 * len(parts) + h
        total = turned[:, at : at + 1] * tree_o_ref[:, cut]
        for s, part in enumerate(parts):
            at = 2 * s + h
            total = total + turned[:, at : at + 1] * part[0:tokens, cut].astype(F32)
        mixed[:, cut] = total

    def rows_of(other):
        rows = [
            mixed[pl.ds(pl.multiple_of(owner * own, 8), own), :]
            for owner in homes(len(parts), other)
        ]
        return jnp.concatenate(rows, axis=0).astype(BF16)

    theirs_ref[...] = dot(rows_of(True), w_ref[...]).astype(BF16)
    ours_ref[...] = dot(rows_of(False), w_ref[...])


def fold_kernel(ours_ref, theirs_ref, *outs):
    own = outs[0].shape[0]
    for i, out_ref in enumerate(outs):
        rows = slice(i * own, (i + 1) * own)
        out_ref[...] = (ours_ref[rows, :] + theirs_ref[rows, :].astype(F32)).astype(out_ref.dtype)


def expert_of_row(rows, experts):
    return jnp.where(iota((rows, experts), 0) // SLOTS == iota((rows, experts), 1), 1.0, 0.0)


def table_kernel(routes_ref, up_hbm, down_hbm, after_ref, *refs):
    place_refs, (weights_ref, sems) = refs[:4], refs[4:]
    del after_ref
    depth, both = up_hbm.shape
    units = down_hbm.shape[0]
    copies = [pltpu.make_async_copy(up_hbm, weights_ref.at[0:depth], sems.at[0])]
    for i in range(down_hbm.shape[1] // both):
        at = depth + i * units
        copies.append(
            pltpu.make_async_copy(
                down_hbm.at[:, i * both : (i + 1) * both],
                weights_ref.at[at : at + units],
                sems.at[1 + i],
            )
        )
    for copy in copies:
        copy.start()
    place_kernel(routes_ref, *place_refs)
    for copy in copies:
        copy.wait()


def place_kernel(routes_ref, place_ref, gather_ref, compact_ref, scatter_ref):
    chunks = place_ref.shape[0]
    _, real, block = gather_ref.shape
    row, column = iota((real, block), 0), iota((real, block), 1)
    base, slot = row // CAP * SLOTS, row % CAP
    gather_ref[0] = jnp.where(column == base + slot, 1.0, 0.0).astype(BF16)
    for k in range(chunks):
        hit = (column == base + CAP + slot // chunks) & (slot % chunks == k)
        gather_ref[1 + k] = jnp.where(hit, 1.0, 0.0).astype(BF16)
    spare = SLOTS - CAP
    compact = compact_ref.shape[1]
    row, column = iota((compact, real), 0), iota((compact, real), 1)
    slot = column % CAP
    for k in range(chunks):
        hit = (column // CAP == row // spare) & (slot == row % spare * chunks + k)
        compact_ref[k] = jnp.where(hit, 1.0, 0.0).astype(BF16)
    row, column = iota((block, real + compact), 0), iota((block, real + compact), 1)
    main = (column < real) & (row == column // CAP * SLOTS + column % CAP)
    column = column - real
    tail = (column >= 0) & (row == column // spare * SLOTS + CAP + column % spare)
    scatter_ref[...] = jnp.where(main | tail, 1.0, 0.0).astype(BF16)
    top, tokens = routes_ref.shape
    chunks, rows, _ = place_ref.shape
    experts = rows // SLOTS
    named = iota((experts, tokens), 0)
    chosen = jnp.zeros((experts, tokens), F32)
    for k in range(top):
        chosen = jnp.where(routes_ref[k : k + 1, :] == named, 1.0, chosen)
    source = iota((tokens, 2 * tokens), 0)
    target = iota((tokens, 2 * tokens), 1) % tokens
    chosen = chosen.astype(BF16)
    rank = dot(chosen, jnp.where(source < target, 1.0, 0.0).astype(BF16))
    both = dot(chosen, jnp.where(source == target, 1.0, 0.0).astype(BF16))
    rank = jnp.where(both > 0.5, rank, -1.0).astype(BF16)
    spread = dot(expert_of_row(rows, experts).astype(BF16), rank)
    slot = iota((rows, 2 * tokens), 0) % SLOTS
    is_tail = iota((rows, 2 * tokens), 1) >= tokens
    for j in range(chunks):
        wanted = jnp.where(is_tail, (slot - CAP) * chunks + j, slot)
        valid = is_tail == (slot >= CAP)
        hit = valid & (spread == wanted.astype(F32))
        place_ref[j] = jnp.where(hit, 1.0, 0.0).astype(BF16)


def residual_kernel(*refs):
    parts = refs[:4]
    x_ref, g_ref, place_ref, res_ref, normed_ref, out_ref = refs[4:]
    tokens, width = parts[0].shape
    chunks = place_ref.shape[0]
    cut = width // (chunks + 1)
    start = pl.multiple_of(homes(len(parts), False)[0] * tokens, 8)
    residual = x_ref[pl.ds(start, tokens), :].astype(F32)
    for part in parts:
        residual = residual + part[...].astype(F32)
    res_ref[...] = residual
    inverse = lax.rsqrt(jnp.mean(residual * residual, axis=-1, keepdims=True) + EPSILON)
    normed = residual * inverse * g_ref[...].astype(F32).reshape(1, -1)
    normed_ref[...] = normed.astype(BF16)
    tail = normed[:, chunks * cut :]
    for j in range(chunks):
        pair = jnp.concatenate([normed[:, j * cut : (j + 1) * cut], tail], axis=0).astype(BF16)
        out_ref[:, j * cut : (j + 1) * cut] = dot(place_ref[j], pair).astype(BF16)


def gate_kernel(normed_ref, router_ref, routes_ref, table_ref):
    top, tokens = routes_ref.shape
    experts = router_ref.shape[0]
    chunks, _, rows = table_ref.shape
    logits = dot_t(normed_ref[...], router_ref[...])
    exponent = jnp.exp(logits)
    chances = exponent / jnp.sum(exponent, axis=-1, keepdims=True)
    named = iota((experts, tokens), 0)
    chosen = jnp.zeros((experts, tokens), F32)
    for k in range(top):
        chosen = jnp.where(routes_ref[k : k + 1, :] == named, 1.0, chosen)
    same = jnp.where(iota((tokens, tokens), 0) == iota((tokens, tokens), 1), 1.0, 0.0)
    chosen = dot_t(same.astype(BF16), chosen.astype(BF16))
    picked = chances * chosen
    gates = picked / jnp.sum(picked, axis=-1, keepdims=True)
    earlier = jnp.where(iota((tokens, tokens), 0) > iota((tokens, tokens), 1), 1.0, 0.0)
    rank = dot(earlier.astype(BF16), chosen.astype(BF16))
    rank = jnp.where(chosen > 0.5, rank, -1.0).astype(BF16)
    first = gates.astype(BF16)
    second = (gates - first.astype(F32)).astype(BF16)
    home = iota((experts, rows), 0) == iota((experts, rows), 1) // SLOTS
    home = jnp.where(home, 1.0, 0.0).astype(BF16)
    rank, first, second = dot(rank, home), dot(first, home), dot(second, home)
    slot = iota((tokens, rows), 1) % SLOTS
    main = (slot < CAP) & (rank == slot.astype(F32))
    for j in range(chunks):
        tail = (slot >= CAP) & (rank == ((slot - CAP) * chunks + j).astype(F32))
        table_ref[j] = jnp.concatenate(
            [
                jnp.where(main, first, 0.0),
                jnp.where(main, second, 0.0),
                jnp.where(tail, first, 0.0),
                jnp.where(tail, second, 0.0),
            ],
            axis=0,
        ).astype(BF16)


def expert_kernel(
    x_ref,
    weights_ref,
    other_ref,
    gather_ref,
    compact_ref,
    scatter_ref,
    normed_ref,
    router_ref,
    routes_ref,
    out_ref,
    table_ref,
):
    gate_kernel(normed_ref, router_ref, routes_ref, table_ref)
    rows, packed = x_ref.shape
    width = normed_ref.shape[1]
    both = weights_ref.shape[1]
    units = both // 2
    cut = width - packed
    chunks = packed // cut
    _, real, block = gather_ref.shape
    mains, tails = [], []
    for at in range(0, rows, block):
        span = slice(at, at + block)
        mains.append(dot(gather_ref[0], x_ref[span, :]).astype(BF16))
        tail = dot(gather_ref[1], x_ref[span, 0:cut])
        for k in range(1, chunks):
            tail = tail + dot(gather_ref[1 + k], x_ref[span, k * cut : (k + 1) * cut])
        tails.append(tail.astype(BF16))
    main, tail = jnp.concatenate(mains, axis=0), jnp.concatenate(tails, axis=0)
    hidden = []
    for weights in (weights_ref, other_ref):
        parts = []
        for at in range(0, units, units // 2):
            gate_cut = slice(at, at + units // 2)
            up_cut = slice(units + at, units + at + units // 2)
            gate = dot(main, weights[0:packed, gate_cut]) + dot(tail, weights[packed:width, gate_cut])
            up = dot(main, weights[0:packed, up_cut]) + dot(tail, weights[packed:width, up_cut])
            parts.append((gate / (1.0 + jnp.exp(-gate)) * up).astype(BF16))
        hidden.append(jnp.concatenate(parts, axis=1))

    def result(k):
        at = width + k * cut // both * units
        rows, columns = slice(at, at + units), slice(k * cut % both, k * cut % both + cut)
        first = dot(hidden[0], weights_ref[rows, columns]).astype(BF16).astype(F32)
        second = dot(hidden[1], other_ref[rows, columns]).astype(BF16).astype(F32)
        return (first + second).astype(BF16)

    last = result(chunks)
    for k in range(chunks):
        columns = slice(k * cut, (k + 1) * cut)
        value = result(k)
        for i in range(rows // block):
            own = slice(i * real, (i + 1) * real)
            tail = dot(compact_ref[k], last[own]).astype(BF16)
            pair = jnp.concatenate([value[own], tail], axis=0)
            out_ref[i * block : (i + 1) * block, columns] = dot(scatter_ref[...], pair).astype(
                BF16
            )


def final_kernel(back_ref, table_ref, res_ref, out_hbm, out_ref, sems):
    tokens, width = res_ref.shape
    chunks = table_ref.shape[0]
    cut = width // (chunks + 1)
    spans = [slice(j * cut, (j + 1) * cut) for j in range(chunks + 1)]
    copies = [
        pltpu.make_async_copy(out_ref.at[:, span], out_hbm.at[:, span], sems.at[j])
        for j, span in enumerate(spans)
    ]
    tail = res_ref[:, spans[-1]]
    for j in range(chunks):
        sums = dot(table_ref[j], back_ref[:, spans[j]])
        main = sums[0:tokens] + sums[tokens : 2 * tokens]
        out_ref[:, spans[j]] = (res_ref[:, spans[j]] + main).astype(BF16)
        copies[j].start()
        tail = tail + (sums[2 * tokens : 3 * tokens] + sums[3 * tokens :])
    out_ref[:, spans[-1]] = tail.astype(BF16)
    copies[-1].start()
    for copy in copies:
        copy.wait()


def per_device(
    hidden,
    gain_attn,
    w_qkv,
    w_out,
    cache_keys,
    cache_values,
    cache_lengths,
    parents,
    gain_moe,
    w_router,
    routes,
    w_gate_up,
    w_down,
):
    z_count = lax.axis_size("z")
    exp_count = z_count * CORES
    tokens, width = hidden.shape
    requests, tree = parents.shape
    page = cache_keys.shape[1]
    local_width = w_qkv.shape[2]
    scale = HEAD_DIM ** (-0.5)
    own = tokens // exp_count
    experts = w_router.shape[1]
    packed = width * CAP // SLOTS
    chunks = packed // (width - packed)
    padded = tokens + 8

    w_three = pltpu.with_memory_space_constraint(jnp.transpose(w_qkv, (1, 0, 2)), HBM)
    cache_keys = pltpu.with_memory_space_constraint(cache_keys, HBM)
    cache_values = pltpu.with_memory_space_constraint(cache_values, HBM)

    query = call(
        query_kernel,
        sds((tokens, local_width), BF16),
        [HBM, HBM, HBM],
        [
            pltpu.VMEM((tokens, width), BF16),
            pltpu.VMEM((width,), BF16),
            pltpu.VMEM((width, local_width), BF16),
            pltpu.SemaphoreType.DMA((4,)),
        ],
        flops=2 * tokens * width * local_width,
        bytes_accessed=2 * width * (tokens + local_width),
    )(
        pltpu.with_memory_space_constraint(hidden, HBM),
        pltpu.with_memory_space_constraint(gain_attn, HBM),
        w_three,
    )

    def over_z(value, step):
        return lax.ppermute(value, "z", [(i, (i + step) % z_count) for i in range(z_count)])

    def over_core(value):
        return lax.ppermute(value, "core", [(0, 1), (1, 0)])

    steps = range(1, z_count)
    pieces = [query] + [over_z(query, step) for step in steps]
    load = call(
        load_kernel,
        sds(cache_keys.shape, BF16),
        [HBM, pl.ANY],
        [pltpu.SemaphoreType.DMA((requests,))],
        bytes_accessed=2 * requests * page * width,
    )
    keys, values = load(cache_keys, query), load(cache_values, query)
    pieces[0], keys = lax.optimization_barrier((pieces[0], keys))
    other_pieces = [over_core(piece) for piece in pieces]

    scratch = [
        pltpu.VMEM((requests, z_count * 2 * tree, page), F32),
        pltpu.VMEM((requests, z_count * 2 * tree, page), BF16),
    ]
    heads = 2 * z_count
    lengths = cache_lengths.reshape(1, requests)
    for_other = call(
        functools.partial(page_kernel, scale, tree, False),
        sds((heads + 1, tokens, HEAD_DIM), BF16),
        [VMEM] * 7,
        scratch,
        flops=2 * tokens * page * width,
        bytes_accessed=2 * requests * page * width,
        vmem=20 << 20,
    )(lengths, *other_pieces, keys, values)
    from_other = over_core(for_other)
    kept, kept_lse = call(
        functools.partial(page_kernel, scale, tree, True),
        (sds((heads, tokens, HEAD_DIM), F32), sds((tokens, 128), F32)),
        [VMEM] * 7 + [pl.ANY],
        scratch,
        flops=2 * tokens * page * width,
        bytes_accessed=2 * requests * page * width,
        vmem=20 << 20,
    )(lengths, *pieces, keys, values, for_other)
    merged = call(
        merge_kernel,
        tuple(sds((padded, local_width), BF16) for _ in range(z_count)),
        [VMEM] * 3,
        [pltpu.VMEM((256, 128), F32)],
        bytes_accessed=1 << 20,
    )(from_other, kept, kept_lse)
    arrived = [merged[0]] + [over_z(merged[step], -step) for step in steps]

    tree_o, tree_lse = call(
        functools.partial(tree_kernel, scale),
        (sds((tokens, local_width), F32), sds((8, 256), F32)),
        [VMEM, VMEM, HBM, VMEM, VMEM, pl.ANY],
        [
            pltpu.VMEM((256, 128), F32),
            pltpu.VMEM((2, width, local_width), BF16),
            pltpu.SemaphoreType.DMA((2,)),
        ],
        flops=4 * tokens * width * local_width,
        bytes_accessed=2 * width * (tokens + 2 * local_width),
    )(hidden, gain_attn, w_three, query, parents, merged[0])
    theirs, ours = call(
        out_kernel,
        (sds((z_count * own, width), BF16), sds((z_count * own, width), F32)),
        [VMEM] * 7,
        [pltpu.VMEM((128, 256), F32), pltpu.VMEM((tokens, local_width), F32)],
        flops=2 * tokens * width * local_width,
        bytes_accessed=2 * width * (tokens + local_width),
    )(*arrived, tree_o, tree_lse, w_out)
    folded = call(
        fold_kernel,
        tuple(sds((own, width), BF16 if step else F32) for step in range(z_count)),
        [VMEM] * 2,
        bytes_accessed=1 << 20,
    )(ours, over_core(theirs))
    mixed = [folded[0]] + [over_z(folded[step], -step) for step in steps]
    block = experts * SLOTS // 2
    real = block // SLOTS * CAP
    weight_rows = width + width * w_down.shape[1] // w_gate_up.shape[2]
    place, gather, compact, scatter, weights = call(
        table_kernel,
        (
            sds((chunks, experts * SLOTS, 2 * own), BF16),
            sds((1 + chunks, real, block), BF16),
            sds((chunks, block - real, real), BF16),
            sds((block, block), BF16),
            sds((weight_rows, w_gate_up.shape[2]), BF16),
        ),
        [VMEM, HBM, HBM, pl.ANY],
        [pltpu.SemaphoreType.DMA((1 + width // w_gate_up.shape[2],))],
        flops=1 << 24,
        bytes_accessed=1 << 23,
        vmem=16 << 20,
    )(
        routes.T,
        pltpu.with_memory_space_constraint(w_gate_up[0], HBM),
        pltpu.with_memory_space_constraint(w_down[0], HBM),
        folded[0],
    )
    *mixed, weights = lax.optimization_barrier((*mixed, weights))
    other_weights = over_core(weights)

    residual, normed, outgoing = call(
        residual_kernel,
        (
            sds((own, width), F32),
            sds((own, width), BF16),
            sds((experts * SLOTS, packed), BF16),
        ),
        [VMEM] * 7,
        flops=1 << 27,
        bytes_accessed=1 << 22,
    )(*mixed, hidden, gain_moe, place)
    rows = lax.all_to_all(
        outgoing.reshape(experts, SLOTS, packed),
        ("req", "z"),
        split_axis=0,
        concat_axis=0,
        tiled=True,
    ).reshape(experts * SLOTS, packed)

    summed, table = call(
        expert_kernel,
        (
            sds((experts * SLOTS, packed), BF16),
            sds((chunks, 4 * own, experts * SLOTS), BF16),
        ),
        [VMEM] * 9,
        flops=12 * experts * CAP * width * w_down.shape[1],
        bytes_accessed=12 * width * w_down.shape[1],
        vmem=24 << 20,
    )(
        rows,
        weights,
        other_weights,
        gather,
        compact,
        scatter,
        normed,
        w_router.T,
        routes.T,
    )
    back = lax.all_to_all(
        summed.reshape(experts, SLOTS, packed),
        ("req", "z"),
        split_axis=0,
        concat_axis=0,
        tiled=True,
    ).reshape(experts * SLOTS, packed)
    return pl.pallas_call(
        final_kernel,
        out_shape=sds((own, width), BF16),
        in_specs=[pl.BlockSpec(memory_space=VMEM)] * 3,
        out_specs=pl.BlockSpec(memory_space=HBM),
        scratch_shapes=[
            pltpu.VMEM((own, width), BF16),
            pltpu.SemaphoreType.DMA((chunks + 1,)),
        ],
        compiler_params=pltpu.CompilerParams(vmem_limit_bytes=10 << 20),
    )(back, table, residual)


def solution(mesh):
    req_count, exp_count = mesh.devices.shape
    split = Mesh(
        mesh.devices.reshape(req_count, exp_count // CORES, CORES), ("req", "z", "core")
    )
    exp = ("z", "core")
    everywhere = ("req", "z", "core")
    in_specs = (
        P("req", None),
        P(),
        P(None, None, exp),
        P(exp, None),
        P("req", exp, None),
        P("req", exp, None),
        P("req"),
        P("req", None),
        P(),
        P(),
        P(everywhere, None),
        P(everywhere, None, None),
        P(everywhere, None, None),
    )
    return jax.shard_map(
        per_device,
        mesh=split,
        in_specs=in_specs,
        out_specs=P(everywhere, None),
        check_vma=False,
    )
```

```python
import functools

import jax
import jax.numpy as jnp
from jax import lax
from jax.experimental import pallas as pl
from jax.experimental.pallas import tpu as pltpu
from jax.sharding import Mesh
from jax.sharding import PartitionSpec as P

HEAD_DIM = 128
EXP_SPLIT = 2
CORES = 2
CAP = 6
SLOTS = 8

EPSILON = 1e-05
NEGATIVE = -1e30
F32 = jnp.float32
BF16 = jnp.bfloat16
VMEM = pltpu.VMEM
SMEM = pltpu.SMEM
HBM = pltpu.HBM


def dot(a, b):
    return jnp.dot(a, b, preferred_element_type=F32)


def dot_t(a, b):
    return lax.dot_general(a, b, (((1,), (1,)), ((), ())), preferred_element_type=F32)


def iota(shape, axis):
    return lax.broadcasted_iota(jnp.int32, shape, axis)


def call(body, out, in_spaces, scratch=(), flops=0, bytes_accessed=0, vmem=10 << 20, aliases={}):
    out_spec = jax.tree.map(lambda _: pl.BlockSpec(memory_space=VMEM), out)
    return pl.pallas_call(
        body,
        out_shape=out,
        in_specs=[pl.BlockSpec(memory_space=s) for s in in_spaces],
        out_specs=out_spec,
        scratch_shapes=list(scratch),
        input_output_aliases=aliases,
        compiler_params=pltpu.CompilerParams(vmem_limit_bytes=vmem),
        cost_estimate=pl.CostEstimate(
            flops=flops, bytes_accessed=bytes_accessed, transcendentals=0
        ),
    )


def sds(shape, dtype):
    return jax.ShapeDtypeStruct(shape, dtype)


def homes(count, other):
    z, core = lax.axis_index("z"), lax.axis_index("core")
    core = 1 - core if other else core
    return [lax.rem(z + count - i, count) * CORES + core for i in range(count)]


def normed_rows(values, gain):
    inverse = lax.rsqrt(jnp.mean(values * values, axis=-1, keepdims=True) + EPSILON)
    return (values * inverse * gain).astype(BF16)


def query_kernel(x_hbm, g_hbm, w_hbm, q_ref, normed_ref, x_ref, g_ref, w_ref, sems):
    x_copy = pltpu.make_async_copy(x_hbm, x_ref, sems.at[0])
    w_copy = pltpu.make_async_copy(w_hbm.at[0], w_ref, sems.at[1])
    g_copy = pltpu.make_async_copy(g_hbm, g_ref, sems.at[2])
    x_copy.start()
    g_copy.start()
    w_copy.start()
    g_copy.wait()
    x_copy.wait()
    gain = g_ref[...].astype(F32).reshape(1, -1)
    normed_ref[...] = normed_rows(x_ref[...].astype(F32), gain)
    w_copy.wait()
    q_ref[...] = dot(normed_ref[...], w_ref[...]).astype(BF16)


def load_kernel(
    k_hbm, v_hbm, up_hbm, after_ref, k_ref, v_ref, visible_ref, up_ref, sems
):
    del after_ref
    up_copy = pltpu.make_async_copy(up_hbm, up_ref, sems.at[2])
    up_copy.start()
    copies = [
        pltpu.make_async_copy(k_hbm, k_ref, sems.at[0]),
        pltpu.make_async_copy(v_hbm, v_ref, sems.at[1]),
    ]
    for copy in copies:
        copy.start()
    up_copy.wait()
    visible_ref[...] = ancestors(up_ref)
    for copy in copies:
        copy.wait()


def ancestors(up_ref):
    requests, tree = up_ref.shape
    tokens = requests * tree
    spread = iota((tree, tokens), 0) == iota((tree, tokens), 1) % tree
    wide = dot(up_ref[...].astype(BF16), jnp.where(spread, 1.0, 0.0).astype(BF16))
    home = iota((requests, tokens), 1) // tree
    wide = jnp.where(iota((requests, tokens), 0) == home, wide + (home * tree).astype(F32), 0.0)
    parent = jnp.sum(wide, axis=0, keepdims=True)
    row = iota((tokens, tokens), 0)
    same = row == iota((tokens, tokens), 1)
    reach = jnp.where(same | (row.astype(F32) == parent), 1.0, 0.0)
    for _ in range((tree - 1).bit_length()):
        half = reach.astype(BF16)
        reach = jnp.minimum(dot(half, half), 1.0)
    return dot_t(jnp.where(same, 1.0, 0.0).astype(BF16), reach.astype(BF16))


def tree_kernel(
    scale, normed_ref, w_ref, q_ref, visible_ref, after_ref, o_ref, lse_ref, turn
):
    del after_ref
    tokens, width = q_ref.shape
    keys = dot(normed_ref[...], w_ref[0]).astype(BF16)
    values = dot(normed_ref[...], w_ref[1]).astype(BF16)
    visible = visible_ref[...] > 0.5
    lane = iota((tokens, 128), 1)
    stats = jnp.zeros((tokens, 128), F32)
    for h in range(width // HEAD_DIM):
        cut = slice(h * HEAD_DIM, (h + 1) * HEAD_DIM)
        scores = dot_t(q_ref[:, cut], keys[:, cut]) * scale
        scores = jnp.where(visible, scores, NEGATIVE)
        high = jnp.max(scores, axis=-1, keepdims=True)
        weights = jnp.where(visible, jnp.exp(scores - high), 0.0)
        total = jnp.sum(weights, axis=-1, keepdims=True)
        o_ref[:, cut] = dot(weights.astype(BF16), values[:, cut]) / total
        stats = jnp.where(lane == h, high + jnp.log(total), stats)
    turn[0:tokens, :] = stats
    lse_ref[...] = jnp.transpose(turn[...])[0:8, :]


def page_kernel(scale, tree, kept, lengths_ref, *refs):
    pieces, (k_ref, v_ref) = refs[:4], refs[4:6]
    outs = refs[7:-2] if kept else refs[7:-3]
    s_all, p_all = refs[-2:] if kept else refs[-3:-1]
    out_ref = outs[0]
    w_copies = []
    if not kept:
        w_hbm, sems = refs[6], refs[-1]
        for i in range(2):
            w_copies.append(
                pltpu.make_async_copy(w_hbm.at[i + 1], outs[1].at[i], sems.at[i])
            )
            w_copies[i].start()
    requests, page = k_ref.shape[0], k_ref.shape[1]
    width = pieces[0].shape[1]
    pair = 2 * tree
    lane = iota((tree, 128), 1)
    wide = iota((tree, width), 1) < HEAD_DIM
    owners = homes(len(pieces), not kept)
    start = (lax.axis_index("z") * CORES + lax.axis_index("core")) * page
    lives = lengths_ref[...] - start

    def columns(i):
        return pl.ds(pl.multiple_of(owners[i] * width, width), width)

    for r in range(requests):
        rows = slice(r * tree, (r + 1) * tree)
        for i, piece in enumerate(pieces):
            query = piece[rows, :]
            zero = jnp.zeros_like(query)
            both = jnp.concatenate(
                [jnp.where(wide, query, zero), jnp.where(wide, zero, query)], axis=0
            )
            s_all[r, i * pair : (i + 1) * pair, :] = dot_t(both, k_ref[r, :, columns(i)])
    for r in range(requests):
        rows = slice(r * tree, (r + 1) * tree)
        scores = s_all[r] * scale
        scores = jnp.where(iota(scores.shape, 1) < lives[:, r : r + 1], scores, NEGATIVE)
        high = jnp.max(scores, axis=-1, keepdims=True)
        weights = jnp.exp(scores - high)
        total = jnp.sum(weights, axis=-1, keepdims=True)
        p_all[r] = weights.astype(BF16)
        inverse = 1.0 / total
        lse = high + jnp.log(total)
        first = lse.astype(BF16).astype(F32)
        second = (lse - first).astype(BF16).astype(F32)
        third = lse - first - second
        stats = jnp.zeros((tree, 128), F32)
        for i in range(len(pieces)):
            summed = dot(p_all[r, i * pair : (i + 1) * pair, :], v_ref[r, :, columns(i)])
            for h in range(2):
                own = slice(i * pair + h * tree, i * pair + (h + 1) * tree)
                cut = slice(h * HEAD_DIM, (h + 1) * HEAD_DIM)
                value = summed[h * tree : (h + 1) * tree, cut] * inverse[own]
                out_ref[2 * i + h, rows, :] = value.astype(out_ref.dtype)
                if kept:
                    stats = jnp.where(lane == i * 8 + h, lse[own], stats)
                else:
                    for j, part in enumerate((first, second, third)):
                        stats = jnp.where(lane == i * 8 + 2 * j + h, part[own], stats)
        if kept:
            outs[1][rows, :] = stats
        else:
            out_ref[8, rows, :] = stats.astype(BF16)
    for w_copy in w_copies:
        w_copy.wait()


def merge_kernel(other_ref, kept_ref, lse_ref, *refs):
    outs, turn = refs[:-1], refs[-1]
    tokens = lse_ref.shape[0]
    sent = other_ref[8].astype(F32)
    other = sent + pltpu.roll(sent, 126, 1) + pltpu.roll(sent, 124, 1)
    kept = lse_ref[...]
    high = jnp.maximum(other, kept)
    other, kept = jnp.exp(other - high), jnp.exp(kept - high)
    whole = other + kept
    inverse = 1.0 / whole
    other, kept = other * inverse, kept * inverse
    lse = jnp.where(iota(high.shape, 1) % 8 < 2, high + jnp.log(whole), 0.0)
    first = lse.astype(BF16).astype(F32)
    second = (lse - first).astype(BF16).astype(F32)
    third = lse - first - second
    turn[0:tokens, :] = first + pltpu.roll(second, 2, 1) + pltpu.roll(third, 4, 1)
    turn[tokens:, :] = jnp.zeros((turn.shape[0] - tokens, 128), F32)
    turned = jnp.transpose(turn[...])
    for i, out_ref in enumerate(outs):
        for h in range(2):
            at = i * 8 + h
            value = other[:, at : at + 1] * other_ref[2 * i + h].astype(F32)
            value = value + kept[:, at : at + 1] * kept_ref[2 * i + h]
            out_ref[0:tokens, h * HEAD_DIM : (h + 1) * HEAD_DIM] = value.astype(BF16)
        out_ref[tokens:, :] = turned[i * 8 : (i + 1) * 8, :].astype(BF16)


def out_kernel(*refs):
    parts = refs[:4]
    tree_o_ref, tree_lse_ref, w_ref, theirs_ref, ours_ref, turn, mixed = refs[4:]
    padded, width = parts[0].shape
    tokens = padded - 8
    heads = width // HEAD_DIM
    own = ours_ref.shape[0] // 4
    lses = []
    for part in parts:
        rows = part[tokens:, :].astype(F32)
        lses.append(rows[0:2] + rows[2:4] + rows[4:6])
    lses.append(tree_lse_ref[0:2, :])
    high = functools.reduce(jnp.maximum, lses)
    factors = [jnp.exp(value - high) for value in lses]
    whole = functools.reduce(lambda a, b: a + b, factors)
    for s, factor in enumerate(factors):
        turn[2 * s : 2 * s + 2, :] = factor / whole
    turned = jnp.transpose(turn[...])[0:tokens, :]
    for h in range(heads):
        cut = slice(h * HEAD_DIM, (h + 1) * HEAD_DIM)
        at = 2 * len(parts) + h
        total = turned[:, at : at + 1] * tree_o_ref[:, cut]
        for s, part in enumerate(parts):
            at = 2 * s + h
            total = total + turned[:, at : at + 1] * part[0:tokens, cut].astype(F32)
        mixed[:, cut] = total

    def rows_of(other):
        rows = [
            mixed[pl.ds(pl.multiple_of(owner * own, 8), own), :]
            for owner in homes(len(parts), other)
        ]
        return jnp.concatenate(rows, axis=0).astype(BF16)

    theirs_ref[...] = dot(rows_of(True), w_ref[...]).astype(BF16)
    ours_ref[...] = dot(rows_of(False), w_ref[...])


def fold_kernel(ours_ref, theirs_ref, *outs):
    own = outs[0].shape[0]
    for i, out_ref in enumerate(outs):
        rows = slice(i * own, (i + 1) * own)
        out_ref[...] = (ours_ref[rows, :] + theirs_ref[rows, :].astype(F32)).astype(out_ref.dtype)


def expert_of_row(rows, experts):
    return jnp.where(iota((rows, experts), 0) // SLOTS == iota((rows, experts), 1), 1.0, 0.0)


def table_kernel(routes_ref, up_hbm, down_hbm, after_ref, *refs):
    place_refs, (weights_ref, sems) = refs[:3], refs[3:]
    del after_ref
    depth, both = up_hbm.shape
    units = down_hbm.shape[0]
    copies = [pltpu.make_async_copy(up_hbm, weights_ref.at[0:depth], sems.at[0])]
    for i in range(down_hbm.shape[1] // both):
        at = depth + i * units
        copies.append(
            pltpu.make_async_copy(
                down_hbm.at[:, i * both : (i + 1) * both],
                weights_ref.at[at : at + units],
                sems.at[1 + i],
            )
        )
    for copy in copies:
        copy.start()
    place_kernel(routes_ref, *place_refs)
    for copy in copies:
        copy.wait()


def place_kernel(routes_ref, place_ref, gather_ref, scatter_ref):
    chunks = place_ref.shape[0]
    _, real, block = gather_ref.shape
    row, column = iota((real, block), 0), iota((real, block), 1)
    base, slot = row // CAP * SLOTS, row % CAP
    gather_ref[0] = jnp.where(column == base + slot, 1.0, 0.0).astype(BF16)
    for k in range(chunks):
        hit = (column == base + CAP + slot // chunks) & (slot % chunks == k)
        gather_ref[1 + k] = jnp.where(hit, 1.0, 0.0).astype(BF16)
    row, column = iota((block, 2 * real), 0), iota((block, 2 * real), 1)
    is_tail = column >= real
    column = column - jnp.where(is_tail, real, 0)
    base, slot = column // CAP * SLOTS, column % CAP
    for k in range(chunks):
        main = (row == base + slot) & jnp.logical_not(is_tail)
        tail = (row == base + CAP + slot // chunks) & (slot % chunks == k) & is_tail
        scatter_ref[k] = jnp.where(main | tail, 1.0, 0.0).astype(BF16)
    top, tokens = routes_ref.shape
    chunks, rows, _ = place_ref.shape
    experts = rows // SLOTS
    named = iota((experts, tokens), 0)
    chosen = jnp.zeros((experts, tokens), F32)
    for k in range(top):
        chosen = jnp.where(routes_ref[k : k + 1, :] == named, 1.0, chosen)
    source = iota((tokens, 2 * tokens), 0)
    target = iota((tokens, 2 * tokens), 1) % tokens
    chosen = chosen.astype(BF16)
    rank = dot(chosen, jnp.where(source < target, 1.0, 0.0).astype(BF16))
    both = dot(chosen, jnp.where(source == target, 1.0, 0.0).astype(BF16))
    rank = jnp.where(both > 0.5, rank, -1.0).astype(BF16)
    spread = dot(expert_of_row(rows, experts).astype(BF16), rank)
    slot = iota((rows, 2 * tokens), 0) % SLOTS
    is_tail = iota((rows, 2 * tokens), 1) >= tokens
    for j in range(chunks):
        wanted = jnp.where(is_tail, (slot - CAP) * chunks + j, slot)
        valid = is_tail == (slot >= CAP)
        hit = valid & (spread == wanted.astype(F32))
        place_ref[j] = jnp.where(hit, 1.0, 0.0).astype(BF16)


def residual_kernel(*refs):
    parts = refs[:4]
    x_ref, g_ref, place_ref, res_ref, normed_ref, out_ref = refs[4:]
    tokens, width = parts[0].shape
    chunks = place_ref.shape[0]
    cut = width // (chunks + 1)
    start = pl.multiple_of(homes(len(parts), False)[0] * tokens, 8)
    residual = x_ref[pl.ds(start, tokens), :].astype(F32)
    for part in parts:
        residual = residual + part[...].astype(F32)
    res_ref[...] = residual
    inverse = lax.rsqrt(jnp.mean(residual * residual, axis=-1, keepdims=True) + EPSILON)
    normed = residual * inverse * g_ref[...].astype(F32).reshape(1, -1)
    normed_ref[...] = normed.astype(BF16)
    tail = normed[:, chunks * cut :]
    for j in range(chunks):
        pair = jnp.concatenate([normed[:, j * cut : (j + 1) * cut], tail], axis=0).astype(BF16)
        out_ref[:, j * cut : (j + 1) * cut] = dot(place_ref[j], pair).astype(BF16)


def gate_kernel(normed_ref, router_ref, routes_ref, table_ref):
    top, tokens = routes_ref.shape
    experts = router_ref.shape[0]
    chunks, _, rows = table_ref.shape
    logits = dot_t(normed_ref[...], router_ref[...])
    exponent = jnp.exp(logits)
    chances = exponent / jnp.sum(exponent, axis=-1, keepdims=True)
    named = iota((experts, tokens), 0)
    chosen = jnp.zeros((experts, tokens), F32)
    for k in range(top):
        chosen = jnp.where(routes_ref[k : k + 1, :] == named, 1.0, chosen)
    same = jnp.where(iota((tokens, tokens), 0) == iota((tokens, tokens), 1), 1.0, 0.0)
    chosen = dot_t(same.astype(BF16), chosen.astype(BF16))
    picked = chances * chosen
    gates = picked / jnp.sum(picked, axis=-1, keepdims=True)
    earlier = jnp.where(iota((tokens, tokens), 0) > iota((tokens, tokens), 1), 1.0, 0.0)
    rank = dot(earlier.astype(BF16), chosen.astype(BF16))
    rank = jnp.where(chosen > 0.5, rank, -1.0).astype(BF16)
    first = gates.astype(BF16)
    second = (gates - first.astype(F32)).astype(BF16)
    home = iota((experts, rows), 0) == iota((experts, rows), 1) // SLOTS
    home = jnp.where(home, 1.0, 0.0).astype(BF16)
    rank, first, second = dot(rank, home), dot(first, home), dot(second, home)
    slot = iota((tokens, rows), 1) % SLOTS
    main = (slot < CAP) & (rank == slot.astype(F32))
    for j in range(chunks):
        tail = (slot >= CAP) & (rank == ((slot - CAP) * chunks + j).astype(F32))
        table_ref[j] = jnp.concatenate(
            [
                jnp.where(main, first, 0.0),
                jnp.where(main, second, 0.0),
                jnp.where(tail, first, 0.0),
                jnp.where(tail, second, 0.0),
            ],
            axis=0,
        ).astype(BF16)


def expert_kernel(
    x_ref,
    weights_ref,
    other_ref,
    gather_ref,
    scatter_ref,
    normed_ref,
    router_ref,
    routes_ref,
    out_ref,
    table_ref,
):
    gate_kernel(normed_ref, router_ref, routes_ref, table_ref)
    rows, packed = x_ref.shape
    width = normed_ref.shape[1]
    both = weights_ref.shape[1]
    units = both // 2
    cut = width - packed
    chunks = packed // cut
    _, real, block = gather_ref.shape
    mains, tails = [], []
    for at in range(0, rows, block):
        span = slice(at, at + block)
        mains.append(dot(gather_ref[0], x_ref[span, :]).astype(BF16))
        tail = dot(gather_ref[1], x_ref[span, 0:cut])
        for k in range(1, chunks):
            tail = tail + dot(gather_ref[1 + k], x_ref[span, k * cut : (k + 1) * cut])
        tails.append(tail.astype(BF16))
    main, tail = jnp.concatenate(mains, axis=0), jnp.concatenate(tails, axis=0)
    hidden = []
    for weights in (weights_ref, other_ref):
        parts = []
        for at in range(0, units, units // 2):
            gate_cut = slice(at, at + units // 2)
            up_cut = slice(units + at, units + at + units // 2)
            gate = dot(main, weights[0:packed, gate_cut]) + dot(tail, weights[packed:width, gate_cut])
            up = dot(main, weights[0:packed, up_cut]) + dot(tail, weights[packed:width, up_cut])
            parts.append((gate / (1.0 + jnp.exp(-gate)) * up).astype(BF16))
        hidden.append(jnp.concatenate(parts, axis=1))

    def result(k):
        at = width + k * cut // both * units
        rows, columns = slice(at, at + units), slice(k * cut % both, k * cut % both + cut)
        first = dot(hidden[0], weights_ref[rows, columns]).astype(BF16).astype(F32)
        second = dot(hidden[1], other_ref[rows, columns]).astype(BF16).astype(F32)
        return (first + second).astype(BF16)

    last = result(chunks)
    for k in range(chunks):
        columns = slice(k * cut, (k + 1) * cut)
        value = result(k)
        for i in range(rows // block):
            own = slice(i * real, (i + 1) * real)
            pair = jnp.concatenate([value[own], last[own]], axis=0)
            out_ref[i * block : (i + 1) * block, columns] = dot(scatter_ref[k], pair).astype(
                BF16
            )


def final_kernel(back_ref, table_ref, res_ref, out_ref):
    tokens, width = res_ref.shape
    chunks = table_ref.shape[0]
    cut = width // (chunks + 1)
    tail = res_ref[:, chunks * cut :]
    for j in range(chunks):
        span = slice(j * cut, (j + 1) * cut)
        sums = dot(table_ref[j], back_ref[:, span])
        main = sums[0:tokens] + sums[tokens : 2 * tokens]
        out_ref[:, span] = (res_ref[:, span] + main).astype(BF16)
        tail = tail + (sums[2 * tokens : 3 * tokens] + sums[3 * tokens :])
    out_ref[:, chunks * cut :] = tail.astype(BF16)


def per_device(
    hidden,
    gain_attn,
    w_qkv,
    w_out,
    cache_keys,
    cache_values,
    cache_lengths,
    parents,
    gain_moe,
    w_router,
    routes,
    w_gate_up,
    w_down,
):
    z_count = lax.axis_size("z")
    exp_count = z_count * CORES
    tokens, width = hidden.shape
    requests, tree = parents.shape
    page = cache_keys.shape[1]
    local_width = w_qkv.shape[2]
    scale = HEAD_DIM ** (-0.5)
    own = tokens // exp_count
    experts = w_router.shape[1]
    packed = width * CAP // SLOTS
    chunks = packed // (width - packed)
    padded = tokens + 8

    w_three = pltpu.with_memory_space_constraint(jnp.transpose(w_qkv, (1, 0, 2)), HBM)
    cache_keys = pltpu.with_memory_space_constraint(cache_keys, HBM)
    cache_values = pltpu.with_memory_space_constraint(cache_values, HBM)

    query, normed_attn = call(
        query_kernel,
        (sds((tokens, local_width), BF16), sds((tokens, width), BF16)),
        [HBM, HBM, HBM],
        [
            pltpu.VMEM((tokens, width), BF16),
            pltpu.VMEM((width,), BF16),
            pltpu.VMEM((width, local_width), BF16),
            pltpu.SemaphoreType.DMA((3,)),
        ],
        flops=2 * tokens * width * local_width,
        bytes_accessed=2 * width * (tokens + local_width),
    )(
        pltpu.with_memory_space_constraint(hidden, HBM),
        pltpu.with_memory_space_constraint(gain_attn, HBM),
        w_three,
    )

    def over_z(value, step):
        return lax.ppermute(value, "z", [(i, (i + step) % z_count) for i in range(z_count)])

    def over_core(value):
        return lax.ppermute(value, "core", [(0, 1), (1, 0)])

    steps = range(1, z_count)
    pieces = [query] + [over_z(query, step) for step in steps]
    keys, values, visible = call(
        load_kernel,
        (
            sds(cache_keys.shape, BF16),
            sds(cache_values.shape, BF16),
            sds((tokens, tokens), F32),
        ),
        [HBM, HBM, HBM, pl.ANY],
        [pltpu.VMEM(parents.shape, jnp.int32), pltpu.SemaphoreType.DMA((3,))],
        bytes_accessed=4 * requests * page * width,
        vmem=16 << 20,
    )(
        cache_keys,
        cache_values,
        pltpu.with_memory_space_constraint(parents, HBM),
        query,
    )
    pieces[0], keys = lax.optimization_barrier((pieces[0], keys))
    other_pieces = [over_core(piece) for piece in pieces]

    scratch = [
        pltpu.VMEM((requests, z_count * 2 * tree, page), F32),
        pltpu.VMEM((requests, z_count * 2 * tree, page), BF16),
    ]
    heads = 2 * z_count
    lengths = cache_lengths.reshape(1, requests)
    for_other, w_pair = call(
        functools.partial(page_kernel, scale, tree, False),
        (sds((heads + 1, tokens, HEAD_DIM), BF16), sds((2, width, local_width), BF16)),
        [VMEM] * 7 + [HBM],
        scratch + [pltpu.SemaphoreType.DMA((2,))],
        flops=2 * tokens * page * width,
        bytes_accessed=2 * requests * page * width,
        vmem=20 << 20,
    )(lengths, *other_pieces, keys, values, w_three)
    from_other = over_core(for_other)
    kept, kept_lse = call(
        functools.partial(page_kernel, scale, tree, True),
        (sds((heads, tokens, HEAD_DIM), F32), sds((tokens, 128), F32)),
        [VMEM] * 7 + [pl.ANY],
        scratch,
        flops=2 * tokens * page * width,
        bytes_accessed=2 * requests * page * width,
        vmem=20 << 20,
    )(lengths, *pieces, keys, values, for_other)
    merged = call(
        merge_kernel,
        tuple(sds((padded, local_width), BF16) for _ in range(z_count)),
        [VMEM] * 3,
        [pltpu.VMEM((256, 128), F32)],
        bytes_accessed=1 << 20,
    )(from_other, kept, kept_lse)
    arrived = [merged[0]] + [over_z(merged[step], -step) for step in steps]

    tree_o, tree_lse = call(
        functools.partial(tree_kernel, scale),
        (sds((tokens, local_width), F32), sds((8, 256), F32)),
        [VMEM] * 4 + [pl.ANY],
        [pltpu.VMEM((256, 128), F32)],
        flops=4 * tokens * width * local_width,
        bytes_accessed=2 * width * (tokens + 2 * local_width),
    )(normed_attn, w_pair, query, visible, merged[0])
    theirs, ours = call(
        out_kernel,
        (sds((z_count * own, width), BF16), sds((z_count * own, width), F32)),
        [VMEM] * 7,
        [pltpu.VMEM((128, 256), F32), pltpu.VMEM((tokens, local_width), F32)],
        flops=2 * tokens * width * local_width,
        bytes_accessed=2 * width * (tokens + local_width),
    )(*arrived, tree_o, tree_lse, w_out)
    folded = call(
        fold_kernel,
        tuple(sds((own, width), BF16 if step else F32) for step in range(z_count)),
        [VMEM] * 2,
        bytes_accessed=1 << 20,
    )(ours, over_core(theirs))
    mixed = [folded[0]] + [over_z(folded[step], -step) for step in steps]
    block = experts * SLOTS // 2
    real = block // SLOTS * CAP
    weight_rows = width + width * w_down.shape[1] // w_gate_up.shape[2]
    place, gather, scatter, weights = call(
        table_kernel,
        (
            sds((chunks, experts * SLOTS, 2 * own), BF16),
            sds((1 + chunks, real, block), BF16),
            sds((chunks, block, 2 * real), BF16),
            sds((weight_rows, w_gate_up.shape[2]), BF16),
        ),
        [VMEM, HBM, HBM, pl.ANY],
        [pltpu.SemaphoreType.DMA((1 + width // w_gate_up.shape[2],))],
        flops=1 << 24,
        bytes_accessed=1 << 23,
        vmem=16 << 20,
    )(
        routes.T,
        pltpu.with_memory_space_constraint(w_gate_up[0], HBM),
        pltpu.with_memory_space_constraint(w_down[0], HBM),
        folded[0],
    )
    *mixed, weights = lax.optimization_barrier((*mixed, weights))
    other_weights = over_core(weights)

    residual, normed, outgoing = call(
        residual_kernel,
        (
            sds((own, width), F32),
            sds((own, width), BF16),
            sds((experts * SLOTS, packed), BF16),
        ),
        [VMEM] * 7,
        flops=1 << 27,
        bytes_accessed=1 << 22,
    )(*mixed, hidden, gain_moe, place)
    rows = lax.all_to_all(
        outgoing.reshape(experts, SLOTS, packed),
        ("req", "z"),
        split_axis=0,
        concat_axis=0,
        tiled=True,
    ).reshape(experts * SLOTS, packed)

    summed, table = call(
        expert_kernel,
        (
            sds((experts * SLOTS, packed), BF16),
            sds((chunks, 4 * own, experts * SLOTS), BF16),
        ),
        [VMEM] * 8,
        flops=12 * experts * CAP * width * w_down.shape[1],
        bytes_accessed=12 * width * w_down.shape[1],
        vmem=24 << 20,
    )(
        rows,
        weights,
        other_weights,
        gather,
        scatter,
        normed,
        w_router.T,
        routes.T,
    )
    back = lax.all_to_all(
        summed.reshape(experts, SLOTS, packed),
        ("req", "z"),
        split_axis=0,
        concat_axis=0,
        tiled=True,
    ).reshape(experts * SLOTS, packed)
    return call(
        final_kernel,
        sds((own, width), BF16),
        [VMEM] * 3,
        flops=1 << 27,
        bytes_accessed=1 << 22,
    )(back, table, residual)


def solution(mesh):
    req_count, exp_count = mesh.devices.shape
    split = Mesh(
        mesh.devices.reshape(req_count, exp_count // CORES, CORES), ("req", "z", "core")
    )
    exp = ("z", "core")
    everywhere = ("req", "z", "core")
    in_specs = (
        P("req", None),
        P(),
        P(None, None, exp),
        P(exp, None),
        P("req", exp, None),
        P("req", exp, None),
        P("req"),
        P("req", None),
        P(),
        P(),
        P(everywhere, None),
        P(everywhere, None, None),
        P(everywhere, None, None),
    )
    return jax.shard_map(
        per_device,
        mesh=split,
        in_specs=in_specs,
        out_specs=P(everywhere, None),
        check_vma=False,
    )
```

```python
import functools

import jax
import jax.numpy as jnp
from jax import lax
from jax.experimental import pallas as pl
from jax.experimental.pallas import tpu as pltpu
from jax.sharding import Mesh
from jax.sharding import PartitionSpec as P

HEAD_DIM = 128
EXP_SPLIT = 2
CORES = 2
CAP = 6
SLOTS = 8

EPSILON = 1e-05
NEGATIVE = -1e30
F32 = jnp.float32
BF16 = jnp.bfloat16
VMEM = pltpu.VMEM
SMEM = pltpu.SMEM
HBM = pltpu.HBM


def dot(a, b):
    return jnp.dot(a, b, preferred_element_type=F32)


def dot_t(a, b):
    return lax.dot_general(a, b, (((1,), (1,)), ((), ())), preferred_element_type=F32)


def iota(shape, axis):
    return lax.broadcasted_iota(jnp.int32, shape, axis)


def call(body, out, in_spaces, scratch=(), flops=0, bytes_accessed=0, vmem=10 << 20, aliases={}):
    out_spec = jax.tree.map(lambda _: pl.BlockSpec(memory_space=VMEM), out)
    return pl.pallas_call(
        body,
        out_shape=out,
        in_specs=[pl.BlockSpec(memory_space=s) for s in in_spaces],
        out_specs=out_spec,
        scratch_shapes=list(scratch),
        input_output_aliases=aliases,
        compiler_params=pltpu.CompilerParams(vmem_limit_bytes=vmem),
        cost_estimate=pl.CostEstimate(
            flops=flops, bytes_accessed=bytes_accessed, transcendentals=0
        ),
    )


def sds(shape, dtype):
    return jax.ShapeDtypeStruct(shape, dtype)


def homes(count, other):
    z, core = lax.axis_index("z"), lax.axis_index("core")
    core = 1 - core if other else core
    return [lax.rem(z + count - i, count) * CORES + core for i in range(count)]


def normed_rows(values, gain):
    inverse = lax.rsqrt(jnp.mean(values * values, axis=-1, keepdims=True) + EPSILON)
    return (values * inverse * gain).astype(BF16)


def query_kernel(x_hbm, g_hbm, w_hbm, q_ref, x_ref, g_ref, w_ref, sems):
    x_copy = pltpu.make_async_copy(x_hbm, x_ref, sems.at[0])
    w_copy = pltpu.make_async_copy(w_hbm.at[0], w_ref, sems.at[1])
    g_copy = pltpu.make_async_copy(g_hbm, g_ref, sems.at[2])
    x_copy.start()
    g_copy.start()
    w_copy.start()
    g_copy.wait()
    x_copy.wait()
    normed = normed_rows(x_ref[...].astype(F32), g_ref[...].astype(F32).reshape(1, -1))
    w_copy.wait()
    q_ref[...] = dot(normed, w_ref[...]).astype(BF16)


def load_kernel(k_hbm, v_hbm, after_ref, k_ref, v_ref, sems):
    del after_ref
    copies = [
        pltpu.make_async_copy(k_hbm, k_ref, sems.at[0]),
        pltpu.make_async_copy(v_hbm, v_ref, sems.at[1]),
    ]
    for copy in copies:
        copy.start()
    for copy in copies:
        copy.wait()


def tree_kernel(scale, x_ref, g_ref, w_hbm, q_ref, up_ref, after_ref, *refs):
    o_ref, lse_ref, turn, w_ref, sems = refs
    del after_ref
    tokens, width = q_ref.shape
    w_copies = [
        pltpu.make_async_copy(w_hbm.at[i + 1], w_ref.at[i], sems.at[i]) for i in range(2)
    ]
    for w_copy in w_copies:
        w_copy.start()
    normed = normed_rows(x_ref[...].astype(F32), g_ref[...].astype(F32).reshape(1, -1))
    w_copies[0].wait()
    keys = dot(normed, w_ref[0]).astype(BF16)
    w_copies[1].wait()
    values = dot(normed, w_ref[1]).astype(BF16)
    requests, tree = up_ref.shape
    spread = iota((tree, tokens), 0) == iota((tree, tokens), 1) % tree
    wide = dot(up_ref[...].astype(BF16), jnp.where(spread, 1.0, 0.0).astype(BF16))
    home = iota((requests, tokens), 1) // tree
    wide = jnp.where(iota((requests, tokens), 0) == home, wide + (home * tree).astype(F32), 0.0)
    parent = jnp.sum(wide, axis=0, keepdims=True)
    row = iota((tokens, tokens), 0)
    same = row == iota((tokens, tokens), 1)
    reach = jnp.where(same | (row.astype(F32) == parent), 1.0, 0.0)
    for _ in range(6):
        half = reach.astype(BF16)
        reach = jnp.minimum(dot(half, half), 1.0)
    visible = dot_t(jnp.where(same, 1.0, 0.0).astype(BF16), reach.astype(BF16)) > 0.5
    lane = iota((tokens, 128), 1)
    stats = jnp.zeros((tokens, 128), F32)
    for h in range(width // HEAD_DIM):
        cut = slice(h * HEAD_DIM, (h + 1) * HEAD_DIM)
        scores = dot_t(q_ref[:, cut], keys[:, cut]) * scale
        scores = jnp.where(visible, scores, NEGATIVE)
        high = jnp.max(scores, axis=-1, keepdims=True)
        weights = jnp.where(visible, jnp.exp(scores - high), 0.0)
        total = jnp.sum(weights, axis=-1, keepdims=True)
        o_ref[:, cut] = dot(weights.astype(BF16), values[:, cut]) / total
        stats = jnp.where(lane == h, high + jnp.log(total), stats)
    turn[0:tokens, :] = stats
    lse_ref[...] = jnp.transpose(turn[...])[0:8, :]


def page_kernel(scale, tree, kept, lengths_ref, *refs):
    pieces, (k_ref, v_ref) = refs[:4], refs[4:6]
    outs = refs[7:-2] if kept else refs[6:-2]
    s_all, p_all = refs[-2:]
    out_ref = outs[0]
    requests, page = k_ref.shape[0], k_ref.shape[1]
    width = pieces[0].shape[1]
    pair = 2 * tree
    lane = iota((tree, 128), 1)
    wide = iota((tree, width), 1) < HEAD_DIM
    owners = homes(len(pieces), not kept)
    start = (lax.axis_index("z") * CORES + lax.axis_index("core")) * page
    lives = lengths_ref[...] - start

    def columns(i):
        return pl.ds(pl.multiple_of(owners[i] * width, width), width)

    for r in range(requests):
        rows = slice(r * tree, (r + 1) * tree)
        for i, piece in enumerate(pieces):
            query = piece[rows, :]
            zero = jnp.zeros_like(query)
            both = jnp.concatenate(
                [jnp.where(wide, query, zero), jnp.where(wide, zero, query)], axis=0
            )
            s_all[r, i * pair : (i + 1) * pair, :] = dot_t(both, k_ref[r, :, columns(i)])
    for r in range(requests):
        rows = slice(r * tree, (r + 1) * tree)
        scores = s_all[r] * scale
        scores = jnp.where(iota(scores.shape, 1) < lives[:, r : r + 1], scores, NEGATIVE)
        high = jnp.max(scores, axis=-1, keepdims=True)
        weights = jnp.exp(scores - high)
        total = jnp.sum(weights, axis=-1, keepdims=True)
        p_all[r] = weights.astype(BF16)
        inverse = 1.0 / total
        lse = high + jnp.log(total)
        first = lse.astype(BF16).astype(F32)
        second = (lse - first).astype(BF16).astype(F32)
        third = lse - first - second
        stats = jnp.zeros((tree, 128), F32)
        for i in range(len(pieces)):
            summed = dot(p_all[r, i * pair : (i + 1) * pair, :], v_ref[r, :, columns(i)])
            for h in range(2):
                own = slice(i * pair + h * tree, i * pair + (h + 1) * tree)
                cut = slice(h * HEAD_DIM, (h + 1) * HEAD_DIM)
                value = summed[h * tree : (h + 1) * tree, cut] * inverse[own]
                out_ref[2 * i + h, rows, :] = value.astype(out_ref.dtype)
                if kept:
                    stats = jnp.where(lane == i * 8 + h, lse[own], stats)
                else:
                    for j, part in enumerate((first, second, third)):
                        stats = jnp.where(lane == i * 8 + 2 * j + h, part[own], stats)
        if kept:
            outs[1][rows, :] = stats
        else:
            out_ref[8, rows, :] = stats.astype(BF16)


def merge_kernel(other_ref, kept_ref, lse_ref, *refs):
    outs, turn = refs[:-1], refs[-1]
    tokens = lse_ref.shape[0]
    sent = other_ref[8].astype(F32)
    other = sent + pltpu.roll(sent, 126, 1) + pltpu.roll(sent, 124, 1)
    kept = lse_ref[...]
    high = jnp.maximum(other, kept)
    other, kept = jnp.exp(other - high), jnp.exp(kept - high)
    whole = other + kept
    inverse = 1.0 / whole
    other, kept = other * inverse, kept * inverse
    lse = jnp.where(iota(high.shape, 1) % 8 < 2, high + jnp.log(whole), 0.0)
    first = lse.astype(BF16).astype(F32)
    second = (lse - first).astype(BF16).astype(F32)
    third = lse - first - second
    turn[0:tokens, :] = first + pltpu.roll(second, 2, 1) + pltpu.roll(third, 4, 1)
    turn[tokens:, :] = jnp.zeros((turn.shape[0] - tokens, 128), F32)
    turned = jnp.transpose(turn[...])
    for i, out_ref in enumerate(outs):
        for h in range(2):
            at = i * 8 + h
            value = other[:, at : at + 1] * other_ref[2 * i + h].astype(F32)
            value = value + kept[:, at : at + 1] * kept_ref[2 * i + h]
            out_ref[0:tokens, h * HEAD_DIM : (h + 1) * HEAD_DIM] = value.astype(BF16)
        out_ref[tokens:, :] = turned[i * 8 : (i + 1) * 8, :].astype(BF16)


def out_kernel(*refs):
    parts = refs[:4]
    tree_o_ref, tree_lse_ref, w_ref, theirs_ref, ours_ref, turn, mixed = refs[4:]
    padded, width = parts[0].shape
    tokens = padded - 8
    heads = width // HEAD_DIM
    own = ours_ref.shape[0] // 4
    lses = []
    for part in parts:
        rows = part[tokens:, :].astype(F32)
        lses.append(rows[0:2] + rows[2:4] + rows[4:6])
    lses.append(tree_lse_ref[0:2, :])
    high = functools.reduce(jnp.maximum, lses)
    factors = [jnp.exp(value - high) for value in lses]
    whole = functools.reduce(lambda a, b: a + b, factors)
    for s, factor in enumerate(factors):
        turn[2 * s : 2 * s + 2, :] = factor / whole
    turned = jnp.transpose(turn[...])[0:tokens, :]
    for h in range(heads):
        cut = slice(h * HEAD_DIM, (h + 1) * HEAD_DIM)
        at = 2 * len(parts) + h
        total = turned[:, at : at + 1] * tree_o_ref[:, cut]
        for s, part in enumerate(parts):
            at = 2 * s + h
            total = total + turned[:, at : at + 1] * part[0:tokens, cut].astype(F32)
        mixed[:, cut] = total

    def rows_of(other):
        rows = [
            mixed[pl.ds(pl.multiple_of(owner * own, 8), own), :]
            for owner in homes(len(parts), other)
        ]
        return jnp.concatenate(rows, axis=0).astype(BF16)

    theirs_ref[...] = dot(rows_of(True), w_ref[...]).astype(BF16)
    ours_ref[...] = dot(rows_of(False), w_ref[...])


def fold_kernel(ours_ref, theirs_ref, *outs):
    own = outs[0].shape[0]
    for i, out_ref in enumerate(outs):
        rows = slice(i * own, (i + 1) * own)
        out_ref[...] = (ours_ref[rows, :] + theirs_ref[rows, :].astype(F32)).astype(out_ref.dtype)


def expert_of_row(rows, experts):
    return jnp.where(iota((rows, experts), 0) // SLOTS == iota((rows, experts), 1), 1.0, 0.0)


def table_kernel(routes_ref, up_hbm, down_hbm, after_ref, *refs):
    place_refs, (weights_ref, sems) = refs[:3], refs[3:]
    del after_ref
    depth, both = up_hbm.shape
    units = down_hbm.shape[0]
    copies = [pltpu.make_async_copy(up_hbm, weights_ref.at[0:depth], sems.at[0])]
    for i in range(down_hbm.shape[1] // both):
        at = depth + i * units
        copies.append(
            pltpu.make_async_copy(
                down_hbm.at[:, i * both : (i + 1) * both],
                weights_ref.at[at : at + units],
                sems.at[1 + i],
            )
        )
    for copy in copies:
        copy.start()
    place_kernel(routes_ref, *place_refs)
    for copy in copies:
        copy.wait()


def place_kernel(routes_ref, place_ref, gather_ref, scatter_ref):
    chunks = place_ref.shape[0]
    _, real, block = gather_ref.shape
    row, column = iota((real, block), 0), iota((real, block), 1)
    base, slot = row // CAP * SLOTS, row % CAP
    gather_ref[0] = jnp.where(column == base + slot, 1.0, 0.0).astype(BF16)
    for k in range(chunks):
        hit = (column == base + CAP + slot // chunks) & (slot % chunks == k)
        gather_ref[1 + k] = jnp.where(hit, 1.0, 0.0).astype(BF16)
    row, column = iota((block, 2 * real), 0), iota((block, 2 * real), 1)
    is_tail = column >= real
    column = column - jnp.where(is_tail, real, 0)
    base, slot = column // CAP * SLOTS, column % CAP
    for k in range(chunks):
        main = (row == base + slot) & jnp.logical_not(is_tail)
        tail = (row == base + CAP + slot // chunks) & (slot % chunks == k) & is_tail
        scatter_ref[k] = jnp.where(main | tail, 1.0, 0.0).astype(BF16)
    top, tokens = routes_ref.shape
    chunks, rows, _ = place_ref.shape
    experts = rows // SLOTS
    named = iota((experts, tokens), 0)
    chosen = jnp.zeros((experts, tokens), F32)
    for k in range(top):
        chosen = jnp.where(routes_ref[k : k + 1, :] == named, 1.0, chosen)
    source = iota((tokens, 2 * tokens), 0)
    target = iota((tokens, 2 * tokens), 1) % tokens
    chosen = chosen.astype(BF16)
    rank = dot(chosen, jnp.where(source < target, 1.0, 0.0).astype(BF16))
    both = dot(chosen, jnp.where(source == target, 1.0, 0.0).astype(BF16))
    rank = jnp.where(both > 0.5, rank, -1.0).astype(BF16)
    spread = dot(expert_of_row(rows, experts).astype(BF16), rank)
    slot = iota((rows, 2 * tokens), 0) % SLOTS
    is_tail = iota((rows, 2 * tokens), 1) >= tokens
    for j in range(chunks):
        wanted = jnp.where(is_tail, (slot - CAP) * chunks + j, slot)
        valid = is_tail == (slot >= CAP)
        hit = valid & (spread == wanted.astype(F32))
        place_ref[j] = jnp.where(hit, 1.0, 0.0).astype(BF16)


def residual_kernel(*refs):
    parts = refs[:4]
    x_ref, g_ref, place_ref, res_ref, normed_ref, out_ref = refs[4:]
    tokens, width = parts[0].shape
    chunks = place_ref.shape[0]
    cut = width // (chunks + 1)
    start = pl.multiple_of(homes(len(parts), False)[0] * tokens, 8)
    residual = x_ref[pl.ds(start, tokens), :].astype(F32)
    for part in parts:
        residual = residual + part[...].astype(F32)
    res_ref[...] = residual
    inverse = lax.rsqrt(jnp.mean(residual * residual, axis=-1, keepdims=True) + EPSILON)
    normed = residual * inverse * g_ref[...].astype(F32).reshape(1, -1)
    normed_ref[...] = normed.astype(BF16)
    tail = normed[:, chunks * cut :]
    for j in range(chunks):
        pair = jnp.concatenate([normed[:, j * cut : (j + 1) * cut], tail], axis=0).astype(BF16)
        out_ref[:, j * cut : (j + 1) * cut] = dot(place_ref[j], pair).astype(BF16)


def gate_kernel(normed_ref, router_ref, routes_ref, table_ref):
    top, tokens = routes_ref.shape
    experts = router_ref.shape[0]
    chunks, _, rows = table_ref.shape
    logits = dot_t(normed_ref[...], router_ref[...])
    exponent = jnp.exp(logits)
    chances = exponent / jnp.sum(exponent, axis=-1, keepdims=True)
    named = iota((experts, tokens), 0)
    chosen = jnp.zeros((experts, tokens), F32)
    for k in range(top):
        chosen = jnp.where(routes_ref[k : k + 1, :] == named, 1.0, chosen)
    same = jnp.where(iota((tokens, tokens), 0) == iota((tokens, tokens), 1), 1.0, 0.0)
    chosen = dot_t(same.astype(BF16), chosen.astype(BF16))
    picked = chances * chosen
    gates = picked / jnp.sum(picked, axis=-1, keepdims=True)
    earlier = jnp.where(iota((tokens, tokens), 0) > iota((tokens, tokens), 1), 1.0, 0.0)
    rank = dot(earlier.astype(BF16), chosen.astype(BF16))
    rank = jnp.where(chosen > 0.5, rank, -1.0).astype(BF16)
    first = gates.astype(BF16)
    second = (gates - first.astype(F32)).astype(BF16)
    home = iota((experts, rows), 0) == iota((experts, rows), 1) // SLOTS
    home = jnp.where(home, 1.0, 0.0).astype(BF16)
    rank, first, second = dot(rank, home), dot(first, home), dot(second, home)
    slot = iota((tokens, rows), 1) % SLOTS
    main = (slot < CAP) & (rank == slot.astype(F32))
    for j in range(chunks):
        tail = (slot >= CAP) & (rank == ((slot - CAP) * chunks + j).astype(F32))
        table_ref[j] = jnp.concatenate(
            [
                jnp.where(main, first, 0.0),
                jnp.where(main, second, 0.0),
                jnp.where(tail, first, 0.0),
                jnp.where(tail, second, 0.0),
            ],
            axis=0,
        ).astype(BF16)


def expert_kernel(
    x_ref,
    weights_ref,
    other_ref,
    gather_ref,
    scatter_ref,
    normed_ref,
    router_ref,
    routes_ref,
    out_ref,
    table_ref,
):
    gate_kernel(normed_ref, router_ref, routes_ref, table_ref)
    rows, packed = x_ref.shape
    width = normed_ref.shape[1]
    both = weights_ref.shape[1]
    units = both // 2
    cut = width - packed
    chunks = packed // cut
    _, real, block = gather_ref.shape
    mains, tails = [], []
    for at in range(0, rows, block):
        span = slice(at, at + block)
        mains.append(dot(gather_ref[0], x_ref[span, :]).astype(BF16))
        tail = dot(gather_ref[1], x_ref[span, 0:cut])
        for k in range(1, chunks):
            tail = tail + dot(gather_ref[1 + k], x_ref[span, k * cut : (k + 1) * cut])
        tails.append(tail.astype(BF16))
    main, tail = jnp.concatenate(mains, axis=0), jnp.concatenate(tails, axis=0)
    hidden = []
    for weights in (weights_ref, other_ref):
        parts = []
        for at in range(0, units, units // 2):
            gate_cut = slice(at, at + units // 2)
            up_cut = slice(units + at, units + at + units // 2)
            gate = dot(main, weights[0:packed, gate_cut]) + dot(tail, weights[packed:width, gate_cut])
            up = dot(main, weights[0:packed, up_cut]) + dot(tail, weights[packed:width, up_cut])
            parts.append((gate / (1.0 + jnp.exp(-gate)) * up).astype(BF16))
        hidden.append(jnp.concatenate(parts, axis=1))

    def result(k):
        at = width + k * cut // both * units
        rows, columns = slice(at, at + units), slice(k * cut % both, k * cut % both + cut)
        first = dot(hidden[0], weights_ref[rows, columns]).astype(BF16).astype(F32)
        second = dot(hidden[1], other_ref[rows, columns]).astype(BF16).astype(F32)
        return (first + second).astype(BF16)

    last = result(chunks)
    for k in range(chunks):
        columns = slice(k * cut, (k + 1) * cut)
        value = result(k)
        for i in range(rows // block):
            own = slice(i * real, (i + 1) * real)
            pair = jnp.concatenate([value[own], last[own]], axis=0)
            out_ref[i * block : (i + 1) * block, columns] = dot(scatter_ref[k], pair).astype(
                BF16
            )


def final_kernel(back_ref, table_ref, res_ref, out_ref):
    tokens, width = res_ref.shape
    chunks = table_ref.shape[0]
    cut = width // (chunks + 1)
    tail = res_ref[:, chunks * cut :]
    for j in range(chunks):
        span = slice(j * cut, (j + 1) * cut)
        sums = dot(table_ref[j], back_ref[:, span])
        main = sums[0:tokens] + sums[tokens : 2 * tokens]
        out_ref[:, span] = (res_ref[:, span] + main).astype(BF16)
        tail = tail + (sums[2 * tokens : 3 * tokens] + sums[3 * tokens :])
    out_ref[:, chunks * cut :] = tail.astype(BF16)


def per_device(
    hidden,
    gain_attn,
    w_qkv,
    w_out,
    cache_keys,
    cache_values,
    cache_lengths,
    parents,
    gain_moe,
    w_router,
    routes,
    w_gate_up,
    w_down,
):
    z_count = lax.axis_size("z")
    exp_count = z_count * CORES
    tokens, width = hidden.shape
    requests, tree = parents.shape
    page = cache_keys.shape[1]
    local_width = w_qkv.shape[2]
    scale = HEAD_DIM ** (-0.5)
    own = tokens // exp_count
    experts = w_router.shape[1]
    packed = width * CAP // SLOTS
    chunks = packed // (width - packed)
    padded = tokens + 8

    w_three = pltpu.with_memory_space_constraint(jnp.transpose(w_qkv, (1, 0, 2)), HBM)
    cache_keys = pltpu.with_memory_space_constraint(cache_keys, HBM)
    cache_values = pltpu.with_memory_space_constraint(cache_values, HBM)

    query = call(
        query_kernel,
        sds((tokens, local_width), BF16),
        [HBM, HBM, HBM],
        [
            pltpu.VMEM((tokens, width), BF16),
            pltpu.VMEM((width,), BF16),
            pltpu.VMEM((width, local_width), BF16),
            pltpu.SemaphoreType.DMA((3,)),
        ],
        flops=2 * tokens * width * local_width,
        bytes_accessed=2 * width * (tokens + local_width),
    )(
        pltpu.with_memory_space_constraint(hidden, HBM),
        pltpu.with_memory_space_constraint(gain_attn, HBM),
        w_three,
    )

    def over_z(value, step):
        return lax.ppermute(value, "z", [(i, (i + step) % z_count) for i in range(z_count)])

    def over_core(value):
        return lax.ppermute(value, "core", [(0, 1), (1, 0)])

    steps = sorted(range(1, z_count), key=lambda step: -min(step, z_count - step))

    pieces = [query] + [over_z(query, step) for step in range(1, z_count)]
    keys, values = call(
        load_kernel,
        (sds(cache_keys.shape, BF16), sds(cache_values.shape, BF16)),
        [HBM, HBM, pl.ANY],
        [pltpu.SemaphoreType.DMA((2,))],
        bytes_accessed=4 * requests * page * width,
        vmem=16 << 20,
    )(cache_keys, cache_values, query)
    pieces[0], keys = lax.optimization_barrier((pieces[0], keys))
    other_pieces = [over_core(piece) for piece in pieces]

    scratch = [
        pltpu.VMEM((requests, z_count * 2 * tree, page), F32),
        pltpu.VMEM((requests, z_count * 2 * tree, page), BF16),
    ]
    heads = 2 * z_count
    lengths = cache_lengths.reshape(1, requests)
    for_other = call(
        functools.partial(page_kernel, scale, tree, False),
        sds((heads + 1, tokens, HEAD_DIM), BF16),
        [VMEM] * 7,
        scratch,
        flops=2 * tokens * page * width,
        bytes_accessed=2 * requests * page * width,
        vmem=20 << 20,
    )(lengths, *other_pieces, keys, values)
    from_other = over_core(for_other)
    kept, kept_lse = call(
        functools.partial(page_kernel, scale, tree, True),
        (sds((heads, tokens, HEAD_DIM), F32), sds((tokens, 128), F32)),
        [VMEM] * 7 + [pl.ANY],
        scratch,
        flops=2 * tokens * page * width,
        bytes_accessed=2 * requests * page * width,
        vmem=20 << 20,
    )(lengths, *pieces, keys, values, for_other)
    merged = call(
        merge_kernel,
        tuple(sds((padded, local_width), BF16) for _ in range(z_count)),
        [VMEM] * 3,
        [pltpu.VMEM((256, 128), F32)],
        bytes_accessed=1 << 20,
    )(from_other, kept, kept_lse)
    arrived = [merged[0]] + [over_z(merged[step], -step) for step in steps]

    tree_o, tree_lse = call(
        functools.partial(tree_kernel, scale),
        (sds((tokens, local_width), F32), sds((8, 256), F32)),
        [VMEM, VMEM, HBM, VMEM, VMEM, pl.ANY],
        [
            pltpu.VMEM((256, 128), F32),
            pltpu.VMEM((2, width, local_width), BF16),
            pltpu.SemaphoreType.DMA((2,)),
        ],
        flops=4 * tokens * width * local_width,
        bytes_accessed=2 * width * (tokens + 2 * local_width),
    )(hidden, gain_attn, w_three, query, parents, merged[0])
    theirs, ours = call(
        out_kernel,
        (sds((z_count * own, width), BF16), sds((z_count * own, width), F32)),
        [VMEM] * 7,
        [pltpu.VMEM((128, 256), F32), pltpu.VMEM((tokens, local_width), F32)],
        flops=2 * tokens * width * local_width,
        bytes_accessed=2 * width * (tokens + local_width),
    )(*arrived, tree_o, tree_lse, w_out)
    folded = call(
        fold_kernel,
        tuple(sds((own, width), BF16 if step else F32) for step in range(z_count)),
        [VMEM] * 2,
        bytes_accessed=1 << 20,
    )(ours, over_core(theirs))
    mixed = [folded[0]] + [over_z(folded[step], -step) for step in steps]
    block = experts * SLOTS // 2
    real = block // SLOTS * CAP
    weight_rows = width + width * w_down.shape[1] // w_gate_up.shape[2]
    place, gather, scatter, weights = call(
        table_kernel,
        (
            sds((chunks, experts * SLOTS, 2 * own), BF16),
            sds((1 + chunks, real, block), BF16),
            sds((chunks, block, 2 * real), BF16),
            sds((weight_rows, w_gate_up.shape[2]), BF16),
        ),
        [VMEM, HBM, HBM, pl.ANY],
        [pltpu.SemaphoreType.DMA((1 + width // w_gate_up.shape[2],))],
        flops=1 << 24,
        bytes_accessed=1 << 23,
        vmem=16 << 20,
    )(
        routes.T,
        pltpu.with_memory_space_constraint(w_gate_up[0], HBM),
        pltpu.with_memory_space_constraint(w_down[0], HBM),
        folded[0],
    )
    *mixed, weights = lax.optimization_barrier((*mixed, weights))
    other_weights = over_core(weights)

    residual, normed, outgoing = call(
        residual_kernel,
        (
            sds((own, width), F32),
            sds((own, width), BF16),
            sds((experts * SLOTS, packed), BF16),
        ),
        [VMEM] * 7,
        flops=1 << 27,
        bytes_accessed=1 << 22,
    )(*mixed, hidden, gain_moe, place)
    rows = lax.all_to_all(
        outgoing.reshape(experts, SLOTS, packed),
        ("req", "z"),
        split_axis=0,
        concat_axis=0,
        tiled=True,
    ).reshape(experts * SLOTS, packed)

    summed, table = call(
        expert_kernel,
        (
            sds((experts * SLOTS, packed), BF16),
            sds((chunks, 4 * own, experts * SLOTS), BF16),
        ),
        [VMEM] * 8,
        flops=12 * experts * CAP * width * w_down.shape[1],
        bytes_accessed=12 * width * w_down.shape[1],
        vmem=24 << 20,
    )(
        rows,
        weights,
        other_weights,
        gather,
        scatter,
        normed,
        w_router.T,
        routes.T,
    )
    back = lax.all_to_all(
        summed.reshape(experts, SLOTS, packed),
        ("req", "z"),
        split_axis=0,
        concat_axis=0,
        tiled=True,
    ).reshape(experts * SLOTS, packed)
    return call(
        final_kernel,
        sds((own, width), BF16),
        [VMEM] * 3,
        flops=1 << 27,
        bytes_accessed=1 << 22,
    )(back, table, residual)


def solution(mesh):
    req_count, exp_count = mesh.devices.shape
    split = Mesh(
        mesh.devices.reshape(req_count, exp_count // CORES, CORES), ("req", "z", "core")
    )
    exp = ("z", "core")
    everywhere = ("req", "z", "core")
    in_specs = (
        P("req", None),
        P(),
        P(None, None, exp),
        P(exp, None),
        P("req", exp, None),
        P("req", exp, None),
        P("req"),
        P("req", None),
        P(),
        P(),
        P(everywhere, None),
        P(everywhere, None, None),
        P(everywhere, None, None),
    )
    return jax.shard_map(
        per_device,
        mesh=split,
        in_specs=in_specs,
        out_specs=P(everywhere, None),
        check_vma=False,
    )
```

```python
import functools

import jax
import jax.numpy as jnp
from jax import lax
from jax.experimental import pallas as pl
from jax.experimental.pallas import tpu as pltpu
from jax.sharding import Mesh
from jax.sharding import PartitionSpec as P

HEAD_DIM = 128
EXP_SPLIT = 2
CORES = 2
CAP = 6
SLOTS = 8

EPSILON = 1e-05
NEGATIVE = -1e30
F32 = jnp.float32
BF16 = jnp.bfloat16
VMEM = pltpu.VMEM
SMEM = pltpu.SMEM
HBM = pltpu.HBM


def dot(a, b):
    return jnp.dot(a, b, preferred_element_type=F32)


def dot_t(a, b):
    return lax.dot_general(a, b, (((1,), (1,)), ((), ())), preferred_element_type=F32)


def iota(shape, axis):
    return lax.broadcasted_iota(jnp.int32, shape, axis)


def call(body, out, in_spaces, scratch=(), flops=0, bytes_accessed=0, vmem=10 << 20, aliases={}):
    out_spec = jax.tree.map(lambda _: pl.BlockSpec(memory_space=VMEM), out)
    return pl.pallas_call(
        body,
        out_shape=out,
        in_specs=[pl.BlockSpec(memory_space=s) for s in in_spaces],
        out_specs=out_spec,
        scratch_shapes=list(scratch),
        input_output_aliases=aliases,
        compiler_params=pltpu.CompilerParams(vmem_limit_bytes=vmem),
        cost_estimate=pl.CostEstimate(
            flops=flops, bytes_accessed=bytes_accessed, transcendentals=0
        ),
    )


def sds(shape, dtype):
    return jax.ShapeDtypeStruct(shape, dtype)


def homes(count, other, order=None):
    z, core = lax.axis_index("z"), lax.axis_index("core")
    core = 1 - core if other else core
    return [lax.rem(z + count - i, count) * CORES + core for i in order or range(count)]


def far_last(count):
    return sorted(range(count), key=lambda step: min(step, count - step))


def normed_rows(values, gain):
    inverse = lax.rsqrt(jnp.mean(values * values, axis=-1, keepdims=True) + EPSILON)
    return (values * inverse * gain).astype(BF16)


def query_kernel(x_hbm, g_hbm, w_hbm, q_ref, normed_ref, x_ref, g_ref, w_ref, sems):
    x_copy = pltpu.make_async_copy(x_hbm, x_ref, sems.at[0])
    w_copy = pltpu.make_async_copy(w_hbm.at[0], w_ref, sems.at[1])
    g_copy = pltpu.make_async_copy(g_hbm, g_ref, sems.at[2])
    x_copy.start()
    g_copy.start()
    w_copy.start()
    g_copy.wait()
    x_copy.wait()
    gain = g_ref[...].astype(F32).reshape(1, -1)
    normed_ref[...] = normed_rows(x_ref[...].astype(F32), gain)
    w_copy.wait()
    q_ref[...] = dot(normed_ref[...], w_ref[...]).astype(BF16)


def load_kernel(
    k_hbm, v_hbm, up_hbm, after_ref, k_ref, v_ref, visible_ref, up_ref, sems
):
    del after_ref
    up_copy = pltpu.make_async_copy(up_hbm, up_ref, sems.at[2])
    up_copy.start()
    copies = [
        pltpu.make_async_copy(k_hbm, k_ref, sems.at[0]),
        pltpu.make_async_copy(v_hbm, v_ref, sems.at[1]),
    ]
    for copy in copies:
        copy.start()
    up_copy.wait()
    visible_ref[...] = ancestors(up_ref)
    for copy in copies:
        copy.wait()


def ancestors(up_ref):
    requests, tree = up_ref.shape
    tokens = requests * tree
    spread = iota((tree, tokens), 0) == iota((tree, tokens), 1) % tree
    wide = dot(up_ref[...].astype(BF16), jnp.where(spread, 1.0, 0.0).astype(BF16))
    home = iota((requests, tokens), 1) // tree
    wide = jnp.where(iota((requests, tokens), 0) == home, wide + (home * tree).astype(F32), 0.0)
    parent = jnp.sum(wide, axis=0, keepdims=True)
    row = iota((tokens, tokens), 0)
    same = row == iota((tokens, tokens), 1)
    reach = jnp.where(same | (row.astype(F32) == parent), 1.0, 0.0)
    for _ in range((tree - 1).bit_length()):
        half = reach.astype(BF16)
        reach = jnp.minimum(dot(half, half), 1.0)
    return dot_t(jnp.where(same, 1.0, 0.0).astype(BF16), reach.astype(BF16))


def tree_kernel(scale, normed_ref, w_hbm, q_ref, visible_ref, after_ref, *refs):
    o_ref, lse_ref, turn, w_ref, sems = refs
    del after_ref
    tokens, width = q_ref.shape
    w_copies = [
        pltpu.make_async_copy(w_hbm.at[i + 1], w_ref.at[i], sems.at[i]) for i in range(2)
    ]
    for w_copy in w_copies:
        w_copy.start()
    w_copies[0].wait()
    keys = dot(normed_ref[...], w_ref[0]).astype(BF16)
    w_copies[1].wait()
    values = dot(normed_ref[...], w_ref[1]).astype(BF16)
    visible = visible_ref[...] > 0.5
    lane = iota((tokens, 128), 1)
    stats = jnp.zeros((tokens, 128), F32)
    for h in range(width // HEAD_DIM):
        cut = slice(h * HEAD_DIM, (h + 1) * HEAD_DIM)
        scores = dot_t(q_ref[:, cut], keys[:, cut]) * scale
        scores = jnp.where(visible, scores, NEGATIVE)
        high = jnp.max(scores, axis=-1, keepdims=True)
        weights = jnp.where(visible, jnp.exp(scores - high), 0.0)
        total = jnp.sum(weights, axis=-1, keepdims=True)
        o_ref[:, cut] = dot(weights.astype(BF16), values[:, cut]) / total
        stats = jnp.where(lane == h, high + jnp.log(total), stats)
    turn[0:tokens, :] = stats
    lse_ref[...] = jnp.transpose(turn[...])[0:8, :]


def page_kernel(scale, tree, kept, lengths_ref, *refs):
    pieces, (k_ref, v_ref) = refs[:4], refs[4:6]
    outs = refs[7:-2] if kept else refs[6:-2]
    s_all, p_all = refs[-2:]
    out_ref = outs[0]
    requests, page = k_ref.shape[0], k_ref.shape[1]
    width = pieces[0].shape[1]
    pair = 2 * tree
    lane = iota((tree, 128), 1)
    wide = iota((tree, width), 1) < HEAD_DIM
    owners = homes(len(pieces), not kept, far_last(len(pieces)))
    start = (lax.axis_index("z") * CORES + lax.axis_index("core")) * page
    lives = lengths_ref[...] - start

    def columns(i):
        return pl.ds(pl.multiple_of(owners[i] * width, width), width)

    for r in range(requests):
        rows = slice(r * tree, (r + 1) * tree)
        for i, piece in enumerate(pieces):
            query = piece[rows, :]
            zero = jnp.zeros_like(query)
            both = jnp.concatenate(
                [jnp.where(wide, query, zero), jnp.where(wide, zero, query)], axis=0
            )
            s_all[r, i * pair : (i + 1) * pair, :] = dot_t(both, k_ref[r, :, columns(i)])
    for r in range(requests):
        rows = slice(r * tree, (r + 1) * tree)
        scores = s_all[r] * scale
        scores = jnp.where(iota(scores.shape, 1) < lives[:, r : r + 1], scores, NEGATIVE)
        high = jnp.max(scores, axis=-1, keepdims=True)
        weights = jnp.exp(scores - high)
        total = jnp.sum(weights, axis=-1, keepdims=True)
        p_all[r] = weights.astype(BF16)
        inverse = 1.0 / total
        lse = high + jnp.log(total)
        first = lse.astype(BF16).astype(F32)
        second = (lse - first).astype(BF16).astype(F32)
        third = lse - first - second
        stats = jnp.zeros((tree, 128), F32)
        for i in range(len(pieces)):
            summed = dot(p_all[r, i * pair : (i + 1) * pair, :], v_ref[r, :, columns(i)])
            for h in range(2):
                own = slice(i * pair + h * tree, i * pair + (h + 1) * tree)
                cut = slice(h * HEAD_DIM, (h + 1) * HEAD_DIM)
                value = summed[h * tree : (h + 1) * tree, cut] * inverse[own]
                out_ref[2 * i + h, rows, :] = value.astype(out_ref.dtype)
                if kept:
                    stats = jnp.where(lane == i * 8 + h, lse[own], stats)
                else:
                    for j, part in enumerate((first, second, third)):
                        stats = jnp.where(lane == i * 8 + 2 * j + h, part[own], stats)
        if kept:
            outs[1][rows, :] = stats
        else:
            out_ref[8, rows, :] = stats.astype(BF16)


def merge_kernel(other_ref, kept_ref, lse_ref, *refs):
    outs, turn = refs[:-1], refs[-1]
    tokens = lse_ref.shape[0]
    sent = other_ref[8].astype(F32)
    other = sent + pltpu.roll(sent, 126, 1) + pltpu.roll(sent, 124, 1)
    kept = lse_ref[...]
    high = jnp.maximum(other, kept)
    other, kept = jnp.exp(other - high), jnp.exp(kept - high)
    whole = other + kept
    inverse = 1.0 / whole
    other, kept = other * inverse, kept * inverse
    lse = jnp.where(iota(high.shape, 1) % 8 < 2, high + jnp.log(whole), 0.0)
    first = lse.astype(BF16).astype(F32)
    second = (lse - first).astype(BF16).astype(F32)
    third = lse - first - second
    turn[0:tokens, :] = first + pltpu.roll(second, 2, 1) + pltpu.roll(third, 4, 1)
    turn[tokens:, :] = jnp.zeros((turn.shape[0] - tokens, 128), F32)
    turned = jnp.transpose(turn[...])
    for i, out_ref in enumerate(outs):
        for h in range(2):
            at = i * 8 + h
            value = other[:, at : at + 1] * other_ref[2 * i + h].astype(F32)
            value = value + kept[:, at : at + 1] * kept_ref[2 * i + h]
            out_ref[0:tokens, h * HEAD_DIM : (h + 1) * HEAD_DIM] = value.astype(BF16)
        out_ref[tokens:, :] = turned[i * 8 : (i + 1) * 8, :].astype(BF16)


def out_kernel(*refs):
    parts = refs[:4]
    tree_o_ref, tree_lse_ref, w_ref, theirs_ref, ours_ref, turn, mixed = refs[4:]
    padded, width = parts[0].shape
    tokens = padded - 8
    heads = width // HEAD_DIM
    own = ours_ref.shape[0] // 4
    lses = []
    for part in parts:
        rows = part[tokens:, :].astype(F32)
        lses.append(rows[0:2] + rows[2:4] + rows[4:6])
    lses.append(tree_lse_ref[0:2, :])
    high = functools.reduce(jnp.maximum, lses)
    factors = [jnp.exp(value - high) for value in lses]
    whole = functools.reduce(lambda a, b: a + b, factors)
    for s, factor in enumerate(factors):
        turn[2 * s : 2 * s + 2, :] = factor / whole
    turned = jnp.transpose(turn[...])[0:tokens, :]
    for h in range(heads):
        cut = slice(h * HEAD_DIM, (h + 1) * HEAD_DIM)
        at = 2 * len(parts) + h
        total = turned[:, at : at + 1] * tree_o_ref[:, cut]
        for s, part in enumerate(parts):
            at = 2 * s + h
            total = total + turned[:, at : at + 1] * part[0:tokens, cut].astype(F32)
        mixed[:, cut] = total

    def rows_of(other):
        rows = [
            mixed[pl.ds(pl.multiple_of(owner * own, 8), own), :]
            for owner in homes(len(parts), other)
        ]
        return jnp.concatenate(rows, axis=0).astype(BF16)

    theirs_ref[...] = dot(rows_of(True), w_ref[...]).astype(BF16)
    ours_ref[...] = dot(rows_of(False), w_ref[...])


def fold_kernel(ours_ref, theirs_ref, *outs):
    own = outs[0].shape[0]
    for i, out_ref in enumerate(outs):
        rows = slice(i * own, (i + 1) * own)
        out_ref[...] = (ours_ref[rows, :] + theirs_ref[rows, :].astype(F32)).astype(out_ref.dtype)


def expert_of_row(rows, experts):
    return jnp.where(iota((rows, experts), 0) // SLOTS == iota((rows, experts), 1), 1.0, 0.0)


def table_kernel(routes_ref, up_hbm, down_hbm, after_ref, *refs):
    place_refs, (weights_ref, sems) = refs[:3], refs[3:]
    del after_ref
    depth, both = up_hbm.shape
    units = down_hbm.shape[0]
    copies = [pltpu.make_async_copy(up_hbm, weights_ref.at[0:depth], sems.at[0])]
    for i in range(down_hbm.shape[1] // both):
        at = depth + i * units
        copies.append(
            pltpu.make_async_copy(
                down_hbm.at[:, i * both : (i + 1) * both],
                weights_ref.at[at : at + units],
                sems.at[1 + i],
            )
        )
    for copy in copies:
        copy.start()
    place_kernel(routes_ref, *place_refs)
    for copy in copies:
        copy.wait()


def place_kernel(routes_ref, place_ref, gather_ref, scatter_ref):
    chunks = place_ref.shape[0]
    _, real, block = gather_ref.shape
    row, column = iota((real, block), 0), iota((real, block), 1)
    base, slot = row // CAP * SLOTS, row % CAP
    gather_ref[0] = jnp.where(column == base + slot, 1.0, 0.0).astype(BF16)
    for k in range(chunks):
        hit = (column == base + CAP + slot // chunks) & (slot % chunks == k)
        gather_ref[1 + k] = jnp.where(hit, 1.0, 0.0).astype(BF16)
    row, column = iota((block, 2 * real), 0), iota((block, 2 * real), 1)
    is_tail = column >= real
    column = column - jnp.where(is_tail, real, 0)
    base, slot = column // CAP * SLOTS, column % CAP
    for k in range(chunks):
        main = (row == base + slot) & jnp.logical_not(is_tail)
        tail = (row == base + CAP + slot // chunks) & (slot % chunks == k) & is_tail
        scatter_ref[k] = jnp.where(main | tail, 1.0, 0.0).astype(BF16)
    top, tokens = routes_ref.shape
    chunks, rows, _ = place_ref.shape
    experts = rows // SLOTS
    named = iota((experts, tokens), 0)
    chosen = jnp.zeros((experts, tokens), F32)
    for k in range(top):
        chosen = jnp.where(routes_ref[k : k + 1, :] == named, 1.0, chosen)
    source = iota((tokens, 2 * tokens), 0)
    target = iota((tokens, 2 * tokens), 1) % tokens
    chosen = chosen.astype(BF16)
    rank = dot(chosen, jnp.where(source < target, 1.0, 0.0).astype(BF16))
    both = dot(chosen, jnp.where(source == target, 1.0, 0.0).astype(BF16))
    rank = jnp.where(both > 0.5, rank, -1.0).astype(BF16)
    spread = dot(expert_of_row(rows, experts).astype(BF16), rank)
    slot = iota((rows, 2 * tokens), 0) % SLOTS
    is_tail = iota((rows, 2 * tokens), 1) >= tokens
    for j in range(chunks):
        wanted = jnp.where(is_tail, (slot - CAP) * chunks + j, slot)
        valid = is_tail == (slot >= CAP)
        hit = valid & (spread == wanted.astype(F32))
        place_ref[j] = jnp.where(hit, 1.0, 0.0).astype(BF16)


def residual_kernel(*refs):
    parts = refs[:4]
    x_ref, g_ref, place_ref, res_ref, normed_ref, out_ref = refs[4:]
    tokens, width = parts[0].shape
    chunks = place_ref.shape[0]
    cut = width // (chunks + 1)
    start = pl.multiple_of(homes(len(parts), False)[0] * tokens, 8)
    residual = x_ref[pl.ds(start, tokens), :].astype(F32)
    for part in parts:
        residual = residual + part[...].astype(F32)
    res_ref[...] = residual
    inverse = lax.rsqrt(jnp.mean(residual * residual, axis=-1, keepdims=True) + EPSILON)
    normed = residual * inverse * g_ref[...].astype(F32).reshape(1, -1)
    normed_ref[...] = normed.astype(BF16)
    tail = normed[:, chunks * cut :]
    for j in range(chunks):
        pair = jnp.concatenate([normed[:, j * cut : (j + 1) * cut], tail], axis=0).astype(BF16)
        out_ref[:, j * cut : (j + 1) * cut] = dot(place_ref[j], pair).astype(BF16)


def gate_kernel(normed_ref, router_ref, routes_ref, table_ref):
    top, tokens = routes_ref.shape
    experts = router_ref.shape[0]
    chunks, _, rows = table_ref.shape
    logits = dot_t(normed_ref[...], router_ref[...])
    exponent = jnp.exp(logits)
    chances = exponent / jnp.sum(exponent, axis=-1, keepdims=True)
    named = iota((experts, tokens), 0)
    chosen = jnp.zeros((experts, tokens), F32)
    for k in range(top):
        chosen = jnp.where(routes_ref[k : k + 1, :] == named, 1.0, chosen)
    same = jnp.where(iota((tokens, tokens), 0) == iota((tokens, tokens), 1), 1.0, 0.0)
    chosen = dot_t(same.astype(BF16), chosen.astype(BF16))
    picked = chances * chosen
    gates = picked / jnp.sum(picked, axis=-1, keepdims=True)
    earlier = jnp.where(iota((tokens, tokens), 0) > iota((tokens, tokens), 1), 1.0, 0.0)
    rank = dot(earlier.astype(BF16), chosen.astype(BF16))
    rank = jnp.where(chosen > 0.5, rank, -1.0).astype(BF16)
    first = gates.astype(BF16)
    second = (gates - first.astype(F32)).astype(BF16)
    home = iota((experts, rows), 0) == iota((experts, rows), 1) // SLOTS
    home = jnp.where(home, 1.0, 0.0).astype(BF16)
    rank, first, second = dot(rank, home), dot(first, home), dot(second, home)
    slot = iota((tokens, rows), 1) % SLOTS
    main = (slot < CAP) & (rank == slot.astype(F32))
    for j in range(chunks):
        tail = (slot >= CAP) & (rank == ((slot - CAP) * chunks + j).astype(F32))
        table_ref[j] = jnp.concatenate(
            [
                jnp.where(main, first, 0.0),
                jnp.where(main, second, 0.0),
                jnp.where(tail, first, 0.0),
                jnp.where(tail, second, 0.0),
            ],
            axis=0,
        ).astype(BF16)


def expert_kernel(
    x_ref,
    weights_ref,
    other_ref,
    gather_ref,
    scatter_ref,
    normed_ref,
    router_ref,
    routes_ref,
    out_ref,
    table_ref,
):
    gate_kernel(normed_ref, router_ref, routes_ref, table_ref)
    rows, packed = x_ref.shape
    width = normed_ref.shape[1]
    both = weights_ref.shape[1]
    units = both // 2
    cut = width - packed
    chunks = packed // cut
    _, real, block = gather_ref.shape
    mains, tails = [], []
    for at in range(0, rows, block):
        span = slice(at, at + block)
        mains.append(dot(gather_ref[0], x_ref[span, :]).astype(BF16))
        tail = dot(gather_ref[1], x_ref[span, 0:cut])
        for k in range(1, chunks):
            tail = tail + dot(gather_ref[1 + k], x_ref[span, k * cut : (k + 1) * cut])
        tails.append(tail.astype(BF16))
    main, tail = jnp.concatenate(mains, axis=0), jnp.concatenate(tails, axis=0)
    hidden = []
    for weights in (weights_ref, other_ref):
        parts = []
        for at in range(0, units, units // 2):
            gate_cut = slice(at, at + units // 2)
            up_cut = slice(units + at, units + at + units // 2)
            gate = dot(main, weights[0:packed, gate_cut]) + dot(tail, weights[packed:width, gate_cut])
            up = dot(main, weights[0:packed, up_cut]) + dot(tail, weights[packed:width, up_cut])
            parts.append((gate / (1.0 + jnp.exp(-gate)) * up).astype(BF16))
        hidden.append(jnp.concatenate(parts, axis=1))

    def result(k):
        at = width + k * cut // both * units
        rows, columns = slice(at, at + units), slice(k * cut % both, k * cut % both + cut)
        first = dot(hidden[0], weights_ref[rows, columns]).astype(BF16).astype(F32)
        second = dot(hidden[1], other_ref[rows, columns]).astype(BF16).astype(F32)
        return (first + second).astype(BF16)

    last = result(chunks)
    for k in range(chunks):
        columns = slice(k * cut, (k + 1) * cut)
        value = result(k)
        for i in range(rows // block):
            own = slice(i * real, (i + 1) * real)
            pair = jnp.concatenate([value[own], last[own]], axis=0)
            out_ref[i * block : (i + 1) * block, columns] = dot(scatter_ref[k], pair).astype(
                BF16
            )


def final_kernel(back_ref, table_ref, res_ref, out_ref):
    tokens, width = res_ref.shape
    chunks = table_ref.shape[0]
    cut = width // (chunks + 1)
    tail = res_ref[:, chunks * cut :]
    for j in range(chunks):
        span = slice(j * cut, (j + 1) * cut)
        sums = dot(table_ref[j], back_ref[:, span])
        main = sums[0:tokens] + sums[tokens : 2 * tokens]
        out_ref[:, span] = (res_ref[:, span] + main).astype(BF16)
        tail = tail + (sums[2 * tokens : 3 * tokens] + sums[3 * tokens :])
    out_ref[:, chunks * cut :] = tail.astype(BF16)


def per_device(
    hidden,
    gain_attn,
    w_qkv,
    w_out,
    cache_keys,
    cache_values,
    cache_lengths,
    parents,
    gain_moe,
    w_router,
    routes,
    w_gate_up,
    w_down,
):
    z_count = lax.axis_size("z")
    exp_count = z_count * CORES
    tokens, width = hidden.shape
    requests, tree = parents.shape
    page = cache_keys.shape[1]
    local_width = w_qkv.shape[2]
    scale = HEAD_DIM ** (-0.5)
    own = tokens // exp_count
    experts = w_router.shape[1]
    packed = width * CAP // SLOTS
    chunks = packed // (width - packed)
    padded = tokens + 8

    w_three = pltpu.with_memory_space_constraint(jnp.transpose(w_qkv, (1, 0, 2)), HBM)
    cache_keys = pltpu.with_memory_space_constraint(cache_keys, HBM)
    cache_values = pltpu.with_memory_space_constraint(cache_values, HBM)

    query, normed_attn = call(
        query_kernel,
        (sds((tokens, local_width), BF16), sds((tokens, width), BF16)),
        [HBM, HBM, HBM],
        [
            pltpu.VMEM((tokens, width), BF16),
            pltpu.VMEM((width,), BF16),
            pltpu.VMEM((width, local_width), BF16),
            pltpu.SemaphoreType.DMA((3,)),
        ],
        flops=2 * tokens * width * local_width,
        bytes_accessed=2 * width * (tokens + local_width),
    )(
        pltpu.with_memory_space_constraint(hidden, HBM),
        pltpu.with_memory_space_constraint(gain_attn, HBM),
        w_three,
    )

    def over_z(value, step):
        return lax.ppermute(value, "z", [(i, (i + step) % z_count) for i in range(z_count)])

    def over_core(value):
        return lax.ppermute(value, "core", [(0, 1), (1, 0)])

    steps = sorted(range(1, z_count), key=lambda step: -min(step, z_count - step))

    order = far_last(z_count)
    pieces = [over_z(query, step) if step else query for step in order]
    keys, values, visible = call(
        load_kernel,
        (
            sds(cache_keys.shape, BF16),
            sds(cache_values.shape, BF16),
            sds((tokens, tokens), F32),
        ),
        [HBM, HBM, HBM, pl.ANY],
        [pltpu.VMEM(parents.shape, jnp.int32), pltpu.SemaphoreType.DMA((3,))],
        bytes_accessed=4 * requests * page * width,
        vmem=16 << 20,
    )(
        cache_keys,
        cache_values,
        pltpu.with_memory_space_constraint(parents, HBM),
        query,
    )
    pieces[0], keys = lax.optimization_barrier((pieces[0], keys))
    other_pieces = [over_core(piece) for piece in pieces]

    scratch = [
        pltpu.VMEM((requests, z_count * 2 * tree, page), F32),
        pltpu.VMEM((requests, z_count * 2 * tree, page), BF16),
    ]
    heads = 2 * z_count
    lengths = cache_lengths.reshape(1, requests)
    for_other = call(
        functools.partial(page_kernel, scale, tree, False),
        sds((heads + 1, tokens, HEAD_DIM), BF16),
        [VMEM] * 7,
        scratch,
        flops=2 * tokens * page * width,
        bytes_accessed=2 * requests * page * width,
        vmem=20 << 20,
    )(lengths, *other_pieces, keys, values)
    from_other = over_core(for_other)
    kept, kept_lse = call(
        functools.partial(page_kernel, scale, tree, True),
        (sds((heads, tokens, HEAD_DIM), F32), sds((tokens, 128), F32)),
        [VMEM] * 7 + [pl.ANY],
        scratch,
        flops=2 * tokens * page * width,
        bytes_accessed=2 * requests * page * width,
        vmem=20 << 20,
    )(lengths, *pieces, keys, values, for_other)
    merged = call(
        merge_kernel,
        tuple(sds((padded, local_width), BF16) for _ in range(z_count)),
        [VMEM] * 3,
        [pltpu.VMEM((256, 128), F32)],
        bytes_accessed=1 << 20,
    )(from_other, kept, kept_lse)
    arrived = [merged[0]] + [over_z(merged[order.index(step)], -step) for step in steps]

    tree_o, tree_lse = call(
        functools.partial(tree_kernel, scale),
        (sds((tokens, local_width), F32), sds((8, 256), F32)),
        [VMEM, HBM, VMEM, VMEM, pl.ANY],
        [
            pltpu.VMEM((256, 128), F32),
            pltpu.VMEM((2, width, local_width), BF16),
            pltpu.SemaphoreType.DMA((2,)),
        ],
        flops=4 * tokens * width * local_width,
        bytes_accessed=2 * width * (tokens + 2 * local_width),
    )(normed_attn, w_three, query, visible, merged[0])
    theirs, ours = call(
        out_kernel,
        (sds((z_count * own, width), BF16), sds((z_count * own, width), F32)),
        [VMEM] * 7,
        [pltpu.VMEM((128, 256), F32), pltpu.VMEM((tokens, local_width), F32)],
        flops=2 * tokens * width * local_width,
        bytes_accessed=2 * width * (tokens + local_width),
    )(*arrived, tree_o, tree_lse, w_out)
    folded = call(
        fold_kernel,
        tuple(sds((own, width), BF16 if step else F32) for step in range(z_count)),
        [VMEM] * 2,
        bytes_accessed=1 << 20,
    )(ours, over_core(theirs))
    mixed = [folded[0]] + [over_z(folded[step], -step) for step in steps]
    block = experts * SLOTS // 2
    real = block // SLOTS * CAP
    weight_rows = width + width * w_down.shape[1] // w_gate_up.shape[2]
    place, gather, scatter, weights = call(
        table_kernel,
        (
            sds((chunks, experts * SLOTS, 2 * own), BF16),
            sds((1 + chunks, real, block), BF16),
            sds((chunks, block, 2 * real), BF16),
            sds((weight_rows, w_gate_up.shape[2]), BF16),
        ),
        [VMEM, HBM, HBM, pl.ANY],
        [pltpu.SemaphoreType.DMA((1 + width // w_gate_up.shape[2],))],
        flops=1 << 24,
        bytes_accessed=1 << 23,
        vmem=16 << 20,
    )(
        routes.T,
        pltpu.with_memory_space_constraint(w_gate_up[0], HBM),
        pltpu.with_memory_space_constraint(w_down[0], HBM),
        folded[0],
    )
    *mixed, weights = lax.optimization_barrier((*mixed, weights))
    other_weights = over_core(weights)

    residual, normed, outgoing = call(
        residual_kernel,
        (
            sds((own, width), F32),
            sds((own, width), BF16),
            sds((experts * SLOTS, packed), BF16),
        ),
        [VMEM] * 7,
        flops=1 << 27,
        bytes_accessed=1 << 22,
    )(*mixed, hidden, gain_moe, place)
    rows = lax.all_to_all(
        outgoing.reshape(experts, SLOTS, packed),
        ("req", "z"),
        split_axis=0,
        concat_axis=0,
        tiled=True,
    ).reshape(experts * SLOTS, packed)

    summed, table = call(
        expert_kernel,
        (
            sds((experts * SLOTS, packed), BF16),
            sds((chunks, 4 * own, experts * SLOTS), BF16),
        ),
        [VMEM] * 8,
        flops=12 * experts * CAP * width * w_down.shape[1],
        bytes_accessed=12 * width * w_down.shape[1],
        vmem=24 << 20,
    )(
        rows,
        weights,
        other_weights,
        gather,
        scatter,
        normed,
        w_router.T,
        routes.T,
    )
    back = lax.all_to_all(
        summed.reshape(experts, SLOTS, packed),
        ("req", "z"),
        split_axis=0,
        concat_axis=0,
        tiled=True,
    ).reshape(experts * SLOTS, packed)
    return call(
        final_kernel,
        sds((own, width), BF16),
        [VMEM] * 3,
        flops=1 << 27,
        bytes_accessed=1 << 22,
    )(back, table, residual)


def solution(mesh):
    req_count, exp_count = mesh.devices.shape
    split = Mesh(
        mesh.devices.reshape(req_count, exp_count // CORES, CORES), ("req", "z", "core")
    )
    exp = ("z", "core")
    everywhere = ("req", "z", "core")
    in_specs = (
        P("req", None),
        P(),
        P(None, None, exp),
        P(exp, None),
        P("req", exp, None),
        P("req", exp, None),
        P("req"),
        P("req", None),
        P(),
        P(),
        P(everywhere, None),
        P(everywhere, None, None),
        P(everywhere, None, None),
    )
    return jax.shard_map(
        per_device,
        mesh=split,
        in_specs=in_specs,
        out_specs=P(everywhere, None),
        check_vma=False,
    )
```

```python
import functools

import jax
import jax.numpy as jnp
from jax import lax
from jax.experimental import pallas as pl
from jax.experimental.pallas import tpu as pltpu
from jax.sharding import Mesh
from jax.sharding import PartitionSpec as P

HEAD_DIM = 128
EXP_SPLIT = 2
CORES = 2
CAP = 6
SLOTS = 8

EPSILON = 1e-05
NEGATIVE = -1e30
F32 = jnp.float32
BF16 = jnp.bfloat16
VMEM = pltpu.VMEM
SMEM = pltpu.SMEM
HBM = pltpu.HBM


def dot(a, b):
    return jnp.dot(a, b, preferred_element_type=F32)


def dot_t(a, b):
    return lax.dot_general(a, b, (((1,), (1,)), ((), ())), preferred_element_type=F32)


def iota(shape, axis):
    return lax.broadcasted_iota(jnp.int32, shape, axis)


def call(body, out, in_spaces, scratch=(), flops=0, bytes_accessed=0, vmem=10 << 20, aliases={}):
    out_spec = jax.tree.map(lambda _: pl.BlockSpec(memory_space=VMEM), out)
    return pl.pallas_call(
        body,
        out_shape=out,
        in_specs=[pl.BlockSpec(memory_space=s) for s in in_spaces],
        out_specs=out_spec,
        scratch_shapes=list(scratch),
        input_output_aliases=aliases,
        compiler_params=pltpu.CompilerParams(vmem_limit_bytes=vmem),
        cost_estimate=pl.CostEstimate(
            flops=flops, bytes_accessed=bytes_accessed, transcendentals=0
        ),
    )


def sds(shape, dtype):
    return jax.ShapeDtypeStruct(shape, dtype)


def homes(count, other, order=None):
    z, core = lax.axis_index("z"), lax.axis_index("core")
    core = 1 - core if other else core
    return [lax.rem(z + count - i, count) * CORES + core for i in order or range(count)]


def far_last(count):
    return sorted(range(count), key=lambda step: min(step, count - step))


def normed_rows(values, gain):
    inverse = lax.rsqrt(jnp.mean(values * values, axis=-1, keepdims=True) + EPSILON)
    return (values * inverse * gain).astype(BF16)


def query_kernel(x_hbm, g_hbm, w_hbm, q_ref, normed_ref, x_ref, g_ref, w_ref, sems):
    x_copy = pltpu.make_async_copy(x_hbm, x_ref, sems.at[0])
    w_copy = pltpu.make_async_copy(w_hbm.at[0], w_ref, sems.at[1])
    g_copy = pltpu.make_async_copy(g_hbm, g_ref, sems.at[2])
    x_copy.start()
    g_copy.start()
    w_copy.start()
    g_copy.wait()
    x_copy.wait()
    gain = g_ref[...].astype(F32).reshape(1, -1)
    normed_ref[...] = normed_rows(x_ref[...].astype(F32), gain)
    w_copy.wait()
    q_ref[...] = dot(normed_ref[...], w_ref[...]).astype(BF16)


def load_kernel(v_hbm, up_hbm, after_ref, v_ref, visible_ref, up_ref, sems):
    del after_ref
    up_copy = pltpu.make_async_copy(up_hbm, up_ref, sems.at[0])
    v_copy = pltpu.make_async_copy(v_hbm, v_ref, sems.at[1])
    up_copy.start()
    v_copy.start()
    up_copy.wait()
    visible_ref[...] = ancestors(up_ref)
    v_copy.wait()


def ancestors(up_ref):
    requests, tree = up_ref.shape
    tokens = requests * tree
    spread = iota((tree, tokens), 0) == iota((tree, tokens), 1) % tree
    wide = dot(up_ref[...].astype(BF16), jnp.where(spread, 1.0, 0.0).astype(BF16))
    home = iota((requests, tokens), 1) // tree
    wide = jnp.where(iota((requests, tokens), 0) == home, wide + (home * tree).astype(F32), 0.0)
    parent = jnp.sum(wide, axis=0, keepdims=True)
    row = iota((tokens, tokens), 0)
    same = row == iota((tokens, tokens), 1)
    reach = jnp.where(same | (row.astype(F32) == parent), 1.0, 0.0)
    for _ in range((tree - 1).bit_length()):
        half = reach.astype(BF16)
        reach = jnp.minimum(dot(half, half), 1.0)
    return dot_t(jnp.where(same, 1.0, 0.0).astype(BF16), reach.astype(BF16))


def tree_kernel(scale, normed_ref, w_hbm, q_ref, visible_ref, after_ref, *refs):
    o_ref, lse_ref, turn, w_ref, sems = refs
    del after_ref
    tokens, width = q_ref.shape
    w_copies = [
        pltpu.make_async_copy(w_hbm.at[i + 1], w_ref.at[i], sems.at[i]) for i in range(2)
    ]
    for w_copy in w_copies:
        w_copy.start()
    w_copies[0].wait()
    keys = dot(normed_ref[...], w_ref[0]).astype(BF16)
    w_copies[1].wait()
    values = dot(normed_ref[...], w_ref[1]).astype(BF16)
    visible = visible_ref[...] > 0.5
    lane = iota((tokens, 128), 1)
    stats = jnp.zeros((tokens, 128), F32)
    for h in range(width // HEAD_DIM):
        cut = slice(h * HEAD_DIM, (h + 1) * HEAD_DIM)
        scores = dot_t(q_ref[:, cut], keys[:, cut]) * scale
        scores = jnp.where(visible, scores, NEGATIVE)
        high = jnp.max(scores, axis=-1, keepdims=True)
        weights = jnp.where(visible, jnp.exp(scores - high), 0.0)
        total = jnp.sum(weights, axis=-1, keepdims=True)
        o_ref[:, cut] = dot(weights.astype(BF16), values[:, cut]) / total
        stats = jnp.where(lane == h, high + jnp.log(total), stats)
    turn[0:tokens, :] = stats
    lse_ref[...] = jnp.transpose(turn[...])[0:8, :]


def page_kernel(scale, tree, kept, lengths_ref, *refs):
    pieces, (k_ref, v_ref) = refs[:4], refs[4:6]
    outs = refs[7:-2] if kept else refs[6:-2]
    s_all, p_all = refs[-2:]
    out_ref = outs[0]
    requests, page = k_ref.shape[0], k_ref.shape[1]
    width = pieces[0].shape[1]
    pair = 2 * tree
    lane = iota((tree, 128), 1)
    wide = iota((tree, width), 1) < HEAD_DIM
    owners = homes(len(pieces), not kept, far_last(len(pieces)))
    start = (lax.axis_index("z") * CORES + lax.axis_index("core")) * page
    lives = lengths_ref[...] - start

    def columns(i):
        return pl.ds(pl.multiple_of(owners[i] * width, width), width)

    for r in range(requests):
        rows = slice(r * tree, (r + 1) * tree)
        for i, piece in enumerate(pieces):
            query = piece[rows, :]
            zero = jnp.zeros_like(query)
            both = jnp.concatenate(
                [jnp.where(wide, query, zero), jnp.where(wide, zero, query)], axis=0
            )
            s_all[r, i * pair : (i + 1) * pair, :] = dot_t(both, k_ref[r, :, columns(i)])
    for r in range(requests):
        rows = slice(r * tree, (r + 1) * tree)
        scores = s_all[r] * scale
        scores = jnp.where(iota(scores.shape, 1) < lives[:, r : r + 1], scores, NEGATIVE)
        high = jnp.max(scores, axis=-1, keepdims=True)
        weights = jnp.exp(scores - high)
        total = jnp.sum(weights, axis=-1, keepdims=True)
        p_all[r] = weights.astype(BF16)
        inverse = 1.0 / total
        lse = high + jnp.log(total)
        first = lse.astype(BF16).astype(F32)
        second = (lse - first).astype(BF16).astype(F32)
        third = lse - first - second
        stats = jnp.zeros((tree, 128), F32)
        for i in range(len(pieces)):
            summed = dot(p_all[r, i * pair : (i + 1) * pair, :], v_ref[r, :, columns(i)])
            for h in range(2):
                own = slice(i * pair + h * tree, i * pair + (h + 1) * tree)
                cut = slice(h * HEAD_DIM, (h + 1) * HEAD_DIM)
                value = summed[h * tree : (h + 1) * tree, cut] * inverse[own]
                out_ref[2 * i + h, rows, :] = value.astype(out_ref.dtype)
                if kept:
                    stats = jnp.where(lane == i * 8 + h, lse[own], stats)
                else:
                    for j, part in enumerate((first, second, third)):
                        stats = jnp.where(lane == i * 8 + 2 * j + h, part[own], stats)
        if kept:
            outs[1][rows, :] = stats
        else:
            out_ref[8, rows, :] = stats.astype(BF16)


def merge_kernel(other_ref, kept_ref, lse_ref, *refs):
    outs, turn = refs[:-1], refs[-1]
    tokens = lse_ref.shape[0]
    sent = other_ref[8].astype(F32)
    other = sent + pltpu.roll(sent, 126, 1) + pltpu.roll(sent, 124, 1)
    kept = lse_ref[...]
    high = jnp.maximum(other, kept)
    other, kept = jnp.exp(other - high), jnp.exp(kept - high)
    whole = other + kept
    inverse = 1.0 / whole
    other, kept = other * inverse, kept * inverse
    lse = jnp.where(iota(high.shape, 1) % 8 < 2, high + jnp.log(whole), 0.0)
    first = lse.astype(BF16).astype(F32)
    second = (lse - first).astype(BF16).astype(F32)
    third = lse - first - second
    turn[0:tokens, :] = first + pltpu.roll(second, 2, 1) + pltpu.roll(third, 4, 1)
    turn[tokens:, :] = jnp.zeros((turn.shape[0] - tokens, 128), F32)
    turned = jnp.transpose(turn[...])
    for i, out_ref in enumerate(outs):
        for h in range(2):
            at = i * 8 + h
            value = other[:, at : at + 1] * other_ref[2 * i + h].astype(F32)
            value = value + kept[:, at : at + 1] * kept_ref[2 * i + h]
            out_ref[0:tokens, h * HEAD_DIM : (h + 1) * HEAD_DIM] = value.astype(BF16)
        out_ref[tokens:, :] = turned[i * 8 : (i + 1) * 8, :].astype(BF16)


def out_kernel(*refs):
    parts = refs[:4]
    tree_o_ref, tree_lse_ref, w_ref, theirs_ref, ours_ref, turn, mixed = refs[4:]
    padded, width = parts[0].shape
    tokens = padded - 8
    heads = width // HEAD_DIM
    own = ours_ref.shape[0] // 4
    lses = []
    for part in parts:
        rows = part[tokens:, :].astype(F32)
        lses.append(rows[0:2] + rows[2:4] + rows[4:6])
    lses.append(tree_lse_ref[0:2, :])
    high = functools.reduce(jnp.maximum, lses)
    factors = [jnp.exp(value - high) for value in lses]
    whole = functools.reduce(lambda a, b: a + b, factors)
    for s, factor in enumerate(factors):
        turn[2 * s : 2 * s + 2, :] = factor / whole
    turned = jnp.transpose(turn[...])[0:tokens, :]
    for h in range(heads):
        cut = slice(h * HEAD_DIM, (h + 1) * HEAD_DIM)
        at = 2 * len(parts) + h
        total = turned[:, at : at + 1] * tree_o_ref[:, cut]
        for s, part in enumerate(parts):
            at = 2 * s + h
            total = total + turned[:, at : at + 1] * part[0:tokens, cut].astype(F32)
        mixed[:, cut] = total

    def rows_of(other):
        rows = [
            mixed[pl.ds(pl.multiple_of(owner * own, 8), own), :]
            for owner in homes(len(parts), other)
        ]
        return jnp.concatenate(rows, axis=0).astype(BF16)

    theirs_ref[...] = dot(rows_of(True), w_ref[...]).astype(BF16)
    ours_ref[...] = dot(rows_of(False), w_ref[...])


def fold_kernel(ours_ref, theirs_ref, *outs):
    own = outs[0].shape[0]
    for i, out_ref in enumerate(outs):
        rows = slice(i * own, (i + 1) * own)
        out_ref[...] = (ours_ref[rows, :] + theirs_ref[rows, :].astype(F32)).astype(out_ref.dtype)


def expert_of_row(rows, experts):
    return jnp.where(iota((rows, experts), 0) // SLOTS == iota((rows, experts), 1), 1.0, 0.0)


def table_kernel(routes_ref, up_hbm, down_hbm, after_ref, *refs):
    place_refs, (weights_ref, sems) = refs[:3], refs[3:]
    del after_ref
    depth, both = up_hbm.shape
    units = down_hbm.shape[0]
    copies = [pltpu.make_async_copy(up_hbm, weights_ref.at[0:depth], sems.at[0])]
    for i in range(down_hbm.shape[1] // both):
        at = depth + i * units
        copies.append(
            pltpu.make_async_copy(
                down_hbm.at[:, i * both : (i + 1) * both],
                weights_ref.at[at : at + units],
                sems.at[1 + i],
            )
        )
    for copy in copies:
        copy.start()
    place_kernel(routes_ref, *place_refs)
    for copy in copies:
        copy.wait()


def place_kernel(routes_ref, place_ref, gather_ref, scatter_ref):
    chunks = place_ref.shape[0]
    _, real, block = gather_ref.shape
    row, column = iota((real, block), 0), iota((real, block), 1)
    base, slot = row // CAP * SLOTS, row % CAP
    gather_ref[0] = jnp.where(column == base + slot, 1.0, 0.0).astype(BF16)
    for k in range(chunks):
        hit = (column == base + CAP + slot // chunks) & (slot % chunks == k)
        gather_ref[1 + k] = jnp.where(hit, 1.0, 0.0).astype(BF16)
    row, column = iota((block, 2 * real), 0), iota((block, 2 * real), 1)
    is_tail = column >= real
    column = column - jnp.where(is_tail, real, 0)
    base, slot = column // CAP * SLOTS, column % CAP
    for k in range(chunks):
        main = (row == base + slot) & jnp.logical_not(is_tail)
        tail = (row == base + CAP + slot // chunks) & (slot % chunks == k) & is_tail
        scatter_ref[k] = jnp.where(main | tail, 1.0, 0.0).astype(BF16)
    top, tokens = routes_ref.shape
    chunks, rows, _ = place_ref.shape
    experts = rows // SLOTS
    named = iota((experts, tokens), 0)
    chosen = jnp.zeros((experts, tokens), F32)
    for k in range(top):
        chosen = jnp.where(routes_ref[k : k + 1, :] == named, 1.0, chosen)
    source = iota((tokens, 2 * tokens), 0)
    target = iota((tokens, 2 * tokens), 1) % tokens
    chosen = chosen.astype(BF16)
    rank = dot(chosen, jnp.where(source < target, 1.0, 0.0).astype(BF16))
    both = dot(chosen, jnp.where(source == target, 1.0, 0.0).astype(BF16))
    rank = jnp.where(both > 0.5, rank, -1.0).astype(BF16)
    spread = dot(expert_of_row(rows, experts).astype(BF16), rank)
    slot = iota((rows, 2 * tokens), 0) % SLOTS
    is_tail = iota((rows, 2 * tokens), 1) >= tokens
    for j in range(chunks):
        wanted = jnp.where(is_tail, (slot - CAP) * chunks + j, slot)
        valid = is_tail == (slot >= CAP)
        hit = valid & (spread == wanted.astype(F32))
        place_ref[j] = jnp.where(hit, 1.0, 0.0).astype(BF16)


def residual_kernel(*refs):
    parts = refs[:4]
    x_ref, g_ref, place_ref, res_ref, normed_ref, out_ref = refs[4:]
    tokens, width = parts[0].shape
    chunks = place_ref.shape[0]
    cut = width // (chunks + 1)
    start = pl.multiple_of(homes(len(parts), False)[0] * tokens, 8)
    residual = x_ref[pl.ds(start, tokens), :].astype(F32)
    for part in parts:
        residual = residual + part[...].astype(F32)
    res_ref[...] = residual
    inverse = lax.rsqrt(jnp.mean(residual * residual, axis=-1, keepdims=True) + EPSILON)
    normed = residual * inverse * g_ref[...].astype(F32).reshape(1, -1)
    normed_ref[...] = normed.astype(BF16)
    tail = normed[:, chunks * cut :]
    for j in range(chunks):
        pair = jnp.concatenate([normed[:, j * cut : (j + 1) * cut], tail], axis=0).astype(BF16)
        out_ref[:, j * cut : (j + 1) * cut] = dot(place_ref[j], pair).astype(BF16)


def gate_kernel(normed_ref, router_ref, routes_ref, table_ref):
    top, tokens = routes_ref.shape
    experts = router_ref.shape[0]
    chunks, _, rows = table_ref.shape
    logits = dot_t(normed_ref[...], router_ref[...])
    exponent = jnp.exp(logits)
    chances = exponent / jnp.sum(exponent, axis=-1, keepdims=True)
    named = iota((experts, tokens), 0)
    chosen = jnp.zeros((experts, tokens), F32)
    for k in range(top):
        chosen = jnp.where(routes_ref[k : k + 1, :] == named, 1.0, chosen)
    same = jnp.where(iota((tokens, tokens), 0) == iota((tokens, tokens), 1), 1.0, 0.0)
    chosen = dot_t(same.astype(BF16), chosen.astype(BF16))
    picked = chances * chosen
    gates = picked / jnp.sum(picked, axis=-1, keepdims=True)
    earlier = jnp.where(iota((tokens, tokens), 0) > iota((tokens, tokens), 1), 1.0, 0.0)
    rank = dot(earlier.astype(BF16), chosen.astype(BF16))
    rank = jnp.where(chosen > 0.5, rank, -1.0).astype(BF16)
    first = gates.astype(BF16)
    second = (gates - first.astype(F32)).astype(BF16)
    home = iota((experts, rows), 0) == iota((experts, rows), 1) // SLOTS
    home = jnp.where(home, 1.0, 0.0).astype(BF16)
    rank, first, second = dot(rank, home), dot(first, home), dot(second, home)
    slot = iota((tokens, rows), 1) % SLOTS
    main = (slot < CAP) & (rank == slot.astype(F32))
    for j in range(chunks):
        tail = (slot >= CAP) & (rank == ((slot - CAP) * chunks + j).astype(F32))
        table_ref[j] = jnp.concatenate(
            [
                jnp.where(main, first, 0.0),
                jnp.where(main, second, 0.0),
                jnp.where(tail, first, 0.0),
                jnp.where(tail, second, 0.0),
            ],
            axis=0,
        ).astype(BF16)


def expert_kernel(
    x_ref,
    weights_ref,
    other_ref,
    gather_ref,
    scatter_ref,
    normed_ref,
    router_ref,
    routes_ref,
    out_ref,
    table_ref,
):
    gate_kernel(normed_ref, router_ref, routes_ref, table_ref)
    rows, packed = x_ref.shape
    width = normed_ref.shape[1]
    both = weights_ref.shape[1]
    units = both // 2
    cut = width - packed
    chunks = packed // cut
    _, real, block = gather_ref.shape
    mains, tails = [], []
    for at in range(0, rows, block):
        span = slice(at, at + block)
        mains.append(dot(gather_ref[0], x_ref[span, :]).astype(BF16))
        tail = dot(gather_ref[1], x_ref[span, 0:cut])
        for k in range(1, chunks):
            tail = tail + dot(gather_ref[1 + k], x_ref[span, k * cut : (k + 1) * cut])
        tails.append(tail.astype(BF16))
    main, tail = jnp.concatenate(mains, axis=0), jnp.concatenate(tails, axis=0)
    hidden = []
    for weights in (weights_ref, other_ref):
        parts = []
        for at in range(0, units, units // 2):
            gate_cut = slice(at, at + units // 2)
            up_cut = slice(units + at, units + at + units // 2)
            gate = dot(main, weights[0:packed, gate_cut]) + dot(tail, weights[packed:width, gate_cut])
            up = dot(main, weights[0:packed, up_cut]) + dot(tail, weights[packed:width, up_cut])
            parts.append((gate / (1.0 + jnp.exp(-gate)) * up).astype(BF16))
        hidden.append(jnp.concatenate(parts, axis=1))

    def result(k):
        at = width + k * cut // both * units
        rows, columns = slice(at, at + units), slice(k * cut % both, k * cut % both + cut)
        first = dot(hidden[0], weights_ref[rows, columns]).astype(BF16).astype(F32)
        second = dot(hidden[1], other_ref[rows, columns]).astype(BF16).astype(F32)
        return (first + second).astype(BF16)

    last = result(chunks)
    for k in range(chunks):
        columns = slice(k * cut, (k + 1) * cut)
        value = result(k)
        for i in range(rows // block):
            own = slice(i * real, (i + 1) * real)
            pair = jnp.concatenate([value[own], last[own]], axis=0)
            out_ref[i * block : (i + 1) * block, columns] = dot(scatter_ref[k], pair).astype(
                BF16
            )


def final_kernel(back_ref, table_ref, res_ref, out_ref):
    tokens, width = res_ref.shape
    chunks = table_ref.shape[0]
    cut = width // (chunks + 1)
    tail = res_ref[:, chunks * cut :]
    for j in range(chunks):
        span = slice(j * cut, (j + 1) * cut)
        sums = dot(table_ref[j], back_ref[:, span])
        main = sums[0:tokens] + sums[tokens : 2 * tokens]
        out_ref[:, span] = (res_ref[:, span] + main).astype(BF16)
        tail = tail + (sums[2 * tokens : 3 * tokens] + sums[3 * tokens :])
    out_ref[:, chunks * cut :] = tail.astype(BF16)


def per_device(
    hidden,
    gain_attn,
    w_qkv,
    w_out,
    cache_keys,
    cache_values,
    cache_lengths,
    parents,
    gain_moe,
    w_router,
    routes,
    w_gate_up,
    w_down,
):
    z_count = lax.axis_size("z")
    exp_count = z_count * CORES
    tokens, width = hidden.shape
    requests, tree = parents.shape
    page = cache_keys.shape[1]
    local_width = w_qkv.shape[2]
    scale = HEAD_DIM ** (-0.5)
    own = tokens // exp_count
    experts = w_router.shape[1]
    packed = width * CAP // SLOTS
    chunks = packed // (width - packed)
    padded = tokens + 8

    w_three = pltpu.with_memory_space_constraint(jnp.transpose(w_qkv, (1, 0, 2)), HBM)
    cache_values = pltpu.with_memory_space_constraint(cache_values, HBM)

    query, normed_attn = call(
        query_kernel,
        (sds((tokens, local_width), BF16), sds((tokens, width), BF16)),
        [HBM, HBM, HBM],
        [
            pltpu.VMEM((tokens, width), BF16),
            pltpu.VMEM((width,), BF16),
            pltpu.VMEM((width, local_width), BF16),
            pltpu.SemaphoreType.DMA((3,)),
        ],
        flops=2 * tokens * width * local_width,
        bytes_accessed=2 * width * (tokens + local_width),
    )(
        pltpu.with_memory_space_constraint(hidden, HBM),
        pltpu.with_memory_space_constraint(gain_attn, HBM),
        w_three,
    )

    def over_z(value, step):
        return lax.ppermute(value, "z", [(i, (i + step) % z_count) for i in range(z_count)])

    def over_core(value):
        return lax.ppermute(value, "core", [(0, 1), (1, 0)])

    steps = sorted(range(1, z_count), key=lambda step: -min(step, z_count - step))

    order = far_last(z_count)
    pieces = [over_z(query, step) if step else query for step in order]
    keys = pltpu.with_memory_space_constraint(cache_keys, VMEM)
    values, visible = call(
        load_kernel,
        (sds(cache_values.shape, BF16), sds((tokens, tokens), F32)),
        [HBM, HBM, pl.ANY],
        [pltpu.VMEM(parents.shape, jnp.int32), pltpu.SemaphoreType.DMA((2,))],
        bytes_accessed=2 * requests * page * width,
        vmem=16 << 20,
    )(cache_values, pltpu.with_memory_space_constraint(parents, HBM), query)
    pieces[0], values = lax.optimization_barrier((pieces[0], values))
    other_pieces = [over_core(piece) for piece in pieces]

    scratch = [
        pltpu.VMEM((requests, z_count * 2 * tree, page), F32),
        pltpu.VMEM((requests, z_count * 2 * tree, page), BF16),
    ]
    heads = 2 * z_count
    lengths = cache_lengths.reshape(1, requests)
    for_other = call(
        functools.partial(page_kernel, scale, tree, False),
        sds((heads + 1, tokens, HEAD_DIM), BF16),
        [VMEM] * 7,
        scratch,
        flops=2 * tokens * page * width,
        bytes_accessed=2 * requests * page * width,
        vmem=20 << 20,
    )(lengths, *other_pieces, keys, values)
    from_other = over_core(for_other)
    kept, kept_lse = call(
        functools.partial(page_kernel, scale, tree, True),
        (sds((heads, tokens, HEAD_DIM), F32), sds((tokens, 128), F32)),
        [VMEM] * 7 + [pl.ANY],
        scratch,
        flops=2 * tokens * page * width,
        bytes_accessed=2 * requests * page * width,
        vmem=20 << 20,
    )(lengths, *pieces, keys, values, for_other)
    merged = call(
        merge_kernel,
        tuple(sds((padded, local_width), BF16) for _ in range(z_count)),
        [VMEM] * 3,
        [pltpu.VMEM((256, 128), F32)],
        bytes_accessed=1 << 20,
    )(from_other, kept, kept_lse)
    arrived = [merged[0]] + [over_z(merged[order.index(step)], -step) for step in steps]

    tree_o, tree_lse = call(
        functools.partial(tree_kernel, scale),
        (sds((tokens, local_width), F32), sds((8, 256), F32)),
        [VMEM, HBM, VMEM, VMEM, pl.ANY],
        [
            pltpu.VMEM((256, 128), F32),
            pltpu.VMEM((2, width, local_width), BF16),
            pltpu.SemaphoreType.DMA((2,)),
        ],
        flops=4 * tokens * width * local_width,
        bytes_accessed=2 * width * (tokens + 2 * local_width),
    )(normed_attn, w_three, query, visible, merged[0])
    theirs, ours = call(
        out_kernel,
        (sds((z_count * own, width), BF16), sds((z_count * own, width), F32)),
        [VMEM] * 7,
        [pltpu.VMEM((128, 256), F32), pltpu.VMEM((tokens, local_width), F32)],
        flops=2 * tokens * width * local_width,
        bytes_accessed=2 * width * (tokens + local_width),
    )(*arrived, tree_o, tree_lse, w_out)
    folded = call(
        fold_kernel,
        tuple(sds((own, width), BF16 if step else F32) for step in range(z_count)),
        [VMEM] * 2,
        bytes_accessed=1 << 20,
    )(ours, over_core(theirs))
    mixed = [folded[0]] + [over_z(folded[step], -step) for step in steps]
    block = experts * SLOTS // 2
    real = block // SLOTS * CAP
    weight_rows = width + width * w_down.shape[1] // w_gate_up.shape[2]
    place, gather, scatter, weights = call(
        table_kernel,
        (
            sds((chunks, experts * SLOTS, 2 * own), BF16),
            sds((1 + chunks, real, block), BF16),
            sds((chunks, block, 2 * real), BF16),
            sds((weight_rows, w_gate_up.shape[2]), BF16),
        ),
        [VMEM, HBM, HBM, pl.ANY],
        [pltpu.SemaphoreType.DMA((1 + width // w_gate_up.shape[2],))],
        flops=1 << 24,
        bytes_accessed=1 << 23,
        vmem=16 << 20,
    )(
        routes.T,
        pltpu.with_memory_space_constraint(w_gate_up[0], HBM),
        pltpu.with_memory_space_constraint(w_down[0], HBM),
        folded[0],
    )
    *mixed, weights = lax.optimization_barrier((*mixed, weights))
    other_weights = over_core(weights)

    residual, normed, outgoing = call(
        residual_kernel,
        (
            sds((own, width), F32),
            sds((own, width), BF16),
            sds((experts * SLOTS, packed), BF16),
        ),
        [VMEM] * 7,
        flops=1 << 27,
        bytes_accessed=1 << 22,
    )(*mixed, hidden, gain_moe, place)
    rows = lax.all_to_all(
        outgoing.reshape(experts, SLOTS, packed),
        ("req", "z"),
        split_axis=0,
        concat_axis=0,
        tiled=True,
    ).reshape(experts * SLOTS, packed)

    summed, table = call(
        expert_kernel,
        (
            sds((experts * SLOTS, packed), BF16),
            sds((chunks, 4 * own, experts * SLOTS), BF16),
        ),
        [VMEM] * 8,
        flops=12 * experts * CAP * width * w_down.shape[1],
        bytes_accessed=12 * width * w_down.shape[1],
        vmem=24 << 20,
    )(
        rows,
        weights,
        other_weights,
        gather,
        scatter,
        normed,
        w_router.T,
        routes.T,
    )
    back = lax.all_to_all(
        summed.reshape(experts, SLOTS, packed),
        ("req", "z"),
        split_axis=0,
        concat_axis=0,
        tiled=True,
    ).reshape(experts * SLOTS, packed)
    return call(
        final_kernel,
        sds((own, width), BF16),
        [VMEM] * 3,
        flops=1 << 27,
        bytes_accessed=1 << 22,
    )(back, table, residual)


def solution(mesh):
    req_count, exp_count = mesh.devices.shape
    split = Mesh(
        mesh.devices.reshape(req_count, exp_count // CORES, CORES), ("req", "z", "core")
    )
    exp = ("z", "core")
    everywhere = ("req", "z", "core")
    in_specs = (
        P("req", None),
        P(),
        P(None, None, exp),
        P(exp, None),
        P("req", exp, None),
        P("req", exp, None),
        P("req"),
        P("req", None),
        P(),
        P(),
        P(everywhere, None),
        P(everywhere, None, None),
        P(everywhere, None, None),
    )
    return jax.shard_map(
        per_device,
        mesh=split,
        in_specs=in_specs,
        out_specs=P(everywhere, None),
        check_vma=False,
    )
```

```python
import functools

import jax
import jax.numpy as jnp
from jax import lax
from jax.experimental import pallas as pl
from jax.experimental.pallas import tpu as pltpu
from jax.sharding import Mesh
from jax.sharding import PartitionSpec as P

HEAD_DIM = 128
EXP_SPLIT = 2
CORES = 2
CAP = 6
SLOTS = 8

EPSILON = 1e-05
NEGATIVE = -1e30
F32 = jnp.float32
BF16 = jnp.bfloat16
VMEM = pltpu.VMEM
SMEM = pltpu.SMEM
HBM = pltpu.HBM


def dot(a, b):
    return jnp.dot(a, b, preferred_element_type=F32)


def dot_t(a, b):
    return lax.dot_general(a, b, (((1,), (1,)), ((), ())), preferred_element_type=F32)


def iota(shape, axis):
    return lax.broadcasted_iota(jnp.int32, shape, axis)


def call(body, out, in_spaces, scratch=(), flops=0, bytes_accessed=0, vmem=10 << 20, aliases={}):
    out_spec = jax.tree.map(lambda _: pl.BlockSpec(memory_space=VMEM), out)
    return pl.pallas_call(
        body,
        out_shape=out,
        in_specs=[pl.BlockSpec(memory_space=s) for s in in_spaces],
        out_specs=out_spec,
        scratch_shapes=list(scratch),
        input_output_aliases=aliases,
        compiler_params=pltpu.CompilerParams(vmem_limit_bytes=vmem),
        cost_estimate=pl.CostEstimate(
            flops=flops, bytes_accessed=bytes_accessed, transcendentals=0
        ),
    )


def sds(shape, dtype):
    return jax.ShapeDtypeStruct(shape, dtype)


def homes(count, other, order=None):
    z, core = lax.axis_index("z"), lax.axis_index("core")
    core = 1 - core if other else core
    return [lax.rem(z + count - i, count) * CORES + core for i in order or range(count)]


def far_last(count):
    return sorted(range(count), key=lambda step: min(step, count - step))


def normed_rows(values, gain):
    inverse = lax.rsqrt(jnp.mean(values * values, axis=-1, keepdims=True) + EPSILON)
    return (values * inverse * gain).astype(BF16)


def query_kernel(x_hbm, g_hbm, w_hbm, q_ref, normed_ref, x_ref, g_ref, w_ref, sems):
    x_copy = pltpu.make_async_copy(x_hbm, x_ref, sems.at[0])
    w_copy = pltpu.make_async_copy(w_hbm.at[0], w_ref, sems.at[1])
    g_copy = pltpu.make_async_copy(g_hbm, g_ref, sems.at[2])
    x_copy.start()
    g_copy.start()
    w_copy.start()
    g_copy.wait()
    x_copy.wait()
    gain = g_ref[...].astype(F32).reshape(1, -1)
    normed_ref[...] = normed_rows(x_ref[...].astype(F32), gain)
    w_copy.wait()
    q_ref[...] = dot(normed_ref[...], w_ref[...]).astype(BF16)


def load_kernel(v_hbm, up_hbm, after_ref, v_ref, visible_ref, up_ref, sems):
    del after_ref
    up_copy = pltpu.make_async_copy(up_hbm, up_ref, sems.at[0])
    v_copy = pltpu.make_async_copy(v_hbm, v_ref, sems.at[1])
    up_copy.start()
    v_copy.start()
    up_copy.wait()
    visible_ref[...] = ancestors(up_ref)
    v_copy.wait()


def ancestors(up_ref):
    requests, tree = up_ref.shape
    tokens = requests * tree
    spread = iota((tree, tokens), 0) == iota((tree, tokens), 1) % tree
    wide = dot(up_ref[...].astype(BF16), jnp.where(spread, 1.0, 0.0).astype(BF16))
    home = iota((requests, tokens), 1) // tree
    wide = jnp.where(iota((requests, tokens), 0) == home, wide + (home * tree).astype(F32), 0.0)
    parent = jnp.sum(wide, axis=0, keepdims=True)
    row = iota((tokens, tokens), 0)
    same = row == iota((tokens, tokens), 1)
    reach = jnp.where(same | (row.astype(F32) == parent), 1.0, 0.0)
    for _ in range((tree - 1).bit_length()):
        half = reach.astype(BF16)
        reach = jnp.minimum(dot(half, half), 1.0)
    return dot_t(jnp.where(same, 1.0, 0.0).astype(BF16), reach.astype(BF16))


def tree_kernel(scale, normed_ref, w_hbm, q_ref, visible_ref, after_ref, *refs):
    o_ref, lse_ref, turn, w_ref, sems = refs
    del after_ref
    tokens, width = q_ref.shape
    w_copies = [
        pltpu.make_async_copy(w_hbm.at[i + 1], w_ref.at[i], sems.at[i]) for i in range(2)
    ]
    for w_copy in w_copies:
        w_copy.start()
    w_copies[0].wait()
    keys = dot(normed_ref[...], w_ref[0]).astype(BF16)
    w_copies[1].wait()
    values = dot(normed_ref[...], w_ref[1]).astype(BF16)
    visible = visible_ref[...] > 0.5
    lane = iota((tokens, 128), 1)
    stats = jnp.zeros((tokens, 128), F32)
    for h in range(width // HEAD_DIM):
        cut = slice(h * HEAD_DIM, (h + 1) * HEAD_DIM)
        scores = dot_t(q_ref[:, cut], keys[:, cut]) * scale
        scores = jnp.where(visible, scores, NEGATIVE)
        high = jnp.max(scores, axis=-1, keepdims=True)
        weights = jnp.where(visible, jnp.exp(scores - high), 0.0)
        total = jnp.sum(weights, axis=-1, keepdims=True)
        o_ref[:, cut] = dot(weights.astype(BF16), values[:, cut]) / total
        stats = jnp.where(lane == h, high + jnp.log(total), stats)
    turn[0:tokens, :] = stats
    lse_ref[...] = jnp.transpose(turn[...])[0:8, :]


def page_kernel(scale, tree, kept, lengths_ref, *refs):
    pieces, (k_ref, v_ref) = refs[:4], refs[4:6]
    outs = refs[7:-2] if kept else refs[6:-2]
    s_all, p_all = refs[-2:]
    out_ref = outs[0]
    requests, page = k_ref.shape[0], k_ref.shape[1]
    width = pieces[0].shape[1]
    pair = 2 * tree
    lane = iota((tree, 128), 1)
    wide = iota((tree, width), 1) < HEAD_DIM
    owners = homes(len(pieces), not kept, far_last(len(pieces)))
    start = (lax.axis_index("z") * CORES + lax.axis_index("core")) * page
    lives = lengths_ref[...] - start

    def columns(i):
        return pl.ds(pl.multiple_of(owners[i] * width, width), width)

    for r in range(requests):
        rows = slice(r * tree, (r + 1) * tree)
        for i, piece in enumerate(pieces):
            query = piece[rows, :]
            zero = jnp.zeros_like(query)
            both = jnp.concatenate(
                [jnp.where(wide, query, zero), jnp.where(wide, zero, query)], axis=0
            )
            s_all[r, i * pair : (i + 1) * pair, :] = dot_t(both, k_ref[r, :, columns(i)])
    for r in range(requests):
        rows = slice(r * tree, (r + 1) * tree)
        scores = s_all[r] * scale
        scores = jnp.where(iota(scores.shape, 1) < lives[:, r : r + 1], scores, NEGATIVE)
        high = jnp.max(scores, axis=-1, keepdims=True)
        weights = jnp.exp(scores - high)
        total = jnp.sum(weights, axis=-1, keepdims=True)
        p_all[r] = weights.astype(BF16)
        inverse = 1.0 / total
        lse = high + jnp.log(total)
        first = lse.astype(BF16).astype(F32)
        second = (lse - first).astype(BF16).astype(F32)
        third = lse - first - second
        stats = jnp.zeros((tree, 128), F32)
        for i in range(len(pieces)):
            summed = dot(p_all[r, i * pair : (i + 1) * pair, :], v_ref[r, :, columns(i)])
            for h in range(2):
                own = slice(i * pair + h * tree, i * pair + (h + 1) * tree)
                cut = slice(h * HEAD_DIM, (h + 1) * HEAD_DIM)
                value = summed[h * tree : (h + 1) * tree, cut] * inverse[own]
                out_ref[2 * i + h, rows, :] = value.astype(out_ref.dtype)
                if kept:
                    stats = jnp.where(lane == i * 8 + h, lse[own], stats)
                else:
                    for j, part in enumerate((first, second, third)):
                        stats = jnp.where(lane == i * 8 + 2 * j + h, part[own], stats)
        if kept:
            outs[1][rows, :] = stats
        else:
            out_ref[8, rows, :] = stats.astype(BF16)


def merge_kernel(other_ref, kept_ref, lse_ref, *refs):
    outs, turn = refs[:-1], refs[-1]
    tokens = lse_ref.shape[0]
    sent = other_ref[8].astype(F32)
    other = sent + pltpu.roll(sent, 126, 1) + pltpu.roll(sent, 124, 1)
    kept = lse_ref[...]
    high = jnp.maximum(other, kept)
    other, kept = jnp.exp(other - high), jnp.exp(kept - high)
    whole = other + kept
    inverse = 1.0 / whole
    other, kept = other * inverse, kept * inverse
    lse = jnp.where(iota(high.shape, 1) % 8 < 2, high + jnp.log(whole), 0.0)
    first = lse.astype(BF16).astype(F32)
    second = (lse - first).astype(BF16).astype(F32)
    third = lse - first - second
    turn[0:tokens, :] = first + pltpu.roll(second, 2, 1) + pltpu.roll(third, 4, 1)
    turn[tokens:, :] = jnp.zeros((turn.shape[0] - tokens, 128), F32)
    turned = jnp.transpose(turn[...])
    for i, out_ref in enumerate(outs):
        for h in range(2):
            at = i * 8 + h
            value = other[:, at : at + 1] * other_ref[2 * i + h].astype(F32)
            value = value + kept[:, at : at + 1] * kept_ref[2 * i + h]
            out_ref[0:tokens, h * HEAD_DIM : (h + 1) * HEAD_DIM] = value.astype(BF16)
        out_ref[tokens:, :] = turned[i * 8 : (i + 1) * 8, :].astype(BF16)


def out_kernel(*refs):
    parts = refs[:4]
    tree_o_ref, tree_lse_ref, w_ref, theirs_ref, ours_ref, turn, mixed = refs[4:]
    padded, width = parts[0].shape
    tokens = padded - 8
    heads = width // HEAD_DIM
    own = ours_ref.shape[0] // 4
    lses = []
    for part in parts:
        rows = part[tokens:, :].astype(F32)
        lses.append(rows[0:2] + rows[2:4] + rows[4:6])
    lses.append(tree_lse_ref[0:2, :])
    high = functools.reduce(jnp.maximum, lses)
    factors = [jnp.exp(value - high) for value in lses]
    whole = functools.reduce(lambda a, b: a + b, factors)
    for s, factor in enumerate(factors):
        turn[2 * s : 2 * s + 2, :] = factor / whole
    turned = jnp.transpose(turn[...])[0:tokens, :]
    for h in range(heads):
        cut = slice(h * HEAD_DIM, (h + 1) * HEAD_DIM)
        at = 2 * len(parts) + h
        total = turned[:, at : at + 1] * tree_o_ref[:, cut]
        for s, part in enumerate(parts):
            at = 2 * s + h
            total = total + turned[:, at : at + 1] * part[0:tokens, cut].astype(F32)
        mixed[:, cut] = total

    def rows_of(other):
        rows = [
            mixed[pl.ds(pl.multiple_of(owner * own, 8), own), :]
            for owner in homes(len(parts), other)
        ]
        return jnp.concatenate(rows, axis=0).astype(BF16)

    theirs_ref[...] = dot(rows_of(True), w_ref[...]).astype(BF16)
    ours_ref[...] = dot(rows_of(False), w_ref[...])


def fold_kernel(ours_ref, theirs_ref, *outs):
    own = outs[0].shape[0]
    for i, out_ref in enumerate(outs):
        rows = slice(i * own, (i + 1) * own)
        out_ref[...] = (ours_ref[rows, :] + theirs_ref[rows, :].astype(F32)).astype(out_ref.dtype)


def expert_of_row(rows, experts):
    return jnp.where(iota((rows, experts), 0) // SLOTS == iota((rows, experts), 1), 1.0, 0.0)


def table_kernel(routes_ref, up_hbm, down_hbm, after_ref, *refs):
    place_refs, (weights_ref, sems) = refs[:3], refs[3:]
    del after_ref
    depth, both = up_hbm.shape
    units = down_hbm.shape[0]
    copies = [pltpu.make_async_copy(up_hbm, weights_ref.at[0:depth], sems.at[0])]
    for i in range(down_hbm.shape[1] // both):
        at = depth + i * units
        copies.append(
            pltpu.make_async_copy(
                down_hbm.at[:, i * both : (i + 1) * both],
                weights_ref.at[at : at + units],
                sems.at[1 + i],
            )
        )
    for copy in copies:
        copy.start()
    place_kernel(routes_ref, *place_refs)
    for copy in copies:
        copy.wait()


def place_kernel(routes_ref, place_ref, gather_ref, scatter_ref):
    chunks = place_ref.shape[0]
    _, real, block = gather_ref.shape
    row, column = iota((real, block), 0), iota((real, block), 1)
    base, slot = row // CAP * SLOTS, row % CAP
    gather_ref[0] = jnp.where(column == base + slot, 1.0, 0.0).astype(BF16)
    for k in range(chunks):
        hit = (column == base + CAP + slot // chunks) & (slot % chunks == k)
        gather_ref[1 + k] = jnp.where(hit, 1.0, 0.0).astype(BF16)
    row, column = iota((block, 2 * real), 0), iota((block, 2 * real), 1)
    is_tail = column >= real
    column = column - jnp.where(is_tail, real, 0)
    base, slot = column // CAP * SLOTS, column % CAP
    for k in range(chunks):
        main = (row == base + slot) & jnp.logical_not(is_tail)
        tail = (row == base + CAP + slot // chunks) & (slot % chunks == k) & is_tail
        scatter_ref[k] = jnp.where(main | tail, 1.0, 0.0).astype(BF16)
    top, tokens = routes_ref.shape
    chunks, rows, _ = place_ref.shape
    experts = rows // SLOTS
    named = iota((experts, tokens), 0)
    chosen = jnp.zeros((experts, tokens), F32)
    for k in range(top):
        chosen = jnp.where(routes_ref[k : k + 1, :] == named, 1.0, chosen)
    source = iota((tokens, 2 * tokens), 0)
    target = iota((tokens, 2 * tokens), 1) % tokens
    chosen = chosen.astype(BF16)
    rank = dot(chosen, jnp.where(source < target, 1.0, 0.0).astype(BF16))
    both = dot(chosen, jnp.where(source == target, 1.0, 0.0).astype(BF16))
    rank = jnp.where(both > 0.5, rank, -1.0).astype(BF16)
    spread = dot(expert_of_row(rows, experts).astype(BF16), rank)
    slot = iota((rows, 2 * tokens), 0) % SLOTS
    is_tail = iota((rows, 2 * tokens), 1) >= tokens
    for j in range(chunks):
        wanted = jnp.where(is_tail, (slot - CAP) * chunks + j, slot)
        valid = is_tail == (slot >= CAP)
        hit = valid & (spread == wanted.astype(F32))
        place_ref[j] = jnp.where(hit, 1.0, 0.0).astype(BF16)


def residual_kernel(*refs):
    parts = refs[:4]
    x_ref, g_ref, place_ref, res_ref, normed_ref, out_ref = refs[4:]
    tokens, width = parts[0].shape
    chunks = place_ref.shape[0]
    cut = width // (chunks + 1)
    start = pl.multiple_of(homes(len(parts), False)[0] * tokens, 8)
    residual = x_ref[pl.ds(start, tokens), :].astype(F32)
    for part in parts:
        residual = residual + part[...].astype(F32)
    res_ref[...] = residual
    inverse = lax.rsqrt(jnp.mean(residual * residual, axis=-1, keepdims=True) + EPSILON)
    normed = residual * inverse * g_ref[...].astype(F32).reshape(1, -1)
    normed_ref[...] = normed.astype(BF16)
    tail = normed[:, chunks * cut :]
    for j in range(chunks):
        pair = jnp.concatenate([normed[:, j * cut : (j + 1) * cut], tail], axis=0).astype(BF16)
        out_ref[:, j * cut : (j + 1) * cut] = dot(place_ref[j], pair).astype(BF16)


def gate_kernel(normed_ref, router_ref, routes_ref, table_ref):
    top, tokens = routes_ref.shape
    experts = router_ref.shape[0]
    chunks, _, rows = table_ref.shape
    logits = dot_t(normed_ref[...], router_ref[...])
    exponent = jnp.exp(logits)
    chances = exponent / jnp.sum(exponent, axis=-1, keepdims=True)
    named = iota((experts, tokens), 0)
    chosen = jnp.zeros((experts, tokens), F32)
    for k in range(top):
        chosen = jnp.where(routes_ref[k : k + 1, :] == named, 1.0, chosen)
    same = jnp.where(iota((tokens, tokens), 0) == iota((tokens, tokens), 1), 1.0, 0.0)
    chosen = dot_t(same.astype(BF16), chosen.astype(BF16))
    picked = chances * chosen
    gates = picked / jnp.sum(picked, axis=-1, keepdims=True)
    earlier = jnp.where(iota((tokens, tokens), 0) > iota((tokens, tokens), 1), 1.0, 0.0)
    rank = dot(earlier.astype(BF16), chosen.astype(BF16))
    rank = jnp.where(chosen > 0.5, rank, -1.0).astype(BF16)
    first = gates.astype(BF16)
    second = (gates - first.astype(F32)).astype(BF16)
    home = iota((experts, rows), 0) == iota((experts, rows), 1) // SLOTS
    home = jnp.where(home, 1.0, 0.0).astype(BF16)
    rank, first, second = dot(rank, home), dot(first, home), dot(second, home)
    slot = iota((tokens, rows), 1) % SLOTS
    main = (slot < CAP) & (rank == slot.astype(F32))
    for j in range(chunks):
        tail = (slot >= CAP) & (rank == ((slot - CAP) * chunks + j).astype(F32))
        table_ref[j] = jnp.concatenate(
            [
                jnp.where(main, first, 0.0),
                jnp.where(main, second, 0.0),
                jnp.where(tail, first, 0.0),
                jnp.where(tail, second, 0.0),
            ],
            axis=0,
        ).astype(BF16)


def expert_kernel(
    x_ref,
    weights_ref,
    other_ref,
    gather_ref,
    scatter_ref,
    normed_ref,
    router_ref,
    routes_ref,
    out_ref,
    table_ref,
):
    rows, packed = x_ref.shape
    width = normed_ref.shape[1]
    both = weights_ref.shape[1]
    units = both // 2
    cut = width - packed
    chunks = packed // cut
    _, real, block = gather_ref.shape
    mains, tails = [], []
    for at in range(0, rows, block):
        span = slice(at, at + block)
        mains.append(dot(gather_ref[0], x_ref[span, :]).astype(BF16))
        tail = dot(gather_ref[1], x_ref[span, 0:cut])
        for k in range(1, chunks):
            tail = tail + dot(gather_ref[1 + k], x_ref[span, k * cut : (k + 1) * cut])
        tails.append(tail.astype(BF16))
    main, tail = jnp.concatenate(mains, axis=0), jnp.concatenate(tails, axis=0)
    hidden = []
    for weights in (weights_ref, other_ref):
        parts = []
        for at in range(0, units, units // 2):
            gate_cut = slice(at, at + units // 2)
            up_cut = slice(units + at, units + at + units // 2)
            gate = dot(main, weights[0:packed, gate_cut]) + dot(tail, weights[packed:width, gate_cut])
            up = dot(main, weights[0:packed, up_cut]) + dot(tail, weights[packed:width, up_cut])
            parts.append((gate / (1.0 + jnp.exp(-gate)) * up).astype(BF16))
        hidden.append(jnp.concatenate(parts, axis=1))

    def result(k):
        at = width + k * cut // both * units
        rows, columns = slice(at, at + units), slice(k * cut % both, k * cut % both + cut)
        first = dot(hidden[0], weights_ref[rows, columns]).astype(BF16).astype(F32)
        second = dot(hidden[1], other_ref[rows, columns]).astype(BF16).astype(F32)
        return (first + second).astype(BF16)

    last = result(chunks)
    for k in range(chunks):
        columns = slice(k * cut, (k + 1) * cut)
        value = result(k)
        for i in range(rows // block):
            own = slice(i * real, (i + 1) * real)
            pair = jnp.concatenate([value[own], last[own]], axis=0)
            out_ref[i * block : (i + 1) * block, columns] = dot(scatter_ref[k], pair).astype(
                BF16
            )
    gate_kernel(normed_ref, router_ref, routes_ref, table_ref)


def final_kernel(back_ref, table_ref, res_ref, out_ref):
    tokens, width = res_ref.shape
    chunks = table_ref.shape[0]
    cut = width // (chunks + 1)
    tail = res_ref[:, chunks * cut :]
    for j in range(chunks):
        span = slice(j * cut, (j + 1) * cut)
        sums = dot(table_ref[j], back_ref[:, span])
        main = sums[0:tokens] + sums[tokens : 2 * tokens]
        out_ref[:, span] = (res_ref[:, span] + main).astype(BF16)
        tail = tail + (sums[2 * tokens : 3 * tokens] + sums[3 * tokens :])
    out_ref[:, chunks * cut :] = tail.astype(BF16)


def per_device(
    hidden,
    gain_attn,
    w_qkv,
    w_out,
    cache_keys,
    cache_values,
    cache_lengths,
    parents,
    gain_moe,
    w_router,
    routes,
    w_gate_up,
    w_down,
):
    z_count = lax.axis_size("z")
    exp_count = z_count * CORES
    tokens, width = hidden.shape
    requests, tree = parents.shape
    page = cache_keys.shape[1]
    local_width = w_qkv.shape[2]
    scale = HEAD_DIM ** (-0.5)
    own = tokens // exp_count
    experts = w_router.shape[1]
    packed = width * CAP // SLOTS
    chunks = packed // (width - packed)
    padded = tokens + 8

    w_three = pltpu.with_memory_space_constraint(jnp.transpose(w_qkv, (1, 0, 2)), HBM)
    cache_values = pltpu.with_memory_space_constraint(cache_values, HBM)

    query, normed_attn = call(
        query_kernel,
        (sds((tokens, local_width), BF16), sds((tokens, width), BF16)),
        [HBM, HBM, HBM],
        [
            pltpu.VMEM((tokens, width), BF16),
            pltpu.VMEM((width,), BF16),
            pltpu.VMEM((width, local_width), BF16),
            pltpu.SemaphoreType.DMA((3,)),
        ],
        flops=2 * tokens * width * local_width,
        bytes_accessed=2 * width * (tokens + local_width),
    )(
        pltpu.with_memory_space_constraint(hidden, HBM),
        pltpu.with_memory_space_constraint(gain_attn, HBM),
        w_three,
    )

    def over_z(value, step):
        return lax.ppermute(value, "z", [(i, (i + step) % z_count) for i in range(z_count)])

    def over_core(value):
        return lax.ppermute(value, "core", [(0, 1), (1, 0)])

    steps = sorted(range(1, z_count), key=lambda step: -min(step, z_count - step))

    order = far_last(z_count)
    pieces = [over_z(query, step) if step else query for step in order]
    keys = pltpu.with_memory_space_constraint(cache_keys, VMEM)
    values, visible = call(
        load_kernel,
        (sds(cache_values.shape, BF16), sds((tokens, tokens), F32)),
        [HBM, HBM, pl.ANY],
        [pltpu.VMEM(parents.shape, jnp.int32), pltpu.SemaphoreType.DMA((2,))],
        bytes_accessed=2 * requests * page * width,
        vmem=16 << 20,
    )(cache_values, pltpu.with_memory_space_constraint(parents, HBM), query)
    pieces[0], values = lax.optimization_barrier((pieces[0], values))
    other_pieces = [over_core(piece) for piece in pieces]

    scratch = [
        pltpu.VMEM((requests, z_count * 2 * tree, page), F32),
        pltpu.VMEM((requests, z_count * 2 * tree, page), BF16),
    ]
    heads = 2 * z_count
    lengths = cache_lengths.reshape(1, requests)
    for_other = call(
        functools.partial(page_kernel, scale, tree, False),
        sds((heads + 1, tokens, HEAD_DIM), BF16),
        [VMEM] * 7,
        scratch,
        flops=2 * tokens * page * width,
        bytes_accessed=2 * requests * page * width,
        vmem=20 << 20,
    )(lengths, *other_pieces, keys, values)
    from_other = over_core(for_other)
    kept, kept_lse = call(
        functools.partial(page_kernel, scale, tree, True),
        (sds((heads, tokens, HEAD_DIM), F32), sds((tokens, 128), F32)),
        [VMEM] * 7 + [pl.ANY],
        scratch,
        flops=2 * tokens * page * width,
        bytes_accessed=2 * requests * page * width,
        vmem=20 << 20,
    )(lengths, *pieces, keys, values, for_other)
    merged = call(
        merge_kernel,
        tuple(sds((padded, local_width), BF16) for _ in range(z_count)),
        [VMEM] * 3,
        [pltpu.VMEM((256, 128), F32)],
        bytes_accessed=1 << 20,
    )(from_other, kept, kept_lse)
    arrived = [merged[0]] + [over_z(merged[order.index(step)], -step) for step in steps]

    tree_o, tree_lse = call(
        functools.partial(tree_kernel, scale),
        (sds((tokens, local_width), F32), sds((8, 256), F32)),
        [VMEM, HBM, VMEM, VMEM, pl.ANY],
        [
            pltpu.VMEM((256, 128), F32),
            pltpu.VMEM((2, width, local_width), BF16),
            pltpu.SemaphoreType.DMA((2,)),
        ],
        flops=4 * tokens * width * local_width,
        bytes_accessed=2 * width * (tokens + 2 * local_width),
    )(normed_attn, w_three, query, visible, merged[0])
    theirs, ours = call(
        out_kernel,
        (sds((z_count * own, width), BF16), sds((z_count * own, width), F32)),
        [VMEM] * 7,
        [pltpu.VMEM((128, 256), F32), pltpu.VMEM((tokens, local_width), F32)],
        flops=2 * tokens * width * local_width,
        bytes_accessed=2 * width * (tokens + local_width),
    )(*arrived, tree_o, tree_lse, w_out)
    folded = call(
        fold_kernel,
        tuple(sds((own, width), BF16 if step else F32) for step in range(z_count)),
        [VMEM] * 2,
        bytes_accessed=1 << 20,
    )(ours, over_core(theirs))
    mixed = [folded[0]] + [over_z(folded[step], -step) for step in steps]
    block = experts * SLOTS // 2
    real = block // SLOTS * CAP
    weight_rows = width + width * w_down.shape[1] // w_gate_up.shape[2]
    place, gather, scatter, weights = call(
        table_kernel,
        (
            sds((chunks, experts * SLOTS, 2 * own), BF16),
            sds((1 + chunks, real, block), BF16),
            sds((chunks, block, 2 * real), BF16),
            sds((weight_rows, w_gate_up.shape[2]), BF16),
        ),
        [VMEM, HBM, HBM, pl.ANY],
        [pltpu.SemaphoreType.DMA((1 + width // w_gate_up.shape[2],))],
        flops=1 << 24,
        bytes_accessed=1 << 23,
        vmem=16 << 20,
    )(
        routes.T,
        pltpu.with_memory_space_constraint(w_gate_up[0], HBM),
        pltpu.with_memory_space_constraint(w_down[0], HBM),
        folded[0],
    )
    *mixed, weights = lax.optimization_barrier((*mixed, weights))
    other_weights = over_core(weights)

    residual, normed, outgoing = call(
        residual_kernel,
        (
            sds((own, width), F32),
            sds((own, width), BF16),
            sds((experts * SLOTS, packed), BF16),
        ),
        [VMEM] * 7,
        flops=1 << 27,
        bytes_accessed=1 << 22,
    )(*mixed, hidden, gain_moe, place)
    rows = lax.all_to_all(
        outgoing.reshape(experts, SLOTS, packed),
        ("req", "z"),
        split_axis=0,
        concat_axis=0,
        tiled=True,
    ).reshape(experts * SLOTS, packed)

    summed, table = call(
        expert_kernel,
        (
            sds((experts * SLOTS, packed), BF16),
            sds((chunks, 4 * own, experts * SLOTS), BF16),
        ),
        [VMEM] * 8,
        flops=12 * experts * CAP * width * w_down.shape[1],
        bytes_accessed=12 * width * w_down.shape[1],
        vmem=24 << 20,
    )(
        rows,
        weights,
        other_weights,
        gather,
        scatter,
        normed,
        w_router.T,
        routes.T,
    )
    back = lax.all_to_all(
        summed.reshape(experts, SLOTS, packed),
        ("req", "z"),
        split_axis=0,
        concat_axis=0,
        tiled=True,
    ).reshape(experts * SLOTS, packed)
    return call(
        final_kernel,
        sds((own, width), BF16),
        [VMEM] * 3,
        flops=1 << 27,
        bytes_accessed=1 << 22,
    )(back, table, residual)


def solution(mesh):
    req_count, exp_count = mesh.devices.shape
    split = Mesh(
        mesh.devices.reshape(req_count, exp_count // CORES, CORES), ("req", "z", "core")
    )
    exp = ("z", "core")
    everywhere = ("req", "z", "core")
    in_specs = (
        P("req", None),
        P(),
        P(None, None, exp),
        P(exp, None),
        P("req", exp, None),
        P("req", exp, None),
        P("req"),
        P("req", None),
        P(),
        P(),
        P(everywhere, None),
        P(everywhere, None, None),
        P(everywhere, None, None),
    )
    return jax.shard_map(
        per_device,
        mesh=split,
        in_specs=in_specs,
        out_specs=P(everywhere, None),
        check_vma=False,
    )
```
